256 devices in a mesh: lon: 64 (over x, y_lo, z), lat: 4 (over y_hi, core).
Axes of the slice: x: 4, y: 4 (y_hi: 2, y_lo: 2; y = y_hi * 2 + y_lo), z: 8, core: 2. Of those that a mesh axis runs over, the one named last changes fastest.
Arguments:
- conditions: bfloat16 [80, 64, 8192], P(None, 'lat', 'lon'), may hold values from -6 to 6
- noisy_state: float32 [1, 80, 64, 8192], P(None, None, 'lat', 'lon'), may hold values from -6 to 6
- noise_level: float32 [1], replicated, may hold values from 0.25 to 1
- kernel_input: bfloat16 [9, 128, 80], replicated, may hold values from -0.21875 to 0.21875
- kernel_coarse: bfloat16 [9, 256, 128], replicated, may hold values from -0.1875 to 0.1875
- kernel_deeper: bfloat16 [9, 256, 256], replicated, may hold values from -0.125 to 0.125
- guide_weight: bfloat16 [128, 256], replicated, may hold values from -0.375 to 0.375
- time_scale: float32 [128], replicated, may hold values from -9 to 9
- time_shift: float32 [128], replicated, may hold values from -3 to 3
- kernel_noisy: bfloat16 [9, 128, 80], replicated, may hold values from -0.21875 to 0.21875
- kernel_block: bfloat16 [9, 128, 128], replicated, may hold values from -0.1875 to 0.1875
- kernel_branch: bfloat16 [9, 128, 128], replicated, may hold values from -0.1875 to 0.1875
- kernel_output: bfloat16 [9, 80, 128], replicated, may hold values from -0.1875 to 0.1875
Outputs:
- denoised: float32 [1, 80, 64, 8192], P(None, None, 'lat', 'lon')
The draws below stay inside these ranges and needn't reach their ends.
All inputs are finite; a program needn't handle non-finite values.
Results may differ from the reference program's by a relative error of at most 0.0075.
Values may be sent and summed in bfloat16 or wider, within the bound.
No kernel may reach another device: no remote copies, remote signals or barrier semaphores. Data moves between devices by JAX's collectives and lax.ppermute only.
A program may use at most 64 MiB of HBM per device.

```python
import math
import jax
import jax.numpy as jnp
from jax import lax

CH = 80
C0 = 128
C1 = 256
MEMBERS = 1
LAT = 64
LON = 8192


def shard_levels(key, shape, split, low, largest):
    def one(position, blocks):
        heights = jax.random.uniform(jax.random.fold_in(jax.random.fold_in(key, 6), position), (blocks,), jnp.float32, low / len(split), largest / len(split))
        return jnp.repeat(jnp.exp(heights), shape[position] // blocks).reshape((-1,) + (1,) * (len(shape) - position - 1))

    loudness = one(*split[0])
    for cut in split[1:]:
        loudness = loudness * one(*cut)
    return loudness


def centred(key, shape, width, limit, pieces=(), held_as=jnp.bfloat16):
    entries = width * jax.random.normal(key, shape, jnp.float32)
    if pieces:
        entries = entries * shard_levels(key, shape, pieces, -0.22, 0.18)
    return jnp.clip(entries, -limit, limit).astype(held_as)


def setup_inputs(seed: int = 0) -> dict:
    key_of = jax.random.split(jax.random.key(seed), 14)
    conditions = centred(key_of[0], (CH, LAT, LON), 1.0, 6.0, ((1, 4), (2, 64)))
    noisy_state = centred(key_of[1], (MEMBERS, CH, LAT, LON), 1.0, 6.0, ((2, 4), (3, 64)), jnp.float32)
    noise_level = jnp.clip(jnp.exp(jax.random.uniform(key_of[2], (MEMBERS,), jnp.float32, math.log(0.25), math.log(1.0))), 0.25, 1.0)
    kernel_input = centred(key_of[3], (9, C0, CH), (9 * CH) ** -0.5, 0.21875)
    kernel_coarse = centred(key_of[4], (9, C1, C0), (9 * C0) ** -0.5, 0.1875)
    kernel_deeper = centred(key_of[5], (9, C1, C1), (9 * C1) ** -0.5, 0.125)
    guide_weight = centred(key_of[6], (C0, C1), C1 ** -0.5, 0.375)
    time_scale = centred(key_of[7], (C0,), 3.0, 9.0, (), jnp.float32)
    time_shift = centred(key_of[8], (C0,), 0.5, 3.0, (), jnp.float32)
    kernel_noisy = centred(key_of[9], (9, C0, CH), (9 * CH) ** -0.5, 0.21875)
    kernel_block = centred(key_of[10], (9, C0, C0), (9 * C0) ** -0.5, 0.1875)
    kernel_branch = centred(key_of[11], (9, C0, C0), (9 * C0) ** -0.5, 0.1875)
    kernel_output = centred(key_of[12], (9, CH, C0), (9 * C0) ** -0.5, 0.1875)
    return dict(conditions=conditions, noisy_state=noisy_state, noise_level=noise_level, kernel_input=kernel_input, kernel_coarse=kernel_coarse, kernel_deeper=kernel_deeper, guide_weight=guide_weight, time_scale=time_scale, time_shift=time_shift, kernel_noisy=kernel_noisy, kernel_block=kernel_block, kernel_branch=kernel_branch, kernel_output=kernel_output)


def pad_band(source):
    dims = source.ndim
    lat_pad = [(0, 0)] * (dims - 2) + [(1, 1), (0, 0)]
    padded = jnp.pad(source, lat_pad)
    lon_pad = [(0, 0)] * (dims - 1) + [(1, 1)]
    return jnp.pad(padded, lon_pad, mode='wrap')

def stencil(padded, kernel):
    out_rows = padded.shape[-2] - 2
    out_cols = padded.shape[-1] - 2
    summed = None
    for tap_id in range(9):
        tap_row = tap_id // 3
        tap_col = tap_id % 3
        window = padded[:, tap_row:tap_row + out_rows, tap_col:tap_col + out_cols].astype(jnp.float32)
        contrib = jnp.einsum('oc,chw->ohw', kernel[tap_id].astype(jnp.float32), window)
        summed = contrib if summed is None else summed + contrib
    return summed

def reference(conditions, noisy_state, noise_level, kernel_input, kernel_coarse, kernel_deeper, guide_weight, time_scale, time_shift, kernel_noisy, kernel_block, kernel_branch, kernel_output):
    first_level = jax.nn.silu(stencil(pad_band(conditions), kernel_input)).astype(jnp.bfloat16)
    feat_count, lat_rows, lon_cols = first_level.shape
    pooled = lax.optimization_barrier(jnp.mean(first_level.astype(jnp.float32).reshape(feat_count, lat_rows // 2, 2, lon_cols // 2, 2), axis=(2, 4))).astype(jnp.bfloat16)
    middle = jax.nn.silu(stencil(pad_band(pooled), kernel_coarse)).astype(jnp.bfloat16)
    deepest = jax.nn.silu(stencil(pad_band(middle), kernel_deeper)).astype(jnp.bfloat16)
    guide_field = jnp.einsum('oc,chw->ohw', guide_weight.astype(jnp.float32), deepest.astype(jnp.float32))
    guide_field = jnp.repeat(jnp.repeat(guide_field, 2, axis=1), 2, axis=2)
    variance = noise_level * noise_level + 0.25
    scale_in = 1.0 / jnp.sqrt(variance)
    scale_skip = 0.25 / variance
    scale_out = 0.5 * noise_level / jnp.sqrt(variance)
    noise_code = jnp.log(noise_level) / 4.0

    def member_step(member_id):
        state = noisy_state[member_id]
        scaled_input = (scale_in[member_id] * state).astype(jnp.bfloat16)
        embedded = time_scale * noise_code[member_id] + time_shift
        opening = stencil(pad_band(scaled_input), kernel_noisy) + guide_field + embedded[:, None, None]
        hidden = jax.nn.silu(opening).astype(jnp.bfloat16)
        inner_act = jax.nn.silu(stencil(pad_band(hidden), kernel_block)).astype(jnp.bfloat16)
        mixed_act = jax.nn.silu(hidden.astype(jnp.float32) + stencil(pad_band(inner_act), kernel_branch)).astype(jnp.bfloat16)
        head_out = stencil(pad_band(mixed_act), kernel_output)
        return scale_skip[member_id] * state + scale_out[member_id] * head_out
    return lax.map(member_step, jnp.arange(noisy_state.shape[0], dtype=jnp.int32))
```

```python
import functools

import jax
import jax.numpy as jnp
from jax import lax
from jax.experimental import pallas as pl
from jax.experimental.pallas import tpu as pltpu
from jax.sharding import PartitionSpec as P

F32 = jnp.float32
BF16 = jnp.bfloat16
PITCH = 80
EDGE = 8
ROWS = 16
PAIRS = 64
CH = 80
DEEP = 9
THIN = 4
VMEM = pltpu.VMEM
AXES = ("lon", "lat")


def swap_pairs(mesh_shape, lat, lon):
    n_lon, n_lat = mesh_shape
    pairs = []
    for o in range(n_lon):
        for a in range(n_lat):
            b, p = a, o
            if lat:
                b = a ^ 1 if lat == "A" else a - 1 + 2 * (a % 2)
            if lon:
                p = (o ^ 1 if lon == "A" else o - 1 + 2 * (o % 2)) % n_lon
            if 0 <= b < n_lat:
                pairs.append((o * n_lat + a, p * n_lat + b))
    return pairs


def silu(v):
    h = v * 0.5
    return h + h * jnp.tanh(h)


def matmul_nt(x, w):
    return lax.dot_general(x, w, (((1,), (1,)), ((), ())), preferred_element_type=F32)


def prep_body(scal, cond, state, own_c, own_s, edge_a, edge_b, lat_a, lat_b, work):
    lon_even = scal[6] > 0.5
    lat_even = scal[7] > 0.5
    work[...] = cond[...].astype(F32)
    row = lax.broadcasted_iota(jnp.int32, (128, 128), 0)
    col = lax.broadcasted_iota(jnp.int32, (128, 128), 1)
    pick = (col == jnp.where(row < PAIRS, 2 * row, 2 * (row - PAIRS) + 1)).astype(BF16)
    blank = jnp.zeros((128 - CH, 128), BF16)
    slot = lax.broadcasted_iota(jnp.int32, (8, 128), 0)
    for i in range(ROWS):
        c_row = work[pl.ds(i, CH, stride=ROWS), :].astype(BF16)
        s_row = (scal[0] * state[pl.ds(i, CH, stride=ROWS), :]).astype(BF16)
        both = matmul_nt(pick, jnp.concatenate([c_row, blank, s_row, blank], 0))
        c_pair = jnp.concatenate([both[:PAIRS, :128], both[PAIRS:, :128]], 1)
        s_pair = jnp.concatenate([both[:PAIRS, 128:], both[PAIRS:, 128:]], 1)
        own_c[i] = c_pair.astype(BF16)
        own_s[i] = s_pair.astype(BF16)
        for half in range(2):
            lanes = slice(128 * half, 128 * half + 128)
            left = jnp.where(slot < 5, c_pair[:8, lanes], pltpu.roll(s_pair[:8, lanes], 5, 0))
            right = jnp.where(slot > 2, c_pair[-8:, lanes], pltpu.roll(s_pair[-8:, lanes], 3, 0))
            edge_a[i, :, lanes] = jnp.where(lon_even, right, left).astype(BF16)
            edge_b[i, :, lanes] = jnp.where(lon_even, left, right).astype(BF16)
    lane = lax.broadcasted_iota(jnp.int32, (PAIRS, 128), 1)
    free = 128 - CH
    for k in range(DEEP):
        for half in range(2):
            lanes = slice(128 * half, 128 * half + 128)
            rows = []
            for first, s_first in ((0, 0), (ROWS - DEEP, ROWS - THIN)):
                value = own_c[first + k, :, lanes].astype(F32)
                n = 2 * k + half
                if n < 4 * THIN:
                    r, h = divmod(n // 2, 2)
                    part = own_s[s_first + r, :, 128 * h : 128 * h + 128].astype(F32)
                    part = pltpu.roll(part, (CH - free * (n % 2)) % 128, 1)
                    value = jnp.where(lane < CH, value, part)
                rows.append(value)
            lat_a[k, :, lanes] = jnp.where(lat_even, rows[1], rows[0]).astype(BF16)
            lat_b[k, :, lanes] = jnp.where(lat_even, rows[0], rows[1]).astype(BF16)


def prep(scal, cond, state):
    vm = pl.BlockSpec(memory_space=VMEM)
    own = jax.ShapeDtypeStruct((ROWS, PAIRS, 256), BF16)
    edge = jax.ShapeDtypeStruct((ROWS, 8, 256), BF16)
    rows = jax.ShapeDtypeStruct((DEEP, PAIRS, 256), BF16)
    return pl.pallas_call(
        prep_body,
        out_shape=(own, own, edge, edge, rows, rows),
        in_specs=[pl.BlockSpec(memory_space=pltpu.SMEM), vm, vm],
        out_specs=[vm] * 6,
        scratch_shapes=[VMEM((CH * ROWS, 128), F32)],
        name="prep",
    )(scal, cond, state)


def pair_weights(w, di):
    k0, k1, k2 = w[3 * di], w[3 * di + 1], w[3 * di + 2]
    z = jnp.zeros_like(k0)
    c = jnp.concatenate
    return c([c([k1, k2], 1), c([k0, k1], 1), c([z, k0], 1), c([k2, z], 1)], 0)


def pair_conv(x, w, centre, rows):
    span = rows * PITCH
    taps = [x[(centre + d - 1) * PITCH : (centre + d - 1) * PITCH + span, :] for d in range(3)]
    weights = jnp.concatenate([pair_weights(w, d) for d in range(3)], 1)
    y = matmul_nt(jnp.concatenate(taps, 1), weights)
    even = y[:, 0:128] + pltpu.roll(y[:, 256:384], 1, 0)
    odd = y[:, 128:256] + pltpu.roll(y[:, 384:512], span - 1, 0)
    return even, odd


def half_conv(x, w, centre, rows):
    span = rows * PITCH
    c = jnp.concatenate
    taps = c([x[(centre + d - 1) * PITCH : (centre + d - 1) * PITCH + span, :] for d in range(3)], 1)
    weights = c([c([w[3 * d + b] for d in range(3)], 1) for b in range(3)], 0)
    y = matmul_nt(taps, weights)
    n = y.shape[1] // 3
    return y[:, n : 2 * n] + pltpu.roll(y[:, :n], 1, 0) + pltpu.roll(y[:, 2 * n :], span - 1, 0)


def net_body(
    scal, own_c, own_s, edge_a, edge_b, lat_a, lat_b, corner_a, corner_b, state,
    k_in, k_coarse, k_deeper, guide_w, scale, shift, k_noisy, k_block, k_branch, k_out,
    out, x_c, x_s, w_in, w_noisy, w_out, pooled, middle, guide, hidden, inner, mixed, turn,
):
    top = scal[4]
    bottom = scal[5]
    lon_even = scal[6] > 0.5
    lat_even = scal[7] > 0.5
    free = 128 - CH
    for tap in range(9):
        for src, dst in ((k_in, w_in), (k_noisy, w_noisy)):
            dst[tap, :, CH:] = jnp.zeros((128, free), BF16)
            dst[tap, :, :CH] = src[tap]
        w_out[tap, CH:, :] = jnp.zeros((free, 128), BF16)
        w_out[tap, :CH, :] = k_out[tap]

    slot = lax.broadcasted_iota(jnp.int32, (8, 256), 0)
    lane = lax.broadcasted_iota(jnp.int32, (1, 128), 1)

    def put(c_row, s_row, left, right, middle_c, middle_s):
        x_c[c_row * PITCH : c_row * PITCH + 8, :] = jnp.where(slot > 2, left, 0.0).astype(BF16)
        x_c[c_row * PITCH + 8 : c_row * PITCH + 72, :] = middle_c
        x_c[c_row * PITCH + 72 : c_row * PITCH + 80, :] = jnp.where(slot < 5, right, 0.0).astype(BF16)
        if s_row is not None:
            s_left = jnp.where(slot > 5, pltpu.roll(left, 5, 0), 0.0)
            s_right = jnp.where(slot < 2, pltpu.roll(right, 3, 0), 0.0)
            x_s[s_row * PITCH : s_row * PITCH + 8, :] = s_left.astype(BF16)
            x_s[s_row * PITCH + 8 : s_row * PITCH + 72, :] = middle_s
            x_s[s_row * PITCH + 72 : s_row * PITCH + 80, :] = s_right.astype(BF16)

    for i in range(ROWS):
        a, b = edge_a[i].astype(F32), edge_b[i].astype(F32)
        put(DEEP + i, THIN + i, jnp.where(lon_even, b, a), jnp.where(lon_even, a, b), own_c[i], own_s[i])
    for below in range(2):
        for k in range(DEEP):
            r = k - (DEEP - THIN) if not below else k
            s_row = r if not below else THIN + ROWS + k
            if not 0 <= r < THIN:
                s_row = None
            picks = []
            for half in range(2):
                lanes = slice(128 * half, 128 * half + 128)
                a, b = lat_a[k, :, lanes].astype(F32), lat_b[k, :, lanes].astype(F32)
                value = jnp.where(lat_even, a, b) if below else jnp.where(lat_even, b, a)
                picks.append(jnp.where(lane < CH, value, 0.0).astype(BF16))
            mid_s = None
            if s_row is not None:
                mids = []
                for h in range(2):
                    n = 2 * (2 * r + h)
                    parts = []
                    for m in (n, n + 1):
                        lanes = slice(128 * (m % 2), 128 * (m % 2) + 128)
                        a, b = lat_a[m // 2, :, lanes].astype(F32), lat_b[m // 2, :, lanes].astype(F32)
                        value = jnp.where(lat_even, a, b) if below else jnp.where(lat_even, b, a)
                        parts.append(pltpu.roll(value, (128 - CH + free * (m % 2)) % 128, 1))
                    mids.append(jnp.where(lane < free, parts[0], jnp.where(lane < CH, parts[1], 0.0)).astype(BF16))
                mid_s = jnp.concatenate(mids, 1)
            sides = []
            for side in range(2):
                pair = []
                for corner in (corner_a, corner_b):
                    pair.append(corner[side, k].astype(F32))
                sides.append(jnp.where(lat_even, pair[0], pair[1]) if below else jnp.where(lat_even, pair[1], pair[0]))
            row = DEEP + ROWS + k if below else k
            put(row, s_row, sides[0], sides[1], jnp.concatenate(picks, 1), mid_s)

    for ch in range(8):
        even, odd = pair_conv(x_c, w_in, 1 + 4 * ch, 4)
        both = silu(even).astype(BF16).astype(F32) + silu(odd).astype(BF16).astype(F32)
        both = both.reshape(2, 2, PITCH, 128)
        mean = (both[:, 0] + both[:, 1]) * 0.25
        if ch < 2 or ch > 5:
            mean = mean * (top if ch < 2 else bottom)
        pooled[2 * ch * PITCH : (2 * ch + 2) * PITCH, :] = mean.reshape(2 * PITCH, 128).astype(BF16)
    for ch in range(7):
        m = silu(half_conv(pooled, k_coarse, 1 + 2 * ch, 2))
        for q in range(2):
            row = 2 * ch + q
            v = m[q * PITCH : (q + 1) * PITCH]
            if row < 3 or row > 10:
                v = v * (top if row < 3 else bottom)
            middle[row * PITCH : (row + 1) * PITCH, :] = v.astype(BF16)
    embedded = scale[...] * scal[3] + shift[...]
    for ch in range(6):
        d = silu(half_conv(middle, k_deeper, 1 + 2 * ch, 2)).astype(BF16)
        guide[2 * ch * PITCH : (2 * ch + 2) * PITCH, :] = matmul_nt(d, guide_w[...]) + embedded
    for ch in range(11):
        even, odd = pair_conv(x_s, w_noisy, 1 + 2 * ch, 2)
        for q in range(2):
            row = 2 * ch + q
            g = guide[(row + 1) // 2 * PITCH : ((row + 1) // 2 + 1) * PITCH, :]
            for half, v in enumerate((even, odd)):
                v = silu(v[q * PITCH : (q + 1) * PITCH] + g)
                if row < 3 or row > 18:
                    v = v * (top if row < 3 else bottom)
                hidden[row * PITCH : (row + 1) * PITCH, 128 * half : 128 * half + 128] = v.astype(BF16)
    for ch in range(10):
        for half, v in enumerate(pair_conv(hidden, k_block, 1 + 2 * ch, 2)):
            v = silu(v)
            if ch in (0, 9):
                v = v * (top if ch == 0 else bottom)
            inner[2 * ch * PITCH : (2 * ch + 2) * PITCH, 128 * half : 128 * half + 128] = v.astype(BF16)
    for ch in range(9):
        h = hidden[(2 + 2 * ch) * PITCH : (4 + 2 * ch) * PITCH, :].astype(F32)
        for half, v in enumerate(pair_conv(inner, k_branch, 1 + 2 * ch, 2)):
            v = silu(v + h[:, 128 * half : 128 * half + 128])
            for q in range(2):
                row = 2 * ch + q
                u = v[q * PITCH : (q + 1) * PITCH]
                if row in (0, 17):
                    u = u * (top if row == 0 else bottom)
                mixed[row * PITCH : (row + 1) * PITCH, 128 * half : 128 * half + 128] = u.astype(BF16)
    for ch in range(8):
        even, odd = pair_conv(mixed, w_out, 1 + 2 * ch, 2)
        for q in range(2):
            row = 2 * ch + q
            at = q * PITCH + EDGE
            turn[row, pl.ds(0, PAIRS, stride=2), :] = even[at : at + PAIRS]
            turn[row, pl.ds(1, PAIRS, stride=2), :] = odd[at : at + PAIRS]
            head = turn[row].T[:CH]
            here = pl.ds(row, CH, stride=ROWS)
            out[here, :] = scal[1] * state[here, :] + scal[2] * head


def net(*args):
    vm = pl.BlockSpec(memory_space=VMEM)
    return pl.pallas_call(
        net_body,
        out_shape=jax.ShapeDtypeStruct((CH * ROWS, 128), F32),
        in_specs=[pl.BlockSpec(memory_space=pltpu.SMEM)] + [vm] * (len(args) - 1),
        out_specs=vm,
        scratch_shapes=[
            VMEM((34 * PITCH, 256), BF16),
            VMEM((24 * PITCH, 256), BF16),
            VMEM((9, 128, 128), BF16),
            VMEM((9, 128, 128), BF16),
            VMEM((9, 128, 128), BF16),
            VMEM((16 * PITCH, 128), BF16),
            VMEM((14 * PITCH, 256), BF16),
            VMEM((12 * PITCH, 128), F32),
            VMEM((22 * PITCH, 256), BF16),
            VMEM((20 * PITCH, 256), BF16),
            VMEM((18 * PITCH, 256), BF16),
            VMEM((ROWS, 128, 128), F32),
        ],
        compiler_params=pltpu.CompilerParams(vmem_limit_bytes=56 << 20),
        name="net",
    )(*args)


def on_device(
    mesh_shape,
    conditions,
    noisy_state,
    noise_level,
    kernel_input,
    kernel_coarse,
    kernel_deeper,
    guide_weight,
    time_scale,
    time_shift,
    kernel_noisy,
    kernel_block,
    kernel_branch,
    kernel_output,
):
    sigma = noise_level[0]
    variance = sigma * sigma + 0.25
    root = jnp.sqrt(variance)
    lon, lat = lax.axis_index("lon"), lax.axis_index("lat")
    flags = [lat > 0, lat < mesh_shape[1] - 1, lon % 2 == 0, lat % 2 == 0]
    scal = jnp.stack(
        [1.0 / root, 0.25 / variance, 0.5 * sigma / root, jnp.log(sigma) / 4.0] + [f.astype(F32) for f in flags]
    )
    cond = conditions.reshape(CH * ROWS, 128)
    state = noisy_state.reshape(CH * ROWS, 128)
    own_c, own_s, edge_a, edge_b, lat_a, lat_b = prep(scal, cond, state)
    permute = lambda value, a, o: lax.ppermute(value, AXES, swap_pairs(mesh_shape, a, o))
    edge_a = permute(edge_a, None, "A")
    edge_b = permute(edge_b, None, "B")
    lat_a = permute(lat_a, "A", None)
    lat_b = permute(lat_b, "B", None)
    lon_even, lat_even = scal[6] > 0.5, scal[7] > 0.5
    sides = jnp.stack([jnp.where(lon_even, edge_b, edge_a), jnp.where(lon_even, edge_a, edge_b)])
    first, last = sides[:, :DEEP], sides[:, ROWS - DEEP :]
    corner_a = permute(jnp.where(lat_even, last, first), "A", None)
    corner_b = permute(jnp.where(lat_even, first, last), "B", None)
    out = net(
        scal, own_c, own_s, edge_a, edge_b, lat_a, lat_b, corner_a, corner_b, state,
        kernel_input, kernel_coarse, kernel_deeper, guide_weight, time_scale[None], time_shift[None],
        kernel_noisy, kernel_block, kernel_branch, kernel_output,
    )
    return out.reshape(noisy_state.shape)


def solution(mesh):
    tile = P(None, "lat", "lon")
    member = P(None, None, "lat", "lon")
    return jax.shard_map(
        functools.partial(on_device, (mesh.shape["lon"], mesh.shape["lat"])),
        mesh=mesh,
        in_specs=(tile, member) + (P(),) * 11,
        out_specs=member,
        check_vma=False,
    )
```

```python
import functools

import jax
import jax.numpy as jnp
from jax import lax
from jax.experimental import pallas as pl
from jax.experimental.pallas import tpu as pltpu
from jax.sharding import PartitionSpec as P

F32 = jnp.float32
BF16 = jnp.bfloat16
PITCH = 80
EDGE = 8
ROWS = 16
PAIRS = 64
CH = 80
DEEP = 9
THIN = 4
VMEM = pltpu.VMEM
AXES = ("lon", "lat")


def swap_pairs(mesh_shape, lat, lon):
    n_lon, n_lat = mesh_shape
    pairs = []
    for o in range(n_lon):
        for a in range(n_lat):
            b, p = a, o
            if lat:
                b = a ^ 1 if lat == "A" else a - 1 + 2 * (a % 2)
            if lon:
                p = (o ^ 1 if lon == "A" else o - 1 + 2 * (o % 2)) % n_lon
            if 0 <= b < n_lat:
                pairs.append((o * n_lat + a, p * n_lat + b))
    return pairs


def silu(v):
    h = v * 0.5
    return h + h * jnp.tanh(h)


def matmul_nt(x, w):
    return lax.dot_general(x, w, (((1,), (1,)), ((), ())), preferred_element_type=F32)


def prep_body(noise, cond, state, own_c, own_s, edge_a, edge_b, lat_a, lat_b, work):
    lon_even = lax.axis_index("lon") % 2 == 0
    lat_even = lax.axis_index("lat") % 2 == 0
    sigma = jnp.full((1, 128), noise[0], F32)
    scale_in = 1.0 / jnp.sqrt(sigma * sigma + 0.25)
    work[...] = cond[...].astype(F32)
    row = lax.broadcasted_iota(jnp.int32, (128, 128), 0)
    col = lax.broadcasted_iota(jnp.int32, (128, 128), 1)
    pick = (col == jnp.where(row < PAIRS, 2 * row, 2 * (row - PAIRS) + 1)).astype(BF16)
    blank = jnp.zeros((128 - CH, 128), BF16)
    slot = lax.broadcasted_iota(jnp.int32, (8, 128), 0)
    for i in range(ROWS):
        c_row = work[pl.ds(i, CH, stride=ROWS), :].astype(BF16)
        s_row = (scale_in * state[pl.ds(i, CH, stride=ROWS), :]).astype(BF16)
        both = matmul_nt(pick, jnp.concatenate([c_row, blank, s_row, blank], 0))
        c_pair = jnp.concatenate([both[:PAIRS, :128], both[PAIRS:, :128]], 1)
        s_pair = jnp.concatenate([both[:PAIRS, 128:], both[PAIRS:, 128:]], 1)
        own_c[i] = c_pair.astype(BF16)
        own_s[i] = s_pair.astype(BF16)
        for half in range(2):
            lanes = slice(128 * half, 128 * half + 128)
            left = jnp.where(slot < 5, c_pair[:8, lanes], pltpu.roll(s_pair[:8, lanes], 5, 0))
            right = jnp.where(slot > 2, c_pair[-8:, lanes], pltpu.roll(s_pair[-8:, lanes], 3, 0))
            edge_a[i, :, lanes] = jnp.where(lon_even, right, left).astype(BF16)
            edge_b[i, :, lanes] = jnp.where(lon_even, left, right).astype(BF16)
    lane = lax.broadcasted_iota(jnp.int32, (PAIRS, 128), 1)
    free = 128 - CH
    for k in range(DEEP):
        for half in range(2):
            lanes = slice(128 * half, 128 * half + 128)
            rows = []
            for first, s_first in ((0, 0), (ROWS - DEEP, ROWS - THIN)):
                value = own_c[first + k, :, lanes].astype(F32)
                n = 2 * k + half
                if n < 4 * THIN:
                    r, h = divmod(n // 2, 2)
                    part = own_s[s_first + r, :, 128 * h : 128 * h + 128].astype(F32)
                    part = pltpu.roll(part, (CH - free * (n % 2)) % 128, 1)
                    value = jnp.where(lane < CH, value, part)
                rows.append(value)
            lat_a[k, :, lanes] = jnp.where(lat_even, rows[1], rows[0]).astype(BF16)
            lat_b[k, :, lanes] = jnp.where(lat_even, rows[0], rows[1]).astype(BF16)


def prep(noise, cond, state):
    vm = pl.BlockSpec(memory_space=VMEM)
    own = jax.ShapeDtypeStruct((ROWS, PAIRS, 256), BF16)
    edge = jax.ShapeDtypeStruct((ROWS, 8, 256), BF16)
    rows = jax.ShapeDtypeStruct((DEEP, PAIRS, 256), BF16)
    return pl.pallas_call(
        prep_body,
        out_shape=(own, own, edge, edge, rows, rows),
        in_specs=[pl.BlockSpec(memory_space=pltpu.SMEM), vm, vm],
        out_specs=[vm] * 6,
        scratch_shapes=[VMEM((CH * ROWS, 128), F32)],
        compiler_params=pltpu.CompilerParams(vmem_limit_bytes=12 << 20),
        name="prep",
    )(noise, cond, state)


def pair_weights(w, di):
    k0, k1, k2 = w[3 * di], w[3 * di + 1], w[3 * di + 2]
    z = jnp.zeros_like(k0)
    c = jnp.concatenate
    return c([c([k1, k2], 1), c([k0, k1], 1), c([z, k0], 1), c([k2, z], 1)], 0)


def pair_weights_by_input(w, di):
    k0, k1, k2 = w[3 * di], w[3 * di + 1], w[3 * di + 2]
    z = jnp.zeros_like(k0)
    c = jnp.concatenate
    return c([c([k1, k0, z, k2], 1), c([k2, k1, k0, z], 1)], 0)


def pair_conv(x, w, centre, rows, by_input=False):
    span = rows * PITCH
    taps = [x[(centre + d - 1) * PITCH : (centre + d - 1) * PITCH + span, :] for d in range(3)]
    taps = jnp.concatenate(taps, 1)
    if by_input:
        weights = jnp.concatenate([pair_weights_by_input(w, d) for d in range(3)], 0)
        y = jnp.dot(taps, weights, preferred_element_type=F32)
    else:
        y = matmul_nt(taps, jnp.concatenate([pair_weights(w, d) for d in range(3)], 1))
    even = y[:, 0:128] + pltpu.roll(y[:, 256:384], 1, 0)
    odd = y[:, 128:256] + pltpu.roll(y[:, 384:512], span - 1, 0)
    return even, odd


def half_conv(x, w, centre, rows):
    span = rows * PITCH
    c = jnp.concatenate
    taps = c([x[(centre + d - 1) * PITCH : (centre + d - 1) * PITCH + span, :] for d in range(3)], 1)
    weights = c([c([w[3 * d + b] for d in range(3)], 1) for b in range(3)], 0)
    y = matmul_nt(taps, weights)
    n = y.shape[1] // 3
    return y[:, n : 2 * n] + pltpu.roll(y[:, :n], 1, 0) + pltpu.roll(y[:, 2 * n :], span - 1, 0)


def net_body(
    n_lat,
    noise, own_c, own_s, edge_a, edge_b, lat_a, lat_b, corner_a, corner_b, state,
    k_in, k_coarse, k_deeper, guide_w, scale, shift, k_noisy, k_block, k_branch, k_out,
    out, x_c, x_s, w_in, w_noisy, w_out, pooled, middle, guide, hidden, inner, mixed, turn,
):
    lat = lax.axis_index("lat")
    top = (lat > 0).astype(F32)
    bottom = (lat < n_lat - 1).astype(F32)
    lon_even = lax.axis_index("lon") % 2 == 0
    lat_even = lat % 2 == 0
    sigma = jnp.full((1, 128), noise[0], F32)
    variance = sigma * sigma + 0.25
    scale_skip = 0.25 / variance
    scale_out = 0.5 * sigma / jnp.sqrt(variance)
    noise_code = jnp.log(sigma) / 4.0
    free = 128 - CH
    for tap in range(9):
        for src, dst in ((k_in, w_in), (k_noisy, w_noisy)):
            dst[tap, CH:, :] = jnp.zeros((free, 128), BF16)
            dst[tap, :CH, :] = src[tap]
        w_out[tap, CH:, :] = jnp.zeros((free, 128), BF16)
        w_out[tap, :CH, :] = k_out[tap]

    slot = lax.broadcasted_iota(jnp.int32, (8, 256), 0)
    lane = lax.broadcasted_iota(jnp.int32, (1, 128), 1)

    def put(c_row, s_row, left, right, middle_c, middle_s):
        x_c[c_row * PITCH : c_row * PITCH + 8, :] = jnp.where(slot > 2, left, 0.0).astype(BF16)
        x_c[c_row * PITCH + 8 : c_row * PITCH + 72, :] = middle_c
        x_c[c_row * PITCH + 72 : c_row * PITCH + 80, :] = jnp.where(slot < 5, right, 0.0).astype(BF16)
        if s_row is not None:
            s_left = jnp.where(slot > 5, pltpu.roll(left, 5, 0), 0.0)
            s_right = jnp.where(slot < 2, pltpu.roll(right, 3, 0), 0.0)
            x_s[s_row * PITCH : s_row * PITCH + 8, :] = s_left.astype(BF16)
            x_s[s_row * PITCH + 8 : s_row * PITCH + 72, :] = middle_s
            x_s[s_row * PITCH + 72 : s_row * PITCH + 80, :] = s_right.astype(BF16)

    for i in range(ROWS):
        a, b = edge_a[i].astype(F32), edge_b[i].astype(F32)
        put(DEEP + i, THIN + i, jnp.where(lon_even, b, a), jnp.where(lon_even, a, b), own_c[i], own_s[i])
    for below in range(2):
        for k in range(DEEP):
            r = k - (DEEP - THIN) if not below else k
            s_row = r if not below else THIN + ROWS + k
            if not 0 <= r < THIN:
                s_row = None
            picks = []
            for half in range(2):
                lanes = slice(128 * half, 128 * half + 128)
                a, b = lat_a[k, :, lanes].astype(F32), lat_b[k, :, lanes].astype(F32)
                value = jnp.where(lat_even, a, b) if below else jnp.where(lat_even, b, a)
                picks.append(jnp.where(lane < CH, value, 0.0).astype(BF16))
            mid_s = None
            if s_row is not None:
                mids = []
                for h in range(2):
                    n = 2 * (2 * r + h)
                    parts = []
                    for m in (n, n + 1):
                        lanes = slice(128 * (m % 2), 128 * (m % 2) + 128)
                        a, b = lat_a[m // 2, :, lanes].astype(F32), lat_b[m // 2, :, lanes].astype(F32)
                        value = jnp.where(lat_even, a, b) if below else jnp.where(lat_even, b, a)
                        parts.append(pltpu.roll(value, (128 - CH + free * (m % 2)) % 128, 1))
                    mids.append(jnp.where(lane < free, parts[0], jnp.where(lane < CH, parts[1], 0.0)).astype(BF16))
                mid_s = jnp.concatenate(mids, 1)
            sides = []
            for side in range(2):
                pair = []
                for corner in (corner_a, corner_b):
                    pair.append(corner[side, k].astype(F32))
                sides.append(jnp.where(lat_even, pair[0], pair[1]) if below else jnp.where(lat_even, pair[1], pair[0]))
            row = DEEP + ROWS + k if below else k
            put(row, s_row, sides[0], sides[1], jnp.concatenate(picks, 1), mid_s)

    for ch in range(8):
        even, odd = pair_conv(x_c, w_in, 1 + 4 * ch, 4, True)
        both = silu(even).astype(BF16).astype(F32) + silu(odd).astype(BF16).astype(F32)
        both = both.reshape(2, 2, PITCH, 128)
        mean = (both[:, 0] + both[:, 1]) * 0.25
        if ch < 2 or ch > 5:
            mean = mean * (top if ch < 2 else bottom)
        pooled[2 * ch * PITCH : (2 * ch + 2) * PITCH, :] = mean.reshape(2 * PITCH, 128).astype(BF16)
    for ch in range(7):
        m = silu(half_conv(pooled, k_coarse, 1 + 2 * ch, 2))
        for q in range(2):
            row = 2 * ch + q
            v = m[q * PITCH : (q + 1) * PITCH]
            if row < 3 or row > 10:
                v = v * (top if row < 3 else bottom)
            middle[row * PITCH : (row + 1) * PITCH, :] = v.astype(BF16)
    embedded = scale[...] * noise_code + shift[...]
    for ch in range(6):
        d = silu(half_conv(middle, k_deeper, 1 + 2 * ch, 2)).astype(BF16)
        guide[2 * ch * PITCH : (2 * ch + 2) * PITCH, :] = matmul_nt(d, guide_w[...]) + embedded
    for ch in range(11):
        even, odd = pair_conv(x_s, w_noisy, 1 + 2 * ch, 2, True)
        for q in range(2):
            row = 2 * ch + q
            g = guide[(row + 1) // 2 * PITCH : ((row + 1) // 2 + 1) * PITCH, :]
            for half, v in enumerate((even, odd)):
                v = silu(v[q * PITCH : (q + 1) * PITCH] + g)
                if row < 3 or row > 18:
                    v = v * (top if row < 3 else bottom)
                hidden[row * PITCH : (row + 1) * PITCH, 128 * half : 128 * half + 128] = v.astype(BF16)
    for ch in range(10):
        for half, v in enumerate(pair_conv(hidden, k_block, 1 + 2 * ch, 2)):
            v = silu(v)
            if ch in (0, 9):
                v = v * (top if ch == 0 else bottom)
            inner[2 * ch * PITCH : (2 * ch + 2) * PITCH, 128 * half : 128 * half + 128] = v.astype(BF16)
    for ch in range(9):
        h = hidden[(2 + 2 * ch) * PITCH : (4 + 2 * ch) * PITCH, :].astype(F32)
        for half, v in enumerate(pair_conv(inner, k_branch, 1 + 2 * ch, 2)):
            v = silu(v + h[:, 128 * half : 128 * half + 128])
            for q in range(2):
                row = 2 * ch + q
                u = v[q * PITCH : (q + 1) * PITCH]
                if row in (0, 17):
                    u = u * (top if row == 0 else bottom)
                mixed[row * PITCH : (row + 1) * PITCH, 128 * half : 128 * half + 128] = u.astype(BF16)
    for ch in range(8):
        even, odd = pair_conv(mixed, w_out, 1 + 2 * ch, 2)
        for q in range(2):
            row = 2 * ch + q
            at = q * PITCH + EDGE
            turn[row, pl.ds(0, PAIRS, stride=2), :] = even[at : at + PAIRS]
            turn[row, pl.ds(1, PAIRS, stride=2), :] = odd[at : at + PAIRS]
            head = turn[row].T[:CH]
            here = pl.ds(row, CH, stride=ROWS)
            out[here, :] = scale_skip * state[here, :] + scale_out * head


def net(n_lat, *args):
    vm = pl.BlockSpec(memory_space=VMEM)
    return pl.pallas_call(
        functools.partial(net_body, n_lat),
        out_shape=jax.ShapeDtypeStruct((CH * ROWS, 128), F32),
        in_specs=[pl.BlockSpec(memory_space=pltpu.SMEM)] + [vm] * (len(args) - 1),
        out_specs=vm,
        scratch_shapes=[
            VMEM((34 * PITCH, 256), BF16),
            VMEM((24 * PITCH, 256), BF16),
            VMEM((9, 128, 128), BF16),
            VMEM((9, 128, 128), BF16),
            VMEM((9, 128, 128), BF16),
            VMEM((16 * PITCH, 128), BF16),
            VMEM((14 * PITCH, 256), BF16),
            VMEM((12 * PITCH, 128), F32),
            VMEM((22 * PITCH, 256), BF16),
            VMEM((20 * PITCH, 256), BF16),
            VMEM((18 * PITCH, 256), BF16),
            VMEM((ROWS, 128, 128), F32),
        ],
        compiler_params=pltpu.CompilerParams(vmem_limit_bytes=24 << 20),
        name="net",
    )(*args)


def on_device(
    mesh_shape,
    conditions,
    noisy_state,
    noise_level,
    kernel_input,
    kernel_coarse,
    kernel_deeper,
    guide_weight,
    time_scale,
    time_shift,
    kernel_noisy,
    kernel_block,
    kernel_branch,
    kernel_output,
):
    lon_even, lat_even = lax.axis_index("lon") % 2 == 0, lax.axis_index("lat") % 2 == 0
    cond = conditions.reshape(CH * ROWS, 128)
    state = noisy_state.reshape(CH * ROWS, 128)
    own_c, own_s, edge_a, edge_b, lat_a, lat_b = prep(noise_level, cond, state)
    permute = lambda value, a, o: lax.ppermute(value, AXES, swap_pairs(mesh_shape, a, o))
    edge_a = permute(edge_a, None, "A")
    edge_b = permute(edge_b, None, "B")
    lat_a = permute(lat_a, "A", None)
    lat_b = permute(lat_b, "B", None)
    sides = jnp.stack([jnp.where(lon_even, edge_b, edge_a), jnp.where(lon_even, edge_a, edge_b)])
    first, last = sides[:, :DEEP], sides[:, ROWS - DEEP :]
    corner_a = permute(jnp.where(lat_even, last, first), "A", None)
    corner_b = permute(jnp.where(lat_even, first, last), "B", None)
    by_input = lambda kernel: kernel.transpose(0, 2, 1)
    out = net(
        mesh_shape[1],
        noise_level, own_c, own_s, edge_a, edge_b, lat_a, lat_b, corner_a, corner_b, state,
        by_input(kernel_input), kernel_coarse, kernel_deeper, guide_weight, time_scale[None], time_shift[None],
        by_input(kernel_noisy), kernel_block, kernel_branch, kernel_output,
    )
    return out.reshape(noisy_state.shape)


def solution(mesh):
    tile = P(None, "lat", "lon")
    member = P(None, None, "lat", "lon")
    return jax.shard_map(
        functools.partial(on_device, (mesh.shape["lon"], mesh.shape["lat"])),
        mesh=mesh,
        in_specs=(tile, member) + (P(),) * 11,
        out_specs=member,
        check_vma=False,
    )
```

```python
import functools

import jax
import jax.numpy as jnp
from jax import lax
from jax.experimental import pallas as pl
from jax.experimental.pallas import tpu as pltpu
from jax.sharding import PartitionSpec as P

F32 = jnp.float32
BF16 = jnp.bfloat16
PITCH = 80
EDGE = 8
ROWS = 16
PAIRS = 64
CH = 80
DEEP = 9
THIN = 4
VMEM = pltpu.VMEM
AXES = ("lon", "lat")


def swap_pairs(mesh_shape, lat, lon):
    n_lon, n_lat = mesh_shape
    pairs = []
    for o in range(n_lon):
        for a in range(n_lat):
            b, p = a, o
            if lat:
                b = a ^ 1 if lat == "A" else a - 1 + 2 * (a % 2)
            if lon:
                p = (o ^ 1 if lon == "A" else o - 1 + 2 * (o % 2)) % n_lon
            if 0 <= b < n_lat:
                pairs.append((o * n_lat + a, p * n_lat + b))
    return pairs


def silu(v):
    h = v * 0.5
    return h + h * jnp.tanh(h)


def matmul_nt(x, w):
    return lax.dot_general(x, w, (((1,), (1,)), ((), ())), preferred_element_type=F32)


def prep_body(noise, cond_hbm, state_hbm, own_c, own_s, edge_a, edge_b, lat_a, lat_b, cond, state, work, arrived):
    copies = [
        pltpu.make_async_copy(cond_hbm, cond, arrived.at[0]),
        pltpu.make_async_copy(state_hbm, state, arrived.at[1]),
    ]
    for copy in copies:
        copy.start()
    lon_even = lax.axis_index("lon") % 2 == 0
    lat_even = lax.axis_index("lat") % 2 == 0
    sigma = jnp.full((1, 128), noise[0], F32)
    scale_in = 1.0 / jnp.sqrt(sigma * sigma + 0.25)
    row = lax.broadcasted_iota(jnp.int32, (128, 128), 0)
    col = lax.broadcasted_iota(jnp.int32, (128, 128), 1)
    pick = (col == jnp.where(row < PAIRS, 2 * row, 2 * (row - PAIRS) + 1)).astype(BF16)
    blank = jnp.zeros((128 - CH, 128), BF16)
    slot = lax.broadcasted_iota(jnp.int32, (8, 128), 0)
    for copy in copies:
        copy.wait()
    work[...] = cond[...].astype(F32)
    for i in range(ROWS):
        c_row = work[pl.ds(i, CH, stride=ROWS), :].astype(BF16)
        s_row = (scale_in * state[pl.ds(i, CH, stride=ROWS), :]).astype(BF16)
        both = matmul_nt(pick, jnp.concatenate([c_row, blank, s_row, blank], 0))
        c_pair = jnp.concatenate([both[:PAIRS, :128], both[PAIRS:, :128]], 1)
        s_pair = jnp.concatenate([both[:PAIRS, 128:], both[PAIRS:, 128:]], 1)
        own_c[i] = c_pair.astype(BF16)
        own_s[i] = s_pair.astype(BF16)
        for half in range(2):
            lanes = slice(128 * half, 128 * half + 128)
            left = jnp.where(slot < 5, c_pair[:8, lanes], pltpu.roll(s_pair[:8, lanes], 5, 0))
            right = jnp.where(slot > 2, c_pair[-8:, lanes], pltpu.roll(s_pair[-8:, lanes], 3, 0))
            edge_a[i, :, lanes] = jnp.where(lon_even, right, left).astype(BF16)
            edge_b[i, :, lanes] = jnp.where(lon_even, left, right).astype(BF16)
    lane = lax.broadcasted_iota(jnp.int32, (PAIRS, 128), 1)
    free = 128 - CH
    for k in range(DEEP):
        for half in range(2):
            lanes = slice(128 * half, 128 * half + 128)
            rows = []
            for first, s_first in ((0, 0), (ROWS - DEEP, ROWS - THIN)):
                value = own_c[first + k, :, lanes].astype(F32)
                n = 2 * k + half
                if n < 4 * THIN:
                    r, h = divmod(n // 2, 2)
                    part = own_s[s_first + r, :, 128 * h : 128 * h + 128].astype(F32)
                    part = pltpu.roll(part, (CH - free * (n % 2)) % 128, 1)
                    value = jnp.where(lane < CH, value, part)
                rows.append(value)
            lat_a[k, :, lanes] = jnp.where(lat_even, rows[1], rows[0]).astype(BF16)
            lat_b[k, :, lanes] = jnp.where(lat_even, rows[0], rows[1]).astype(BF16)


def prep(noise, cond, state):
    vm = pl.BlockSpec(memory_space=VMEM)
    own = jax.ShapeDtypeStruct((ROWS, PAIRS, 256), BF16)
    edge = jax.ShapeDtypeStruct((ROWS, 8, 256), BF16)
    rows = jax.ShapeDtypeStruct((DEEP, PAIRS, 256), BF16)
    return pl.pallas_call(
        prep_body,
        out_shape=(own, own, edge, edge, rows, rows),
        in_specs=[pl.BlockSpec(memory_space=pltpu.SMEM)] + [pl.BlockSpec(memory_space=pltpu.HBM)] * 2,
        out_specs=[vm] * 6,
        scratch_shapes=[
            VMEM((CH * ROWS, 128), BF16),
            VMEM((CH * ROWS, 128), F32),
            VMEM((CH * ROWS, 128), F32),
            pltpu.SemaphoreType.DMA((2,)),
        ],
        compiler_params=pltpu.CompilerParams(vmem_limit_bytes=12 << 20),
        name="prep",
    )(noise, cond, state)


def pair_weights(w, di):
    k0, k1, k2 = w[3 * di], w[3 * di + 1], w[3 * di + 2]
    z = jnp.zeros_like(k0)
    c = jnp.concatenate
    return c([c([k1, k2], 1), c([k0, k1], 1), c([z, k0], 1), c([k2, z], 1)], 0)


def pair_weights_by_input(w, di):
    k0, k1, k2 = w[3 * di], w[3 * di + 1], w[3 * di + 2]
    z = jnp.zeros_like(k0)
    c = jnp.concatenate
    return c([c([k1, k0, z, k2], 1), c([k2, k1, k0, z], 1)], 0)


def pair_conv(x, w, centre, rows, by_input=False):
    span = rows * PITCH
    taps = [x[(centre + d - 1) * PITCH : (centre + d - 1) * PITCH + span, :] for d in range(3)]
    taps = jnp.concatenate(taps, 1)
    if by_input:
        weights = jnp.concatenate([pair_weights_by_input(w, d) for d in range(3)], 0)
        y = jnp.dot(taps, weights, preferred_element_type=F32)
    else:
        y = matmul_nt(taps, jnp.concatenate([pair_weights(w, d) for d in range(3)], 1))
    even = y[:, 0:128] + pltpu.roll(y[:, 256:384], 1, 0)
    odd = y[:, 128:256] + pltpu.roll(y[:, 384:512], span - 1, 0)
    return even, odd


def half_conv(x, w, centre, rows):
    span = rows * PITCH
    c = jnp.concatenate
    taps = c([x[(centre + d - 1) * PITCH : (centre + d - 1) * PITCH + span, :] for d in range(3)], 1)
    weights = c([c([w[3 * d + b] for d in range(3)], 1) for b in range(3)], 0)
    y = matmul_nt(taps, weights)
    n = y.shape[1] // 3
    return y[:, n : 2 * n] + pltpu.roll(y[:, :n], 1, 0) + pltpu.roll(y[:, 2 * n :], span - 1, 0)


def pool(x, w, centre, rows):
    even, odd = pair_conv(x, w, centre, rows, True)
    both = silu(even).astype(BF16).astype(F32) + silu(odd).astype(BF16).astype(F32)
    both = both.reshape(rows // 2, 2, PITCH, 128)
    return ((both[:, 0] + both[:, 1]) * 0.25).reshape(rows // 2 * PITCH, 128)


def put_row(x_c, c_row, x_s, s_row, left, right, middle_c, middle_s):
    slot = lax.broadcasted_iota(jnp.int32, (8, 256), 0)
    if c_row is not None:
        at = c_row * PITCH
        x_c[at : at + 8, :] = jnp.where(slot > 2, left, 0.0).astype(BF16)
        x_c[at + 8 : at + 72, :] = middle_c
        x_c[at + 72 : at + 80, :] = jnp.where(slot < 5, right, 0.0).astype(BF16)
    if s_row is not None:
        at = s_row * PITCH
        x_s[at : at + 8, :] = jnp.where(slot > 5, pltpu.roll(left, 5, 0), 0.0).astype(BF16)
        x_s[at + 8 : at + 72, :] = middle_s
        x_s[at + 72 : at + 80, :] = jnp.where(slot < 2, pltpu.roll(right, 3, 0), 0.0).astype(BF16)


def inner_body(
    own_c, own_s, edge_a, edge_b, k_in, k_noisy, k_coarse, k_deeper, k_guide, k_block, k_branch, k_out,
    w_in, w_noisy, w_coarse, w_deeper, w_guide, w_block, w_branch, w_out, pooled, opening, middle, guide,
    x_c, x_s, arrived,
):
    free = 128 - CH
    narrow = lambda w: w.at[:, :CH, :]
    moves = [
        (k_in, narrow(w_in)), (k_noisy, narrow(w_noisy)), (k_coarse, w_coarse), (k_deeper, w_deeper),
        (k_guide, w_guide), (k_block, w_block), (k_branch, w_branch), (k_out, narrow(w_out)),
    ]
    copies = [pltpu.make_async_copy(src, dst, arrived.at[n]) for n, (src, dst) in enumerate(moves)]
    for copy in copies:
        copy.start()
    for w in (w_in, w_noisy, w_out):
        w[:, CH:, :] = jnp.zeros((9, free, 128), BF16)
    lon_even = lax.axis_index("lon") % 2 == 0
    for i in range(ROWS):
        a, b = edge_a[i].astype(F32), edge_b[i].astype(F32)
        put_row(x_c, i, x_s, i, jnp.where(lon_even, b, a), jnp.where(lon_even, a, b), own_c[i], own_s[i])
    copies[0].wait()
    for ch in range(2):
        pooled[3 * ch * PITCH : (3 * ch + 3) * PITCH, :] = pool(x_c, w_in, 2 + 6 * ch, 6).astype(BF16)
    copies[1].wait()
    for ch in range(2):
        for half, v in enumerate(pair_conv(x_s, w_noisy, 1 + 7 * ch, 7, True)):
            opening[7 * ch * PITCH : (7 * ch + 7) * PITCH, 128 * half : 128 * half + 128] = v
    copies[2].wait()
    middle[...] = silu(half_conv(pooled, w_coarse, 1, 4)).astype(BF16)
    copies[3].wait()
    copies[4].wait()
    guide[...] = matmul_nt(silu(half_conv(middle, w_deeper, 1, 2)).astype(BF16), w_guide[...])
    for copy in copies[5:]:
        copy.wait()


def inner(*args):
    vm = pl.BlockSpec(memory_space=VMEM)
    wide = lambda n, k: jax.ShapeDtypeStruct((9, n, k), BF16)
    rows = lambda n, lanes, dtype: jax.ShapeDtypeStruct((n * PITCH, lanes), dtype)
    out_shape = (
        wide(128, 128), wide(128, 128), wide(256, 128), wide(256, 256), jax.ShapeDtypeStruct((128, 256), BF16),
        wide(128, 128), wide(128, 128), wide(128, 128),
        rows(6, 128, BF16), rows(14, 256, F32), rows(4, 256, BF16), rows(2, 128, F32),
    )
    return pl.pallas_call(
        inner_body,
        out_shape=out_shape,
        in_specs=[vm] * 4 + [pl.BlockSpec(memory_space=pltpu.HBM)] * 8,
        out_specs=[vm] * len(out_shape),
        scratch_shapes=[
            VMEM((ROWS * PITCH, 256), BF16),
            VMEM((ROWS * PITCH, 256), BF16),
            pltpu.SemaphoreType.DMA((8,)),
        ],
        compiler_params=pltpu.CompilerParams(vmem_limit_bytes=16 << 20),
        cost_estimate=pl.CostEstimate(flops=3 * 10**9, bytes_accessed=6 * 10**6, transcendentals=10**6),
        name="inner",
    )(*args)


def net_body(
    n_lat,
    noise, own_c, own_s, edge_a, edge_b, lat_a, lat_b, corner_a, corner_b, state, scale, shift,
    w_in, w_noisy, w_coarse, w_deeper, w_guide, w_block, w_branch, w_out, pooled_in, opening, middle_in, guide_in,
    out, x_c, x_s, pooled, middle, guide, hidden, inner, mixed, turn,
):
    lat = lax.axis_index("lat")
    top = (lat > 0).astype(F32)
    bottom = (lat < n_lat - 1).astype(F32)
    lon_even = lax.axis_index("lon") % 2 == 0
    lat_even = lat % 2 == 0
    sigma = jnp.full((1, 128), noise[0], F32)
    variance = sigma * sigma + 0.25
    scale_skip = 0.25 / variance
    scale_out = 0.5 * sigma / jnp.sqrt(variance)
    noise_code = jnp.log(sigma) / 4.0
    free = 128 - CH
    lane = lax.broadcasted_iota(jnp.int32, (1, 128), 1)

    for i in (0, 1, 2, 13, 14, 15):
        a, b = edge_a[i].astype(F32), edge_b[i].astype(F32)
        s_row = THIN + i if i < 2 else i - 8 if i > 13 else None
        put_row(
            x_c, DEEP + i if i < 3 else i - 1, x_s, s_row,
            jnp.where(lon_even, b, a), jnp.where(lon_even, a, b), own_c[i], own_s[i],
        )
    for below in range(2):
        for k in range(DEEP):
            r = k if below else k - (DEEP - THIN)
            s_row = (8 + r if below else r) if 0 <= r < THIN else None
            picks = []
            for half in range(2):
                lanes = slice(128 * half, 128 * half + 128)
                a, b = lat_a[k, :, lanes].astype(F32), lat_b[k, :, lanes].astype(F32)
                value = jnp.where(lat_even, a, b) if below else jnp.where(lat_even, b, a)
                picks.append(jnp.where(lane < CH, value, 0.0).astype(BF16))
            mid_s = None
            if s_row is not None:
                mids = []
                for h in range(2):
                    n = 2 * (2 * r + h)
                    parts = []
                    for m in (n, n + 1):
                        lanes = slice(128 * (m % 2), 128 * (m % 2) + 128)
                        a, b = lat_a[m // 2, :, lanes].astype(F32), lat_b[m // 2, :, lanes].astype(F32)
                        value = jnp.where(lat_even, a, b) if below else jnp.where(lat_even, b, a)
                        parts.append(pltpu.roll(value, (128 - CH + free * (m % 2)) % 128, 1))
                    mids.append(jnp.where(lane < free, parts[0], jnp.where(lane < CH, parts[1], 0.0)).astype(BF16))
                mid_s = jnp.concatenate(mids, 1)
            sides = []
            for side in range(2):
                a, b = corner_a[side, k].astype(F32), corner_b[side, k].astype(F32)
                sides.append(jnp.where(lat_even, a, b) if below else jnp.where(lat_even, b, a))
            put_row(x_c, 15 + k if below else k, x_s, s_row, sides[0], sides[1], jnp.concatenate(picks, 1), mid_s)

    def put(ref, row, rows, value, above, below, lanes=slice(None)):
        for q in range(rows):
            v = value[q * PITCH : (q + 1) * PITCH]
            if row + q < above:
                v = v * top
            if row + q >= below:
                v = v * bottom
            ref[(row + q) * PITCH : (row + q + 1) * PITCH, lanes] = v.astype(ref.dtype)

    pooled[5 * PITCH : 11 * PITCH, :] = pooled_in[...]
    for centre, rows, row in ((1, 10, 0), (13, 10, 11)):
        put(pooled, row, rows // 2, pool(x_c, w_in, centre, rows), 4, 12)
    middle[5 * PITCH : 9 * PITCH, :] = middle_in[...]
    for row, rows in ((0, 5), (9, 5)):
        put(middle, row, rows, silu(half_conv(pooled, w_coarse, row + 1, rows)), 3, 11)
    embedded = scale[...] * noise_code + shift[...]
    guide[5 * PITCH : 7 * PITCH, :] = guide_in[...] + embedded
    for row, rows in ((0, 5), (7, 5)):
        d = silu(half_conv(middle, w_deeper, row + 1, rows)).astype(BF16)
        guide[row * PITCH : (row + rows) * PITCH, :] = matmul_nt(d, w_guide[...]) + embedded
    for row, rows in ((0, 4), (4, 14), (18, 4)):
        if rows == 14:
            sums = opening[:, 0:128], opening[:, 128:256]
        else:
            sums = pair_conv(x_s, w_noisy, 1 if row == 0 else 7, rows, True)
        for half, v in enumerate(sums):
            g = [guide[(row + q + 1) // 2 * PITCH : ((row + q + 1) // 2 + 1) * PITCH, :] for q in range(rows)]
            v = silu(v + jnp.concatenate(g, 0))
            put(hidden, row, rows, v, 3, 19, slice(128 * half, 128 * half + 128))
    for row in (0, 10):
        for half, v in enumerate(pair_conv(hidden, w_block, 1 + row, 10)):
            put(inner, row, 10, silu(v), 2, 18, slice(128 * half, 128 * half + 128))
    for row in (0, 9):
        h = hidden[(2 + row) * PITCH : (11 + row) * PITCH, :].astype(F32)
        for half, v in enumerate(pair_conv(inner, w_branch, 1 + row, 9)):
            lanes = slice(128 * half, 128 * half + 128)
            put(mixed, row, 9, silu(v + h[:, lanes]), 1, 17, lanes)
    for first in (0, 8):
        even, odd = pair_conv(mixed, w_out, 1 + first, 8)
        for q in range(8):
            row = first + q
            at = q * PITCH + EDGE
            turn[row, pl.ds(0, PAIRS, stride=2), :] = even[at : at + PAIRS]
            turn[row, pl.ds(1, PAIRS, stride=2), :] = odd[at : at + PAIRS]
            head = turn[row].T[:CH]
            here = pl.ds(row, CH, stride=ROWS)
            out[here, :] = scale_skip * state[here, :] + scale_out * head


def net(n_lat, *args):
    vm = pl.BlockSpec(memory_space=VMEM)
    return pl.pallas_call(
        functools.partial(net_body, n_lat),
        out_shape=jax.ShapeDtypeStruct((CH * ROWS, 128), F32),
        in_specs=[pl.BlockSpec(memory_space=pltpu.SMEM)] + [vm] * (len(args) - 1),
        out_specs=vm,
        scratch_shapes=[
            VMEM((24 * PITCH, 256), BF16),
            VMEM((12 * PITCH, 256), BF16),
            VMEM((16 * PITCH, 128), BF16),
            VMEM((14 * PITCH, 256), BF16),
            VMEM((12 * PITCH, 128), F32),
            VMEM((22 * PITCH, 256), BF16),
            VMEM((20 * PITCH, 256), BF16),
            VMEM((18 * PITCH, 256), BF16),
            VMEM((ROWS, 128, 128), F32),
        ],
        compiler_params=pltpu.CompilerParams(vmem_limit_bytes=24 << 20),
        name="net",
    )(*args)


def on_device(
    mesh_shape,
    conditions,
    noisy_state,
    noise_level,
    kernel_input,
    kernel_coarse,
    kernel_deeper,
    guide_weight,
    time_scale,
    time_shift,
    kernel_noisy,
    kernel_block,
    kernel_branch,
    kernel_output,
):
    lon_even, lat_even = lax.axis_index("lon") % 2 == 0, lax.axis_index("lat") % 2 == 0
    cond = conditions.reshape(CH * ROWS, 128)
    state = noisy_state.reshape(CH * ROWS, 128)
    own_c, own_s, edge_a, edge_b, lat_a, lat_b = prep(noise_level, *(pltpu.with_memory_space_constraint(value, pltpu.HBM) for value in (cond, state)))
    permute = lambda value, a, o: lax.ppermute(value, AXES, swap_pairs(mesh_shape, a, o))
    edge_a = permute(edge_a, None, "A")
    edge_b = permute(edge_b, None, "B")
    lat_a = permute(lat_a, "A", None)
    lat_b = permute(lat_b, "B", None)
    sides = jnp.stack([jnp.where(lon_even, edge_b, edge_a), jnp.where(lon_even, edge_a, edge_b)])
    first, last = sides[:, :DEEP], sides[:, ROWS - DEEP :]
    corner_a = permute(jnp.where(lat_even, last, first), "A", None)
    corner_b = permute(jnp.where(lat_even, first, last), "B", None)
    by_input = lambda kernel: kernel.transpose(0, 2, 1)
    weights = (
        by_input(kernel_input), by_input(kernel_noisy), kernel_coarse, kernel_deeper,
        guide_weight, kernel_block, kernel_branch, kernel_output,
    )
    in_hbm = lambda value: pltpu.with_memory_space_constraint(value, pltpu.HBM)
    rest = inner(own_c, own_s, edge_a, edge_b, *map(in_hbm, weights))
    out = net(
        mesh_shape[1], noise_level, own_c, own_s, edge_a, edge_b, lat_a, lat_b, corner_a, corner_b, state,
        time_scale[None], time_shift[None], *rest,
    )
    return out.reshape(noisy_state.shape)


def solution(mesh):
    tile = P(None, "lat", "lon")
    member = P(None, None, "lat", "lon")
    return jax.shard_map(
        functools.partial(on_device, (mesh.shape["lon"], mesh.shape["lat"])),
        mesh=mesh,
        in_specs=(tile, member) + (P(),) * 11,
        out_specs=member,
        check_vma=False,
    )
```

```python
import functools

import jax
import jax.numpy as jnp
from jax import lax
from jax.experimental import pallas as pl
from jax.experimental.pallas import tpu as pltpu
from jax.sharding import PartitionSpec as P

F32 = jnp.float32
BF16 = jnp.bfloat16
PITCH = 72
EDGE = 4
WIDE = 80
ROWS = 16
PAIRS = 64
CH = 80
DEEP = 9
THIN = 4
VMEM = pltpu.VMEM
AXES = ("lon", "lat")


def swap_pairs(mesh_shape, lat, lon):
    n_lon, n_lat = mesh_shape
    pairs = []
    for o in range(n_lon):
        for a in range(n_lat):
            b, p = a, o
            if lat:
                b = a ^ 1 if lat == "A" else a - 1 + 2 * (a % 2)
            if lon:
                p = (o ^ 1 if lon == "A" else o - 1 + 2 * (o % 2)) % n_lon
            if 0 <= b < n_lat:
                pairs.append((o * n_lat + a, p * n_lat + b))
    return pairs


def silu(v):
    h = v * 0.5
    return h + h * jnp.tanh(h)


def matmul_nt(x, w):
    return lax.dot_general(x, w, (((1,), (1,)), ((), ())), preferred_element_type=F32)


def prep_body(
    noise, cond_hbm, state_hbm, k_in, k_noisy, own_c, own_s, edge_a, edge_b, lat_a, lat_b, w_in, w_noisy,
    cond, state, work, arrived,
):
    copies = [
        pltpu.make_async_copy(cond_hbm, cond, arrived.at[0]),
        pltpu.make_async_copy(state_hbm, state, arrived.at[1]),
        pltpu.make_async_copy(k_in, w_in.at[:, :CH, :], arrived.at[2]),
        pltpu.make_async_copy(k_noisy, w_noisy.at[:, :CH, :], arrived.at[3]),
    ]
    for copy in copies:
        copy.start()
    lon_even = lax.axis_index("lon") % 2 == 0
    lat_even = lax.axis_index("lat") % 2 == 0
    sigma = jnp.full((1, 128), noise[0], F32)
    scale_in = 1.0 / jnp.sqrt(sigma * sigma + 0.25)
    row = lax.broadcasted_iota(jnp.int32, (128, 128), 0)
    col = lax.broadcasted_iota(jnp.int32, (128, 128), 1)
    pick = (col == jnp.where(row < PAIRS, 2 * row, 2 * (row - PAIRS) + 1)).astype(BF16)
    blank = jnp.zeros((128 - CH, 128), BF16)
    slot = lax.broadcasted_iota(jnp.int32, (8, 128), 0)
    for w in (w_in, w_noisy):
        w[:, CH:, :] = jnp.zeros((9, 128 - CH, 128), BF16)
    for copy in copies[:2]:
        copy.wait()
    work[...] = cond[...].astype(F32)
    for i in range(ROWS):
        c_row = work[pl.ds(i, CH, stride=ROWS), :].astype(BF16)
        s_row = (scale_in * state[pl.ds(i, CH, stride=ROWS), :]).astype(BF16)
        both = matmul_nt(pick, jnp.concatenate([c_row, blank, s_row, blank], 0))
        c_pair = jnp.concatenate([both[:PAIRS, :128], both[PAIRS:, :128]], 1)
        s_pair = jnp.concatenate([both[:PAIRS, 128:], both[PAIRS:, 128:]], 1)
        own_c[i] = c_pair.astype(BF16)
        own_s[i] = s_pair.astype(BF16)
        for half in range(2):
            lanes = slice(128 * half, 128 * half + 128)
            left = jnp.where(slot < 5, c_pair[:8, lanes], pltpu.roll(s_pair[:8, lanes], 5, 0))
            right = jnp.where(slot > 2, c_pair[-8:, lanes], pltpu.roll(s_pair[-8:, lanes], 3, 0))
            edge_a[i, :, lanes] = jnp.where(lon_even, right, left).astype(BF16)
            edge_b[i, :, lanes] = jnp.where(lon_even, left, right).astype(BF16)
    lane = lax.broadcasted_iota(jnp.int32, (PAIRS, 128), 1)
    free = 128 - CH
    for k in range(DEEP):
        for half in range(2):
            lanes = slice(128 * half, 128 * half + 128)
            rows = []
            for first, s_first in ((0, 0), (ROWS - DEEP, ROWS - THIN)):
                value = own_c[first + k, :, lanes].astype(F32)
                n = 2 * k + half
                if n < 4 * THIN:
                    r, h = divmod(n // 2, 2)
                    part = own_s[s_first + r, :, 128 * h : 128 * h + 128].astype(F32)
                    part = pltpu.roll(part, (CH - free * (n % 2)) % 128, 1)
                    value = jnp.where(lane < CH, value, part)
                rows.append(value)
            lat_a[k, :, lanes] = jnp.where(lat_even, rows[1], rows[0]).astype(BF16)
            lat_b[k, :, lanes] = jnp.where(lat_even, rows[0], rows[1]).astype(BF16)
    for copy in copies[2:]:
        copy.wait()


def prep(noise, *args):
    vm = pl.BlockSpec(memory_space=VMEM)
    own = jax.ShapeDtypeStruct((ROWS, PAIRS, 256), BF16)
    edge = jax.ShapeDtypeStruct((ROWS, 8, 256), BF16)
    rows = jax.ShapeDtypeStruct((DEEP, PAIRS, 256), BF16)
    weights = jax.ShapeDtypeStruct((9, 128, 128), BF16)
    return pl.pallas_call(
        prep_body,
        out_shape=(own, own, edge, edge, rows, rows, weights, weights),
        in_specs=[pl.BlockSpec(memory_space=pltpu.SMEM)] + [pl.BlockSpec(memory_space=pltpu.HBM)] * 4,
        out_specs=[vm] * 8,
        scratch_shapes=[
            VMEM((CH * ROWS, 128), BF16),
            VMEM((CH * ROWS, 128), F32),
            VMEM((CH * ROWS, 128), F32),
            pltpu.SemaphoreType.DMA((4,)),
        ],
        compiler_params=pltpu.CompilerParams(vmem_limit_bytes=12 << 20),
        name="prep",
    )(noise, *args)


def pair_weights(w, di):
    k0, k1, k2 = w[3 * di], w[3 * di + 1], w[3 * di + 2]
    z = jnp.zeros_like(k0)
    c = jnp.concatenate
    return c([c([k1, k2], 1), c([k0, k1], 1), c([z, k0], 1), c([k2, z], 1)], 0)


def pair_weights_by_input(w, di):
    k0, k1, k2 = w[3 * di], w[3 * di + 1], w[3 * di + 2]
    z = jnp.zeros_like(k0)
    c = jnp.concatenate
    return c([c([k1, k0, z, k2], 1), c([k2, k1, k0, z], 1)], 0)


def pair_conv(x, w, centre, rows, by_input=False, pitch=PITCH):
    span = rows * pitch
    taps = [x[(centre + d - 1) * pitch : (centre + d - 1) * pitch + span, :] for d in range(3)]
    taps = jnp.concatenate(taps, 1)
    if by_input:
        weights = jnp.concatenate([pair_weights_by_input(w, d) for d in range(3)], 0)
        y = jnp.dot(taps, weights, preferred_element_type=F32)
    else:
        y = matmul_nt(taps, jnp.concatenate([pair_weights(w, d) for d in range(3)], 1))
    even = y[:, 0:128] + pltpu.roll(y[:, 256:384], 1, 0)
    odd = y[:, 128:256] + pltpu.roll(y[:, 384:512], span - 1, 0)
    return even, odd


def half_conv(x, w, centre, rows):
    span = rows * PITCH
    c = jnp.concatenate
    taps = c([x[(centre + d - 1) * PITCH : (centre + d - 1) * PITCH + span, :] for d in range(3)], 1)
    weights = c([c([w[3 * d + b] for d in range(3)], 1) for b in range(3)], 0)
    y = matmul_nt(taps, weights)
    n = y.shape[1] // 3
    return y[:, n : 2 * n] + pltpu.roll(y[:, :n], 1, 0) + pltpu.roll(y[:, 2 * n :], span - 1, 0)


def pool(x, w, centre, rows):
    even, odd = pair_conv(x, w, centre, rows, True, WIDE)
    both = silu(even).astype(BF16).astype(F32) + silu(odd).astype(BF16).astype(F32)
    both = both.reshape(rows // 2, 2, WIDE, 128)
    mean = (both[:, 0] + both[:, 1]) * 0.25
    shift = 8 - EDGE
    return mean[:, shift : shift + PITCH].reshape(rows // 2 * PITCH, 128)


def put_row(x_c, c_row, x_s, s_row, left, right, middle_c, middle_s):
    slot = lax.broadcasted_iota(jnp.int32, (8, 256), 0)
    if c_row is not None:
        at = c_row * WIDE
        x_c[at : at + 8, :] = jnp.where(slot > 2, left, 0.0).astype(BF16)
        x_c[at + 8 : at + 72, :] = middle_c
        x_c[at + 72 : at + 80, :] = jnp.where(slot < 5, right, 0.0).astype(BF16)
    if s_row is not None:
        at = s_row * PITCH
        x_s[at : at + 4, :] = jnp.where(slot > 1, pltpu.roll(left, 1, 0), 0.0)[:4].astype(BF16)
        x_s[at + 4 : at + 68, :] = middle_s
        x_s[at + 68 : at + 72, :] = jnp.where(slot < 2, pltpu.roll(right, 3, 0), 0.0)[:4].astype(BF16)


def inner_body(
    own_c, own_s, edge_a, edge_b, w_in, w_noisy, k_coarse, k_deeper, k_guide, k_block, k_branch, k_out,
    w_coarse, w_deeper, w_guide, w_block, w_branch, w_out, pooled, opening, middle, guide,
    x_c, x_s, arrived,
):
    moves = [
        (k_coarse, w_coarse), (k_deeper, w_deeper), (k_guide, w_guide),
        (k_block, w_block), (k_branch, w_branch), (k_out, w_out.at[:, :CH, :]),
    ]
    copies = [pltpu.make_async_copy(src, dst, arrived.at[n]) for n, (src, dst) in enumerate(moves)]
    for copy in copies:
        copy.start()
    w_out[:, CH:, :] = jnp.zeros((9, 128 - CH, 128), BF16)
    lon_even = lax.axis_index("lon") % 2 == 0
    for i in range(ROWS):
        a, b = edge_a[i].astype(F32), edge_b[i].astype(F32)
        put_row(x_c, i, x_s, i, jnp.where(lon_even, b, a), jnp.where(lon_even, a, b), own_c[i], own_s[i])
    for ch in range(2):
        pooled[3 * ch * PITCH : (3 * ch + 3) * PITCH, :] = pool(x_c, w_in, 2 + 6 * ch, 6).astype(BF16)
    for row, rows in ((0, 6), (6, 8)):
        for half, v in enumerate(pair_conv(x_s, w_noisy, 1 + row, rows, True)):
            opening[row * PITCH : (row + rows) * PITCH, 128 * half : 128 * half + 128] = v
    copies[0].wait()
    middle[...] = silu(half_conv(pooled, w_coarse, 1, 4)).astype(BF16)
    copies[1].wait()
    copies[2].wait()
    guide[...] = matmul_nt(silu(half_conv(middle, w_deeper, 1, 2)).astype(BF16), w_guide[...])
    for copy in copies[3:]:
        copy.wait()


def inner(*args):
    vm = pl.BlockSpec(memory_space=VMEM)
    wide = lambda n, k: jax.ShapeDtypeStruct((9, n, k), BF16)
    rows = lambda n, lanes, dtype: jax.ShapeDtypeStruct((n * PITCH, lanes), dtype)
    out_shape = (
        wide(256, 128), wide(256, 256), jax.ShapeDtypeStruct((128, 256), BF16),
        wide(128, 128), wide(128, 128), wide(128, 128),
        rows(6, 128, BF16), rows(14, 256, F32), rows(4, 256, BF16), rows(2, 128, F32),
    )
    return pl.pallas_call(
        inner_body,
        out_shape=out_shape,
        in_specs=[vm] * 6 + [pl.BlockSpec(memory_space=pltpu.HBM)] * 6,
        out_specs=[vm] * len(out_shape),
        scratch_shapes=[
            VMEM((ROWS * WIDE, 256), BF16),
            VMEM((ROWS * PITCH, 256), BF16),
            pltpu.SemaphoreType.DMA((6,)),
        ],
        compiler_params=pltpu.CompilerParams(vmem_limit_bytes=16 << 20),
        cost_estimate=pl.CostEstimate(flops=3 * 10**9, bytes_accessed=6 * 10**6, transcendentals=10**6),
        name="inner",
    )(*args)


def net_body(
    n_lat,
    noise, own_c, own_s, edge_a, edge_b, lat_a, lat_b, corner_a, corner_b, state, scale, shift,
    w_in, w_noisy, w_coarse, w_deeper, w_guide, w_block, w_branch, w_out, pooled_in, opening, middle_in, guide_in,
    out, x_c, x_s, pooled, middle, guide, hidden, inner, mixed, turn,
):
    lat = lax.axis_index("lat")
    top = (lat > 0).astype(F32)
    bottom = (lat < n_lat - 1).astype(F32)
    lon_even = lax.axis_index("lon") % 2 == 0
    lat_even = lat % 2 == 0
    sigma = jnp.full((1, 128), noise[0], F32)
    variance = sigma * sigma + 0.25
    scale_skip = 0.25 / variance
    scale_out = 0.5 * sigma / jnp.sqrt(variance)
    noise_code = jnp.log(sigma) / 4.0
    free = 128 - CH
    lane = lax.broadcasted_iota(jnp.int32, (1, 128), 1)

    for i in (0, 1, 2, 13, 14, 15):
        a, b = edge_a[i].astype(F32), edge_b[i].astype(F32)
        s_row = THIN + i if i < 2 else i - 8 if i > 13 else None
        put_row(
            x_c, DEEP + i if i < 3 else i - 1, x_s, s_row,
            jnp.where(lon_even, b, a), jnp.where(lon_even, a, b), own_c[i], own_s[i],
        )
    for below in range(2):
        for k in range(DEEP):
            r = k if below else k - (DEEP - THIN)
            s_row = (8 + r if below else r) if 0 <= r < THIN else None
            picks = []
            for half in range(2):
                lanes = slice(128 * half, 128 * half + 128)
                a, b = lat_a[k, :, lanes].astype(F32), lat_b[k, :, lanes].astype(F32)
                value = jnp.where(lat_even, a, b) if below else jnp.where(lat_even, b, a)
                picks.append(jnp.where(lane < CH, value, 0.0).astype(BF16))
            mid_s = None
            if s_row is not None:
                mids = []
                for h in range(2):
                    n = 2 * (2 * r + h)
                    parts = []
                    for m in (n, n + 1):
                        lanes = slice(128 * (m % 2), 128 * (m % 2) + 128)
                        a, b = lat_a[m // 2, :, lanes].astype(F32), lat_b[m // 2, :, lanes].astype(F32)
                        value = jnp.where(lat_even, a, b) if below else jnp.where(lat_even, b, a)
                        parts.append(pltpu.roll(value, (128 - CH + free * (m % 2)) % 128, 1))
                    mids.append(jnp.where(lane < free, parts[0], jnp.where(lane < CH, parts[1], 0.0)).astype(BF16))
                mid_s = jnp.concatenate(mids, 1)
            sides = []
            for side in range(2):
                a, b = corner_a[side, k].astype(F32), corner_b[side, k].astype(F32)
                sides.append(jnp.where(lat_even, a, b) if below else jnp.where(lat_even, b, a))
            put_row(x_c, 15 + k if below else k, x_s, s_row, sides[0], sides[1], jnp.concatenate(picks, 1), mid_s)

    def put(ref, row, rows, value, above, below, lanes=slice(None)):
        over = min(max(above - row, 0), rows)
        under = min(max(row + rows - below, 0), rows)
        parts = [value[over * PITCH : (rows - under) * PITCH]]
        if over:
            parts.insert(0, value[: over * PITCH] * top)
        if under:
            parts.append(value[(rows - under) * PITCH :] * bottom)
        ref[row * PITCH : (row + rows) * PITCH, lanes] = jnp.concatenate(parts, 0).astype(ref.dtype)

    pooled[5 * PITCH : 11 * PITCH, :] = pooled_in[...]
    for centre, rows, row in ((1, 10, 0), (13, 10, 11)):
        put(pooled, row, rows // 2, pool(x_c, w_in, centre, rows), 4, 12)
    middle[5 * PITCH : 9 * PITCH, :] = middle_in[...]
    for row, rows in ((0, 5), (9, 5)):
        put(middle, row, rows, silu(half_conv(pooled, w_coarse, row + 1, rows)), 3, 11)
    embedded = scale[...] * noise_code + shift[...]
    guide[5 * PITCH : 7 * PITCH, :] = guide_in[...] + embedded
    for row, rows in ((0, 5), (7, 5)):
        d = silu(half_conv(middle, w_deeper, row + 1, rows)).astype(BF16)
        guide[row * PITCH : (row + rows) * PITCH, :] = matmul_nt(d, w_guide[...]) + embedded
    for row, rows in ((0, 4), (4, 14), (18, 4)):
        if rows == 14:
            sums = opening[:, 0:128], opening[:, 128:256]
        else:
            sums = pair_conv(x_s, w_noisy, 1 if row == 0 else 7, rows, True)
        for half, v in enumerate(sums):
            g = [guide[(row + q + 1) // 2 * PITCH : ((row + q + 1) // 2 + 1) * PITCH, :] for q in range(rows)]
            v = silu(v + jnp.concatenate(g, 0))
            put(hidden, row, rows, v, 3, 19, slice(128 * half, 128 * half + 128))
    for row in (0, 10):
        for half, v in enumerate(pair_conv(hidden, w_block, 1 + row, 10)):
            put(inner, row, 10, silu(v), 2, 18, slice(128 * half, 128 * half + 128))
    for row, rows in ((0, 10), (10, 8)):
        h = hidden[(2 + row) * PITCH : (2 + row + rows) * PITCH, :].astype(F32)
        for half, v in enumerate(pair_conv(inner, w_branch, 1 + row, rows)):
            lanes = slice(128 * half, 128 * half + 128)
            put(mixed, row, rows, silu(v + h[:, lanes]), 1, 17, lanes)
    for first, rows in ((0, 6), (6, 6), (12, 4)):
        even, odd = pair_conv(mixed, w_out, 1 + first, rows)
        for q in range(rows):
            row = first + q
            at = slice(q * PITCH, (q + 1) * PITCH)
            turn[row, pl.ds(0, PITCH, stride=2), :] = even[at]
            turn[row, pl.ds(1, PITCH, stride=2), :] = odd[at]
            head = turn[row, 2 * EDGE : 2 * (EDGE + PAIRS), :].T[:CH]
            here = pl.ds(row, CH, stride=ROWS)
            out[here, :] = scale_skip * state[here, :] + scale_out * head


def net(n_lat, *args):
    vm = pl.BlockSpec(memory_space=VMEM)
    return pl.pallas_call(
        functools.partial(net_body, n_lat),
        out_shape=jax.ShapeDtypeStruct((CH * ROWS, 128), F32),
        in_specs=[pl.BlockSpec(memory_space=pltpu.SMEM)] + [vm] * (len(args) - 1),
        out_specs=vm,
        scratch_shapes=[
            VMEM((24 * WIDE, 256), BF16),
            VMEM((12 * PITCH, 256), BF16),
            VMEM((16 * PITCH, 128), BF16),
            VMEM((14 * PITCH, 256), BF16),
            VMEM((12 * PITCH, 128), F32),
            VMEM((22 * PITCH, 256), BF16),
            VMEM((20 * PITCH, 256), BF16),
            VMEM((18 * PITCH, 256), BF16),
            VMEM((ROWS, 2 * PITCH, 128), F32),
        ],
        compiler_params=pltpu.CompilerParams(vmem_limit_bytes=24 << 20),
        name="net",
    )(*args)


def on_device(
    mesh_shape,
    conditions,
    noisy_state,
    noise_level,
    kernel_input,
    kernel_coarse,
    kernel_deeper,
    guide_weight,
    time_scale,
    time_shift,
    kernel_noisy,
    kernel_block,
    kernel_branch,
    kernel_output,
):
    lon_even, lat_even = lax.axis_index("lon") % 2 == 0, lax.axis_index("lat") % 2 == 0
    cond = conditions.reshape(CH * ROWS, 128)
    state = noisy_state.reshape(CH * ROWS, 128)
    by_input = lambda kernel: kernel.transpose(0, 2, 1)
    in_hbm = lambda *values: [pltpu.with_memory_space_constraint(value, pltpu.HBM) for value in values]
    own_c, own_s, edge_a, edge_b, lat_a, lat_b, w_in, w_noisy = prep(
        noise_level, *in_hbm(cond, state, by_input(kernel_input), by_input(kernel_noisy))
    )
    permute = lambda value, a, o: lax.ppermute(value, AXES, swap_pairs(mesh_shape, a, o))
    edge_b = permute(edge_b, None, "B")
    edge_a = permute(edge_a, None, "A")
    lat_a = permute(lat_a, "A", None)
    lat_b = permute(lat_b, "B", None)
    sides = jnp.stack([jnp.where(lon_even, edge_b, edge_a), jnp.where(lon_even, edge_a, edge_b)])
    first, last = sides[:, :DEEP], sides[:, ROWS - DEEP :]
    corner_a = permute(jnp.where(lat_even, last, first), "A", None)
    corner_b = permute(jnp.where(lat_even, first, last), "B", None)
    weights = in_hbm(kernel_coarse, kernel_deeper, guide_weight, kernel_block, kernel_branch, kernel_output)
    rest = inner(own_c, own_s, edge_a, edge_b, w_in, w_noisy, *weights)
    out = net(
        mesh_shape[1], noise_level, own_c, own_s, edge_a, edge_b, lat_a, lat_b, corner_a, corner_b, state,
        time_scale[None], time_shift[None], w_in, w_noisy, *rest,
    )
    return out.reshape(noisy_state.shape)


def solution(mesh):
    tile = P(None, "lat", "lon")
    member = P(None, None, "lat", "lon")
    return jax.shard_map(
        functools.partial(on_device, (mesh.shape["lon"], mesh.shape["lat"])),
        mesh=mesh,
        in_specs=(tile, member) + (P(),) * 11,
        out_specs=member,
        check_vma=False,
    )
```

```python
import functools

import jax
import jax.numpy as jnp
from jax import lax
from jax.experimental import pallas as pl
from jax.experimental.pallas import tpu as pltpu
from jax.sharding import PartitionSpec as P

F32 = jnp.float32
BF16 = jnp.bfloat16
PITCH = 72
EDGE = 4
STRIP = 16
ROWS = 16
PAIRS = 64
CH = 80
DEEP = 9
THIN = 4
VMEM = pltpu.VMEM
AXES = ("lon", "lat")


def swap_pairs(mesh_shape, lat, lon):
    n_lon, n_lat = mesh_shape
    pairs = []
    for o in range(n_lon):
        for a in range(n_lat):
            b, p = a, o
            if lat:
                b = a ^ 1 if lat == "A" else a - 1 + 2 * (a % 2)
            if lon:
                p = (o ^ 1 if lon == "A" else o - 1 + 2 * (o % 2)) % n_lon
            if 0 <= b < n_lat:
                pairs.append((o * n_lat + a, p * n_lat + b))
    return pairs


def silu(v):
    h = v * 0.5
    return h + h * jnp.tanh(h)


def matmul_nt(x, w):
    return lax.dot_general(x, w, (((1,), (1,)), ((), ())), preferred_element_type=F32)


def prep_body(
    noise, cond_hbm, state_hbm, k_in, k_noisy, own_c, own_s, left, right, small_a, small_b, lat_a, lat_b, w_in, w_noisy,
    cond, state, work, arrived,
):
    copies = [
        pltpu.make_async_copy(cond_hbm, cond, arrived.at[0]),
        pltpu.make_async_copy(state_hbm, state, arrived.at[1]),
        pltpu.make_async_copy(k_in, w_in.at[:, :CH, :], arrived.at[2]),
        pltpu.make_async_copy(k_noisy, w_noisy.at[:, :CH, :], arrived.at[3]),
    ]
    for copy in copies:
        copy.start()
    lat_even = lax.axis_index("lat") % 2 == 0
    sigma = jnp.full((1, 128), noise[0], F32)
    scale_in = 1.0 / jnp.sqrt(sigma * sigma + 0.25)
    row = lax.broadcasted_iota(jnp.int32, (128, 128), 0)
    col = lax.broadcasted_iota(jnp.int32, (128, 128), 1)
    pick = (col == jnp.where(row < PAIRS, 2 * row, 2 * (row - PAIRS) + 1)).astype(BF16)
    blank = jnp.zeros((128 - CH, 128), BF16)
    slot = lax.broadcasted_iota(jnp.int32, (8, 128), 0)
    for w in (w_in, w_noisy):
        w[:, CH:, :] = jnp.zeros((9, 128 - CH, 128), BF16)
    for copy in copies[:2]:
        copy.wait()
    work[...] = cond[...].astype(F32)
    for i in range(ROWS):
        c_row = work[pl.ds(i, CH, stride=ROWS), :].astype(BF16)
        s_row = (scale_in * state[pl.ds(i, CH, stride=ROWS), :]).astype(BF16)
        both = matmul_nt(pick, jnp.concatenate([c_row, blank, s_row, blank], 0))
        c_pair = jnp.concatenate([both[:PAIRS, :128], both[PAIRS:, :128]], 1)
        s_pair = jnp.concatenate([both[:PAIRS, 128:], both[PAIRS:, 128:]], 1)
        own_c[i] = c_pair.astype(BF16)
        own_s[i] = s_pair.astype(BF16)
        for half in range(2):
            lanes = slice(128 * half, 128 * half + 128)
            left[i, :, lanes] = jnp.where(slot < 5, c_pair[:8, lanes], pltpu.roll(s_pair[:8, lanes], 5, 0)).astype(BF16)
            right[i, :, lanes] = jnp.where(slot > 2, c_pair[-8:, lanes], pltpu.roll(s_pair[-8:, lanes], 3, 0)).astype(BF16)
    for side, edge in enumerate((left, right)):
        first, last = edge[:DEEP].astype(F32), edge[ROWS - DEEP :].astype(F32)
        small_a[side] = jnp.where(lat_even, last, first).astype(BF16)
        small_b[side] = jnp.where(lat_even, first, last).astype(BF16)
    lane = lax.broadcasted_iota(jnp.int32, (PAIRS, 128), 1)
    free = 128 - CH
    for k in range(DEEP):
        for half in range(2):
            lanes = slice(128 * half, 128 * half + 128)
            rows = []
            for first, s_first in ((0, 0), (ROWS - DEEP, ROWS - THIN)):
                value = own_c[first + k, :, lanes].astype(F32)
                n = 2 * k + half
                if n < 4 * THIN:
                    r, h = divmod(n // 2, 2)
                    part = own_s[s_first + r, :, 128 * h : 128 * h + 128].astype(F32)
                    part = pltpu.roll(part, (CH - free * (n % 2)) % 128, 1)
                    value = jnp.where(lane < CH, value, part)
                rows.append(value)
            lat_a[k, :, lanes] = jnp.where(lat_even, rows[1], rows[0]).astype(BF16)
            lat_b[k, :, lanes] = jnp.where(lat_even, rows[0], rows[1]).astype(BF16)
    for copy in copies[2:]:
        copy.wait()


def prep(noise, *args):
    vm = pl.BlockSpec(memory_space=VMEM)
    own = jax.ShapeDtypeStruct((ROWS, PAIRS, 256), BF16)
    edge = jax.ShapeDtypeStruct((ROWS, 8, 256), BF16)
    small = jax.ShapeDtypeStruct((2, DEEP, 8, 256), BF16)
    rows = jax.ShapeDtypeStruct((DEEP, PAIRS, 256), BF16)
    weights = jax.ShapeDtypeStruct((9, 128, 128), BF16)
    return pl.pallas_call(
        prep_body,
        out_shape=(own, own, edge, edge, small, small, rows, rows, weights, weights),
        in_specs=[pl.BlockSpec(memory_space=pltpu.SMEM)] + [pl.BlockSpec(memory_space=pltpu.HBM)] * 4,
        out_specs=[vm] * 10,
        scratch_shapes=[
            VMEM((CH * ROWS, 128), BF16),
            VMEM((CH * ROWS, 128), F32),
            VMEM((CH * ROWS, 128), F32),
            pltpu.SemaphoreType.DMA((4,)),
        ],
        compiler_params=pltpu.CompilerParams(vmem_limit_bytes=12 << 20),
        name="prep",
    )(noise, *args)


def pair_weights(w, di):
    k0, k1, k2 = w[3 * di], w[3 * di + 1], w[3 * di + 2]
    z = jnp.zeros_like(k0)
    c = jnp.concatenate
    return c([c([k1, k2], 1), c([k0, k1], 1), c([z, k0], 1), c([k2, z], 1)], 0)


def pair_weights_by_input(w, di):
    k0, k1, k2 = w[3 * di], w[3 * di + 1], w[3 * di + 2]
    z = jnp.zeros_like(k0)
    c = jnp.concatenate
    return c([c([k1, k0, z, k2], 1), c([k2, k1, k0, z], 1)], 0)


def pair_conv(x, w, centre, rows, by_input=False, pitch=PITCH):
    span = rows * pitch
    taps = [x[(centre + d - 1) * pitch : (centre + d - 1) * pitch + span, :] for d in range(3)]
    taps = jnp.concatenate(taps, 1)
    if by_input:
        weights = jnp.concatenate([pair_weights_by_input(w, d) for d in range(3)], 0)
        y = jnp.dot(taps, weights, preferred_element_type=F32)
    else:
        y = matmul_nt(taps, jnp.concatenate([pair_weights(w, d) for d in range(3)], 1))
    even = y[:, 0:128] + pltpu.roll(y[:, 256:384], 1, 0)
    odd = y[:, 128:256] + pltpu.roll(y[:, 384:512], span - 1, 0)
    return even, odd


def half_conv(x, w, centre, rows):
    span = rows * PITCH
    c = jnp.concatenate
    taps = c([x[(centre + d - 1) * PITCH : (centre + d - 1) * PITCH + span, :] for d in range(3)], 1)
    weights = c([c([w[3 * d + b] for d in range(3)], 1) for b in range(3)], 0)
    y = matmul_nt(taps, weights)
    n = y.shape[1] // 3
    return y[:, n : 2 * n] + pltpu.roll(y[:, :n], 1, 0) + pltpu.roll(y[:, 2 * n :], span - 1, 0)


def pool(x, w, centre, rows, pitch):
    even, odd = pair_conv(x, w, centre, rows, True, pitch)
    both = silu(even).astype(BF16).astype(F32) + silu(odd).astype(BF16).astype(F32)
    both = both.reshape(rows // 2, 2, pitch, 128)
    return (both[:, 0] + both[:, 1]) * 0.25


def band(n_lat):
    lat = lax.axis_index("lat")
    return (lat > 0).astype(F32), (lat < n_lat - 1).astype(F32)


def inner_body(
    n_lat,
    own_c, own_s, lat_a, lat_b, w_in, w_noisy, k_coarse, k_deeper, k_guide, k_block, k_branch, k_out,
    w_coarse, w_deeper, w_guide, w_block, w_branch, w_out, pooled, opening,
    x_c, x_s, arrived,
):
    moves = [
        (k_coarse, w_coarse), (k_deeper, w_deeper), (k_guide, w_guide),
        (k_block, w_block), (k_branch, w_branch), (k_out, w_out.at[:, :CH, :]),
    ]
    copies = [pltpu.make_async_copy(src, dst, arrived.at[n]) for n, (src, dst) in enumerate(moves)]
    for copy in copies:
        copy.start()
    w_out[:, CH:, :] = jnp.zeros((9, 128 - CH, 128), BF16)
    top, bottom = band(n_lat)
    lat_even = lax.axis_index("lat") % 2 == 0
    free = 128 - CH
    lane = lax.broadcasted_iota(jnp.int32, (1, 128), 1)
    x_c[DEEP * PAIRS : (DEEP + ROWS) * PAIRS, :] = own_c[...].reshape(ROWS * PAIRS, 256)
    x_s[THIN * PAIRS : (THIN + ROWS) * PAIRS, :] = own_s[...].reshape(ROWS * PAIRS, 256)
    for below in range(2):

        def received(k, lanes):
            a, b = lat_a[k, :, lanes].astype(F32), lat_b[k, :, lanes].astype(F32)
            return jnp.where(lat_even, a, b) if below else jnp.where(lat_even, b, a)

        for k in range(DEEP):
            at = (DEEP + ROWS + k if below else k) * PAIRS
            x_c[at : at + PAIRS, :] = received(k, slice(None)).astype(BF16)
        for r in range(THIN):
            at = (THIN + ROWS + r if below else r) * PAIRS
            for h in range(2):
                n = 2 * (2 * r + h)
                parts = [
                    pltpu.roll(received(m // 2, slice(128 * (m % 2), 128 * (m % 2) + 128)), (128 - CH + free * (m % 2)) % 128, 1)
                    for m in (n, n + 1)
                ]
                x_s[at : at + PAIRS, 128 * h : 128 * h + 128] = jnp.where(lane < free, *parts).astype(BF16)
    for row, rows in ((0, 5), (5, 5), (10, 6)):
        mean = pool(x_c, w_in, 1 + 2 * row, 2 * rows, PAIRS)
        for q in range(rows):
            v = mean[q]
            if row + q < 4:
                v = v * top
            if row + q >= 12:
                v = v * bottom
            at = (row + q) * PITCH + EDGE
            pooled[at : at + PAIRS, :] = v.astype(BF16)
    for row, rows in ((0, 10), (10, 12)):
        for half, v in enumerate(pair_conv(x_s, w_noisy, 1 + row, rows, True, PAIRS)):
            for q in range(rows):
                at = (row + q) * PITCH + EDGE
                opening[at : at + PAIRS, 128 * half : 128 * half + 128] = v[q * PAIRS : (q + 1) * PAIRS]
    for copy in copies:
        copy.wait()


def inner(n_lat, *args):
    vm = pl.BlockSpec(memory_space=VMEM)
    wide = lambda n, k: jax.ShapeDtypeStruct((9, n, k), BF16)
    out_shape = (
        wide(256, 128), wide(256, 256), jax.ShapeDtypeStruct((128, 256), BF16),
        wide(128, 128), wide(128, 128), wide(128, 128),
        jax.ShapeDtypeStruct((16 * PITCH, 128), BF16), jax.ShapeDtypeStruct((22 * PITCH, 256), F32),
    )
    return pl.pallas_call(
        functools.partial(inner_body, n_lat),
        out_shape=out_shape,
        in_specs=[vm] * 6 + [pl.BlockSpec(memory_space=pltpu.HBM)] * 6,
        out_specs=[vm] * len(out_shape),
        scratch_shapes=[
            VMEM((34 * PAIRS, 256), BF16),
            VMEM((24 * PAIRS, 256), BF16),
            pltpu.SemaphoreType.DMA((6,)),
        ],
        compiler_params=pltpu.CompilerParams(vmem_limit_bytes=20 << 20),
        cost_estimate=pl.CostEstimate(flops=3 * 10**9, bytes_accessed=6 * 10**6, transcendentals=10**6),
        name="inner",
    )(*args)


def net_body(
    n_lat,
    noise, sent_a, sent_b, edge_a, edge_b, state, scale, shift,
    w_in, w_noisy, w_coarse, w_deeper, w_guide, w_block, w_branch, w_out, pooled_in, opening,
    out, x_c, x_s, pooled, middle, guide, hidden, inner, mixed, turn,
):
    top, bottom = band(n_lat)
    lon_even = lax.axis_index("lon") % 2 == 0
    sigma = jnp.full((1, 128), noise[0], F32)
    variance = sigma * sigma + 0.25
    scale_skip = 0.25 / variance
    scale_out = 0.5 * sigma / jnp.sqrt(variance)
    noise_code = jnp.log(sigma) / 4.0

    slot = lax.broadcasted_iota(jnp.int32, (8, 256), 0)
    for k in range(DEEP + ROWS + DEEP):
        sa, sb = sent_a[k].astype(F32), sent_b[k].astype(F32)
        ea, eb = edge_a[k].astype(F32), edge_b[k].astype(F32)
        own_left, own_right = jnp.where(lon_even, sb, sa), jnp.where(lon_even, sa, sb)
        left, right = jnp.where(lon_even, eb, ea), jnp.where(lon_even, ea, eb)
        strip = [
            pltpu.roll(jnp.where(slot > 2, left, own_left), 5, 0),
            pltpu.roll(jnp.where(slot < 5, right, own_right), 3, 0),
        ]
        x_c[k * STRIP : (k + 1) * STRIP, :] = jnp.concatenate(strip, 0).astype(BF16)
        r = k - (DEEP - THIN)
        if 0 <= r < THIN + ROWS + THIN:
            strip = [
                jnp.where(slot < 2, pltpu.roll(left, 7, 0), jnp.where(slot < 5, pltpu.roll(own_left, 5, 0), 0.0)),
                jnp.where(slot > 4, right, jnp.where(slot > 1, pltpu.roll(own_right, 2, 0), 0.0)),
            ]
            x_s[r * STRIP : (r + 1) * STRIP, :] = jnp.concatenate(strip, 0).astype(BF16)

    def put(ref, row, rows, value, above, below, lanes=slice(None)):
        over = min(max(above - row, 0), rows)
        under = min(max(row + rows - below, 0), rows)
        parts = [value[over * PITCH : (rows - under) * PITCH]]
        if over:
            parts.insert(0, value[: over * PITCH] * top)
        if under:
            parts.append(value[(rows - under) * PITCH :] * bottom)
        ref[row * PITCH : (row + rows) * PITCH, lanes] = jnp.concatenate(parts, 0).astype(ref.dtype)

    place = lax.broadcasted_iota(jnp.int32, (8, 128), 0)
    pooled[...] = pooled_in[...]
    mean = pool(x_c, w_in, 1, 32, STRIP)
    for row in range(16):
        v = mean[row] * top if row < 4 else mean[row] * bottom if row > 11 else mean[row]
        at = row * PITCH
        first = pooled_in[at : at + 8, :].astype(F32)
        pooled[at : at + 8, :] = jnp.where(place < 5, pltpu.roll(v[:8], 7, 0), first).astype(BF16)
        last = pooled_in[at + 64 : at + 72, :].astype(F32)
        pooled[at + 64 : at + 72, :] = jnp.where(place > 2, pltpu.roll(v[8:], 1, 0), last).astype(BF16)
    for row, rows in ((0, 8), (8, 6)):
        put(middle, row, rows, silu(half_conv(pooled, w_coarse, row + 1, rows)), 3, 11)
    embedded = scale[...] * noise_code + shift[...]
    for row, rows in ((0, 6), (6, 6)):
        d = silu(half_conv(middle, w_deeper, row + 1, rows)).astype(BF16)
        guide[row * PITCH : (row + rows) * PITCH, :] = matmul_nt(d, w_guide[...]) + embedded
    strips = pair_conv(x_s, w_noisy, 1, 22, True, STRIP)
    for row, rows in ((0, 12), (12, 10)):
        for half, strip in enumerate(strips):
            lanes = slice(128 * half, 128 * half + 128)
            parts = []
            for q in range(row, row + rows):
                at = q * PITCH
                left = pltpu.roll(strip[q * STRIP : q * STRIP + 8], 2, 0)
                first = jnp.where(place < 2, 0.0, jnp.where(place < 5, left, opening[at : at + 8, lanes]))
                right = pltpu.roll(strip[q * STRIP + 8 : q * STRIP + 16], 7, 0)
                last = jnp.where(place > 5, 0.0, jnp.where(place > 2, right, opening[at + 64 : at + 72, lanes]))
                g = (q + 1) // 2 * PITCH
                parts.append(jnp.concatenate([first, opening[at + 8 : at + 64, lanes], last], 0) + guide[g : g + PITCH, :])
            put(hidden, row, rows, silu(jnp.concatenate(parts, 0)), 3, 19, lanes)
    for row in (0, 10):
        for half, v in enumerate(pair_conv(hidden, w_block, 1 + row, 10)):
            put(inner, row, 10, silu(v), 2, 18, slice(128 * half, 128 * half + 128))
    for row, rows in ((0, 10), (10, 8)):
        h = hidden[(2 + row) * PITCH : (2 + row + rows) * PITCH, :].astype(F32)
        for half, v in enumerate(pair_conv(inner, w_branch, 1 + row, rows)):
            lanes = slice(128 * half, 128 * half + 128)
            put(mixed, row, rows, silu(v + h[:, lanes]), 1, 17, lanes)
    for first, rows in ((0, 6), (6, 6), (12, 4)):
        even, odd = pair_conv(mixed, w_out, 1 + first, rows)
        for q in range(rows):
            row = first + q
            at = slice(q * PITCH, (q + 1) * PITCH)
            turn[row, pl.ds(0, PITCH, stride=2), :] = even[at]
            turn[row, pl.ds(1, PITCH, stride=2), :] = odd[at]
            head = turn[row, 2 * EDGE : 2 * (EDGE + PAIRS), :].T[:CH]
            here = pl.ds(row, CH, stride=ROWS)
            out[here, :] = scale_skip * state[here, :] + scale_out * head


def net(n_lat, *args):
    vm = pl.BlockSpec(memory_space=VMEM)
    return pl.pallas_call(
        functools.partial(net_body, n_lat),
        out_shape=jax.ShapeDtypeStruct((CH * ROWS, 128), F32),
        in_specs=[pl.BlockSpec(memory_space=pltpu.SMEM)] + [vm] * (len(args) - 1),
        out_specs=vm,
        scratch_shapes=[
            VMEM((34 * STRIP, 256), BF16),
            VMEM((24 * STRIP, 256), BF16),
            VMEM((16 * PITCH, 128), BF16),
            VMEM((14 * PITCH, 256), BF16),
            VMEM((12 * PITCH, 128), F32),
            VMEM((22 * PITCH, 256), BF16),
            VMEM((20 * PITCH, 256), BF16),
            VMEM((18 * PITCH, 256), BF16),
            VMEM((ROWS, 2 * PITCH, 128), F32),
        ],
        compiler_params=pltpu.CompilerParams(vmem_limit_bytes=24 << 20),
        name="net",
    )(*args)


def on_device(
    mesh_shape,
    conditions,
    noisy_state,
    noise_level,
    kernel_input,
    kernel_coarse,
    kernel_deeper,
    guide_weight,
    time_scale,
    time_shift,
    kernel_noisy,
    kernel_block,
    kernel_branch,
    kernel_output,
):
    lon_even, lat_even = lax.axis_index("lon") % 2 == 0, lax.axis_index("lat") % 2 == 0
    cond = conditions.reshape(CH * ROWS, 128)
    state = noisy_state.reshape(CH * ROWS, 128)
    by_input = lambda kernel: kernel.transpose(0, 2, 1)
    in_hbm = lambda *values: [pltpu.with_memory_space_constraint(value, pltpu.HBM) for value in values]
    own_c, own_s, left, right, small_a, small_b, lat_a, lat_b, w_in, w_noisy = prep(
        noise_level, *in_hbm(cond, state, by_input(kernel_input), by_input(kernel_noisy))
    )
    permute = lambda value, a, o: lax.ppermute(value, AXES, swap_pairs(mesh_shape, a, o))
    small_b = permute(small_b, "B", None)
    small_a = permute(small_a, "A", None)
    lat_b = permute(lat_b, "B", None)
    lat_a = permute(lat_a, "A", None)
    above, below = jnp.where(lat_even, small_b, small_a), jnp.where(lat_even, small_a, small_b)
    left, right = (jnp.concatenate([above[n], edge, below[n]]) for n, edge in enumerate((left, right)))
    sent_a, sent_b = jnp.where(lon_even, right, left), jnp.where(lon_even, left, right)
    edge_b = permute(sent_b, None, "B")
    edge_a = permute(sent_a, None, "A")
    weights = in_hbm(kernel_coarse, kernel_deeper, guide_weight, kernel_block, kernel_branch, kernel_output)
    rest = inner(mesh_shape[1], own_c, own_s, lat_a, lat_b, w_in, w_noisy, *weights)
    out = net(
        mesh_shape[1], noise_level, sent_a, sent_b, edge_a, edge_b, state,
        time_scale[None], time_shift[None], w_in, w_noisy, *rest,
    )
    return out.reshape(noisy_state.shape)


def solution(mesh):
    tile = P(None, "lat", "lon")
    member = P(None, None, "lat", "lon")
    return jax.shard_map(
        functools.partial(on_device, (mesh.shape["lon"], mesh.shape["lat"])),
        mesh=mesh,
        in_specs=(tile, member) + (P(),) * 11,
        out_specs=member,
        check_vma=False,
    )
```

```python
import functools

import jax
import jax.numpy as jnp
from jax import lax
from jax.experimental import pallas as pl
from jax.experimental.pallas import tpu as pltpu
from jax.sharding import PartitionSpec as P

F32 = jnp.float32
BF16 = jnp.bfloat16
PITCH = 72
EDGE = 4
STRIP = 16
ROWS = 16
PAIRS = 64
CH = 80
DEEP = 9
THIN = 4
VMEM = pltpu.VMEM
AXES = ("lon", "lat")


def swap_pairs(mesh_shape, lat, lon):
    n_lon, n_lat = mesh_shape
    pairs = []
    for o in range(n_lon):
        for a in range(n_lat):
            b, p = a, o
            if lat:
                b = a ^ 1 if lat == "A" else a - 1 + 2 * (a % 2)
            if lon:
                p = (o ^ 1 if lon == "A" else o - 1 + 2 * (o % 2)) % n_lon
            if 0 <= b < n_lat:
                pairs.append((o * n_lat + a, p * n_lat + b))
    return pairs


def silu(v):
    h = v * 0.5
    return h + h * jnp.tanh(h)


def matmul_nt(x, w):
    return lax.dot_general(x, w, (((1,), (1,)), ((), ())), preferred_element_type=F32)


def prep_body(
    noise, cond_hbm, state_hbm, k_in, k_noisy, own_c, own_s, left, right, small_a, small_b, lat_a, lat_b, w_in, w_noisy,
    cond, state, work, arrived,
):
    copies = [
        pltpu.make_async_copy(cond_hbm, cond, arrived.at[0]),
        pltpu.make_async_copy(state_hbm, state, arrived.at[1]),
        pltpu.make_async_copy(k_in, w_in.at[:, :CH, :], arrived.at[2]),
        pltpu.make_async_copy(k_noisy, w_noisy.at[:, :CH, :], arrived.at[3]),
    ]
    for copy in copies:
        copy.start()
    lat_even = lax.axis_index("lat") % 2 == 0
    sigma = jnp.full((1, 128), noise[0], F32)
    scale_in = 1.0 / jnp.sqrt(sigma * sigma + 0.25)
    row = lax.broadcasted_iota(jnp.int32, (128, 128), 0)
    col = lax.broadcasted_iota(jnp.int32, (128, 128), 1)
    pick = (col == jnp.where(row < PAIRS, 2 * row, 2 * (row - PAIRS) + 1)).astype(BF16)
    blank = jnp.zeros((128 - CH, 128), BF16)
    slot = lax.broadcasted_iota(jnp.int32, (8, 128), 0)
    for w in (w_in, w_noisy):
        w[:, CH:, :] = jnp.zeros((9, 128 - CH, 128), BF16)
    for copy in copies[:2]:
        copy.wait()
    work[...] = cond[...].astype(F32)
    for i in range(ROWS):
        c_row = work[pl.ds(i, CH, stride=ROWS), :].astype(BF16)
        s_row = (scale_in * state[pl.ds(i, CH, stride=ROWS), :]).astype(BF16)
        both = matmul_nt(pick, jnp.concatenate([c_row, blank, s_row, blank], 0))
        c_pair = jnp.concatenate([both[:PAIRS, :128], both[PAIRS:, :128]], 1)
        s_pair = jnp.concatenate([both[:PAIRS, 128:], both[PAIRS:, 128:]], 1)
        own_c[i * PAIRS : (i + 1) * PAIRS, :] = c_pair.astype(BF16)
        own_s[i * PAIRS : (i + 1) * PAIRS, :] = s_pair.astype(BF16)
        for half in range(2):
            lanes = slice(128 * half, 128 * half + 128)
            left[i, :, lanes] = jnp.where(slot < 5, c_pair[:8, lanes], pltpu.roll(s_pair[:8, lanes], 5, 0)).astype(BF16)
            right[i, :, lanes] = jnp.where(slot > 2, c_pair[-8:, lanes], pltpu.roll(s_pair[-8:, lanes], 3, 0)).astype(BF16)
    for side, edge in enumerate((left, right)):
        first, last = edge[:DEEP].astype(F32), edge[ROWS - DEEP :].astype(F32)
        small_a[side] = jnp.where(lat_even, last, first).astype(BF16)
        small_b[side] = jnp.where(lat_even, first, last).astype(BF16)
    lane = lax.broadcasted_iota(jnp.int32, (PAIRS, 128), 1)
    free = 128 - CH
    for k in range(DEEP):
        for half in range(2):
            lanes = slice(128 * half, 128 * half + 128)
            rows = []
            for first, s_first in ((0, 0), (ROWS - DEEP, ROWS - THIN)):
                at = (first + k) * PAIRS
                value = own_c[at : at + PAIRS, lanes].astype(F32)
                n = 2 * k + half
                if n < 4 * THIN:
                    r, h = divmod(n // 2, 2)
                    at = (s_first + r) * PAIRS
                    part = own_s[at : at + PAIRS, 128 * h : 128 * h + 128].astype(F32)
                    part = pltpu.roll(part, (CH - free * (n % 2)) % 128, 1)
                    value = jnp.where(lane < CH, value, part)
                rows.append(value)
            lat_a[k, :, lanes] = jnp.where(lat_even, rows[1], rows[0]).astype(BF16)
            lat_b[k, :, lanes] = jnp.where(lat_even, rows[0], rows[1]).astype(BF16)
    for copy in copies[2:]:
        copy.wait()


def prep(noise, *args):
    vm = pl.BlockSpec(memory_space=VMEM)
    own = jax.ShapeDtypeStruct((ROWS * PAIRS, 256), BF16)
    edge = jax.ShapeDtypeStruct((ROWS, 8, 256), BF16)
    small = jax.ShapeDtypeStruct((2, DEEP, 8, 256), BF16)
    rows = jax.ShapeDtypeStruct((DEEP, PAIRS, 256), BF16)
    weights = jax.ShapeDtypeStruct((9, 128, 128), BF16)
    return pl.pallas_call(
        prep_body,
        out_shape=(own, own, edge, edge, small, small, rows, rows, weights, weights),
        in_specs=[pl.BlockSpec(memory_space=pltpu.SMEM)] + [pl.BlockSpec(memory_space=pltpu.HBM)] * 4,
        out_specs=[vm] * 10,
        scratch_shapes=[
            VMEM((CH * ROWS, 128), BF16),
            VMEM((CH * ROWS, 128), F32),
            VMEM((CH * ROWS, 128), F32),
            pltpu.SemaphoreType.DMA((4,)),
        ],
        compiler_params=pltpu.CompilerParams(vmem_limit_bytes=12 << 20),
        name="prep",
    )(noise, *args)


def pair_weights(w, di):
    k0, k1, k2 = w[3 * di], w[3 * di + 1], w[3 * di + 2]
    z = jnp.zeros_like(k0)
    c = jnp.concatenate
    return c([c([k1, k2], 1), c([k0, k1], 1), c([z, k0], 1), c([k2, z], 1)], 0)


def pair_weights_by_input(w, di):
    k0, k1, k2 = w[3 * di], w[3 * di + 1], w[3 * di + 2]
    z = jnp.zeros_like(k0)
    c = jnp.concatenate
    return c([c([k1, k0, z, k2], 1), c([k2, k1, k0, z], 1)], 0)


def pair_conv(x, w, centre, rows, by_input=False, pitch=PITCH):
    span = rows * pitch
    taps = [x[(centre + d - 1) * pitch : (centre + d - 1) * pitch + span, :] for d in range(3)]
    taps = jnp.concatenate(taps, 1)
    if by_input:
        weights = jnp.concatenate([pair_weights_by_input(w, d) for d in range(3)], 0)
        y = jnp.dot(taps, weights, preferred_element_type=F32)
    else:
        y = matmul_nt(taps, jnp.concatenate([pair_weights(w, d) for d in range(3)], 1))
    even = y[:, 0:128] + pltpu.roll(y[:, 256:384], 1, 0)
    odd = y[:, 128:256] + pltpu.roll(y[:, 384:512], span - 1, 0)
    return even, odd


def half_conv(x, w, centre, rows):
    span = rows * PITCH
    c = jnp.concatenate
    taps = c([x[(centre + d - 1) * PITCH : (centre + d - 1) * PITCH + span, :] for d in range(3)], 1)
    weights = c([c([w[3 * d + b] for d in range(3)], 1) for b in range(3)], 0)
    y = matmul_nt(taps, weights)
    n = y.shape[1] // 3
    return y[:, n : 2 * n] + pltpu.roll(y[:, :n], 1, 0) + pltpu.roll(y[:, 2 * n :], span - 1, 0)


def pool(x, w, centre, rows, pitch):
    even, odd = pair_conv(x, w, centre, rows, True, pitch)
    both = silu(even).astype(BF16).astype(F32) + silu(odd).astype(BF16).astype(F32)
    both = both.reshape(rows // 2, 2, pitch, 128)
    return (both[:, 0] + both[:, 1]) * 0.25


def band(n_lat):
    lat = lax.axis_index("lat")
    return (lat > 0).astype(F32), (lat < n_lat - 1).astype(F32)


def early():
    return lax.axis_index("lon") % 8 < 2


def own_body(ahead, own_c, own_s, w_in, w_noisy, pooled, opening):
    @pl.when(early() if ahead else jnp.logical_not(early()))
    def _():
        mean = pool(own_c, w_in, 2, 12, PAIRS)
        for q in range(6):
            pooled[q * PITCH + EDGE : q * PITCH + EDGE + PAIRS, :] = mean[q].astype(BF16)
        for row, rows in ((0, 6), (6, 8)):
            for half, v in enumerate(pair_conv(own_s, w_noisy, 1 + row, rows, True, PAIRS)):
                for q in range(rows):
                    at = (row + q) * PITCH + EDGE
                    opening[at : at + PAIRS, 128 * half : 128 * half + 128] = v[q * PAIRS : (q + 1) * PAIRS]


def own_rows(ahead, *args):
    vm = pl.BlockSpec(memory_space=VMEM)
    return pl.pallas_call(
        functools.partial(own_body, ahead),
        out_shape=(jax.ShapeDtypeStruct((6 * PITCH, 128), BF16), jax.ShapeDtypeStruct((14 * PITCH, 256), F32)),
        in_specs=[vm] * len(args),
        out_specs=[vm] * 2,
        compiler_params=pltpu.CompilerParams(vmem_limit_bytes=6 << 20),
        cost_estimate=pl.CostEstimate(flops=2 * 10**9, bytes_accessed=3 * 10**6, transcendentals=5 * 10**5),
        name="own_rows",
    )(*args)


def inner_body(
    n_lat,
    own_c, own_s, lat_a, lat_b, w_in, w_noisy, pool_1, open_1, pool_2, open_2,
    k_coarse, k_deeper, k_guide, k_block, k_branch, k_out,
    w_coarse, w_deeper, w_guide, w_block, w_branch, w_out, pooled, opening,
    x_c, x_s, arrived,
):
    moves = [
        (k_coarse, w_coarse), (k_deeper, w_deeper), (k_guide, w_guide),
        (k_block, w_block), (k_branch, w_branch), (k_out, w_out.at[:, :CH, :]),
    ]
    copies = [pltpu.make_async_copy(src, dst, arrived.at[n]) for n, (src, dst) in enumerate(moves)]
    for copy in copies:
        copy.start()
    w_out[:, CH:, :] = jnp.zeros((9, 128 - CH, 128), BF16)
    top, bottom = band(n_lat)
    lat_even = lax.axis_index("lat") % 2 == 0
    free = 128 - CH
    lane = lax.broadcasted_iota(jnp.int32, (1, 128), 1)
    for x, own, n, deep in ((x_c, own_c, 3, DEEP), (x_s, own_s, 2, THIN)):
        x[deep * PAIRS : (deep + n) * PAIRS, :] = own[: n * PAIRS, :]
        x[(deep + n) * PAIRS : (deep + 2 * n) * PAIRS, :] = own[(ROWS - n) * PAIRS :, :]
    for below in range(2):

        def received(k, lanes):
            a, b = lat_a[k, :, lanes].astype(F32), lat_b[k, :, lanes].astype(F32)
            return jnp.where(lat_even, a, b) if below else jnp.where(lat_even, b, a)

        for k in range(DEEP):
            at = (DEEP + 6 + k if below else k) * PAIRS
            x_c[at : at + PAIRS, :] = received(k, slice(None)).astype(BF16)
        for r in range(THIN):
            at = (THIN + 4 + r if below else r) * PAIRS
            for h in range(2):
                n = 2 * (2 * r + h)
                parts = [
                    pltpu.roll(received(m // 2, slice(128 * (m % 2), 128 * (m % 2) + 128)), (128 - CH + free * (m % 2)) % 128, 1)
                    for m in (n, n + 1)
                ]
                x_s[at : at + PAIRS, 128 * h : 128 * h + 128] = jnp.where(lane < free, *parts).astype(BF16)
    for row, centre in ((0, 1), (11, 13)):
        mean = pool(x_c, w_in, centre, 10, PAIRS)
        for q in range(5):
            v = mean[q]
            if row + q < 4:
                v = v * top
            if row + q >= 12:
                v = v * bottom
            at = (row + q) * PITCH + EDGE
            pooled[at : at + PAIRS, :] = v.astype(BF16)
    for row, centre in ((0, 1), (18, 7)):
        for half, v in enumerate(pair_conv(x_s, w_noisy, centre, 4, True, PAIRS)):
            for q in range(4):
                at = (row + q) * PITCH + EDGE
                opening[at : at + PAIRS, 128 * half : 128 * half + 128] = v[q * PAIRS : (q + 1) * PAIRS]
    first = early()
    pooled[5 * PITCH : 11 * PITCH, :] = jnp.where(first, pool_1[...].astype(F32), pool_2[...].astype(F32)).astype(BF16)
    opening[4 * PITCH : 18 * PITCH, :] = jnp.where(first, open_1[...], open_2[...])
    for copy in copies:
        copy.wait()


def inner(n_lat, *args):
    vm = pl.BlockSpec(memory_space=VMEM)
    wide = lambda n, k: jax.ShapeDtypeStruct((9, n, k), BF16)
    out_shape = (
        wide(256, 128), wide(256, 256), jax.ShapeDtypeStruct((128, 256), BF16),
        wide(128, 128), wide(128, 128), wide(128, 128),
        jax.ShapeDtypeStruct((16 * PITCH, 128), BF16), jax.ShapeDtypeStruct((22 * PITCH, 256), F32),
    )
    return pl.pallas_call(
        functools.partial(inner_body, n_lat),
        out_shape=out_shape,
        in_specs=[vm] * 10 + [pl.BlockSpec(memory_space=pltpu.HBM)] * 6,
        out_specs=[vm] * len(out_shape),
        scratch_shapes=[
            VMEM((24 * PAIRS, 256), BF16),
            VMEM((12 * PAIRS, 256), BF16),
            pltpu.SemaphoreType.DMA((6,)),
        ],
        compiler_params=pltpu.CompilerParams(vmem_limit_bytes=10 << 20),
        cost_estimate=pl.CostEstimate(flops=3 * 10**9, bytes_accessed=6 * 10**6, transcendentals=10**6),
        name="inner",
    )(*args)


def net_body(
    n_lat,
    noise, sent_a, sent_b, edge_a, edge_b, state, scale, shift,
    w_in, w_noisy, w_coarse, w_deeper, w_guide, w_block, w_branch, w_out, pooled_in, opening,
    out, x_c, x_s, pooled, middle, guide, hidden, inner, mixed, turn,
):
    top, bottom = band(n_lat)
    lon_even = lax.axis_index("lon") % 2 == 0
    sigma = jnp.full((1, 128), noise[0], F32)
    variance = sigma * sigma + 0.25
    scale_skip = 0.25 / variance
    scale_out = 0.5 * sigma / jnp.sqrt(variance)
    noise_code = jnp.log(sigma) / 4.0

    slot = lax.broadcasted_iota(jnp.int32, (8, 256), 0)
    for k in range(DEEP + ROWS + DEEP):
        sa, sb = sent_a[k].astype(F32), sent_b[k].astype(F32)
        ea, eb = edge_a[k].astype(F32), edge_b[k].astype(F32)
        own_left, own_right = jnp.where(lon_even, sb, sa), jnp.where(lon_even, sa, sb)
        left, right = jnp.where(lon_even, eb, ea), jnp.where(lon_even, ea, eb)
        strip = [
            pltpu.roll(jnp.where(slot > 2, left, own_left), 5, 0),
            pltpu.roll(jnp.where(slot < 5, right, own_right), 3, 0),
        ]
        x_c[k * STRIP : (k + 1) * STRIP, :] = jnp.concatenate(strip, 0).astype(BF16)
        r = k - (DEEP - THIN)
        if 0 <= r < THIN + ROWS + THIN:
            strip = [
                jnp.where(slot < 2, pltpu.roll(left, 7, 0), jnp.where(slot < 5, pltpu.roll(own_left, 5, 0), 0.0)),
                jnp.where(slot > 4, right, jnp.where(slot > 1, pltpu.roll(own_right, 2, 0), 0.0)),
            ]
            x_s[r * STRIP : (r + 1) * STRIP, :] = jnp.concatenate(strip, 0).astype(BF16)

    def put(ref, row, rows, value, above, below, lanes=slice(None)):
        over = min(max(above - row, 0), rows)
        under = min(max(row + rows - below, 0), rows)
        parts = [value[over * PITCH : (rows - under) * PITCH]]
        if over:
            parts.insert(0, value[: over * PITCH] * top)
        if under:
            parts.append(value[(rows - under) * PITCH :] * bottom)
        ref[row * PITCH : (row + rows) * PITCH, lanes] = jnp.concatenate(parts, 0).astype(ref.dtype)

    place = lax.broadcasted_iota(jnp.int32, (8, 128), 0)
    pooled[...] = pooled_in[...]
    mean = pool(x_c, w_in, 1, 32, STRIP)
    for row in range(16):
        v = mean[row] * top if row < 4 else mean[row] * bottom if row > 11 else mean[row]
        at = row * PITCH
        first = pooled_in[at : at + 8, :].astype(F32)
        pooled[at : at + 8, :] = jnp.where(place < 5, pltpu.roll(v[:8], 7, 0), first).astype(BF16)
        last = pooled_in[at + 64 : at + 72, :].astype(F32)
        pooled[at + 64 : at + 72, :] = jnp.where(place > 2, pltpu.roll(v[8:], 1, 0), last).astype(BF16)
    for row, rows in ((0, 14),):
        put(middle, row, rows, silu(half_conv(pooled, w_coarse, row + 1, rows)), 3, 11)
    embedded = scale[...] * noise_code + shift[...]
    for row, rows in ((0, 6), (6, 6)):
        d = silu(half_conv(middle, w_deeper, row + 1, rows)).astype(BF16)
        guide[row * PITCH : (row + rows) * PITCH, :] = matmul_nt(d, w_guide[...]) + embedded
    strips = pair_conv(x_s, w_noisy, 1, 22, True, STRIP)
    for row, rows in ((0, 12), (12, 10)):
        for half, strip in enumerate(strips):
            lanes = slice(128 * half, 128 * half + 128)
            parts = []
            for q in range(row, row + rows):
                at = q * PITCH
                left = pltpu.roll(strip[q * STRIP : q * STRIP + 8], 2, 0)
                first = jnp.where(place < 2, 0.0, jnp.where(place < 5, left, opening[at : at + 8, lanes]))
                right = pltpu.roll(strip[q * STRIP + 8 : q * STRIP + 16], 7, 0)
                last = jnp.where(place > 5, 0.0, jnp.where(place > 2, right, opening[at + 64 : at + 72, lanes]))
                g = (q + 1) // 2 * PITCH
                parts.append(jnp.concatenate([first, opening[at + 8 : at + 64, lanes], last], 0) + guide[g : g + PITCH, :])
            put(hidden, row, rows, silu(jnp.concatenate(parts, 0)), 3, 19, lanes)
    for row in (0, 10):
        for half, v in enumerate(pair_conv(hidden, w_block, 1 + row, 10)):
            put(inner, row, 10, silu(v), 2, 18, slice(128 * half, 128 * half + 128))
    for row, rows in ((0, 10), (10, 8)):
        h = hidden[(2 + row) * PITCH : (2 + row + rows) * PITCH, :].astype(F32)
        for half, v in enumerate(pair_conv(inner, w_branch, 1 + row, rows)):
            lanes = slice(128 * half, 128 * half + 128)
            put(mixed, row, rows, silu(v + h[:, lanes]), 1, 17, lanes)
    for first, rows in ((0, 6), (6, 6), (12, 4)):
        even, odd = pair_conv(mixed, w_out, 1 + first, rows)
        for q in range(rows):
            row = first + q
            at = slice(q * PITCH, (q + 1) * PITCH)
            turn[row, pl.ds(0, PITCH, stride=2), :] = even[at]
            turn[row, pl.ds(1, PITCH, stride=2), :] = odd[at]
            head = turn[row, 2 * EDGE : 2 * (EDGE + PAIRS), :].T[:CH]
            here = pl.ds(row, CH, stride=ROWS)
            out[here, :] = scale_skip * state[here, :] + scale_out * head


def net(n_lat, *args):
    vm = pl.BlockSpec(memory_space=VMEM)
    return pl.pallas_call(
        functools.partial(net_body, n_lat),
        out_shape=jax.ShapeDtypeStruct((CH * ROWS, 128), F32),
        in_specs=[pl.BlockSpec(memory_space=pltpu.SMEM)] + [vm] * (len(args) - 1),
        out_specs=vm,
        scratch_shapes=[
            VMEM((34 * STRIP, 256), BF16),
            VMEM((24 * STRIP, 256), BF16),
            VMEM((16 * PITCH, 128), BF16),
            VMEM((14 * PITCH, 256), BF16),
            VMEM((12 * PITCH, 128), F32),
            VMEM((22 * PITCH, 256), BF16),
            VMEM((20 * PITCH, 256), BF16),
            VMEM((18 * PITCH, 256), BF16),
            VMEM((ROWS, 2 * PITCH, 128), F32),
        ],
        compiler_params=pltpu.CompilerParams(vmem_limit_bytes=14 << 20),
        name="net",
    )(*args)


def on_device(
    mesh_shape,
    conditions,
    noisy_state,
    noise_level,
    kernel_input,
    kernel_coarse,
    kernel_deeper,
    guide_weight,
    time_scale,
    time_shift,
    kernel_noisy,
    kernel_block,
    kernel_branch,
    kernel_output,
):
    lon_even, lat_even = lax.axis_index("lon") % 2 == 0, lax.axis_index("lat") % 2 == 0
    cond = conditions.reshape(CH * ROWS, 128)
    state = noisy_state.reshape(CH * ROWS, 128)
    by_input = lambda kernel: kernel.transpose(0, 2, 1)
    in_hbm = lambda *values: [pltpu.with_memory_space_constraint(value, pltpu.HBM) for value in values]
    own_c, own_s, left, right, small_a, small_b, lat_a, lat_b, w_in, w_noisy = prep(
        noise_level, *in_hbm(cond, state, by_input(kernel_input), by_input(kernel_noisy))
    )
    permute = lambda value, a, o: lax.ppermute(value, AXES, swap_pairs(mesh_shape, a, o))
    small_b = permute(small_b, "B", None)
    small_a = permute(small_a, "A", None)
    lat_b = permute(lat_b, "B", None)
    lat_a = permute(lat_a, "A", None)
    above, below = jnp.where(lat_even, small_b, small_a), jnp.where(lat_even, small_a, small_b)
    left, right = (jnp.concatenate([above[n], edge, below[n]]) for n, edge in enumerate((left, right)))
    sent_a, sent_b = jnp.where(lon_even, right, left), jnp.where(lon_even, left, right)
    ahead = own_rows(True, own_c, own_s, w_in, w_noisy)
    sent_a, sent_b, ahead, now_c, now_s = lax.optimization_barrier((sent_a, sent_b, ahead, own_c, own_s))
    near = swap_pairs(mesh_shape, None, "A")
    seam = lambda index: index // mesh_shape[1] % 8 < 2
    edge_s = lax.ppermute(sent_a, AXES, [(i, j if seam(i) else i) for i, j in near])
    edge_b = permute(sent_b, None, "B")
    sent_late, edge_s = lax.optimization_barrier((sent_a, edge_s))
    edge_a = lax.ppermute(sent_late, AXES, [(i, i if seam(i) else j) for i, j in near])
    during = own_rows(False, now_c, now_s, w_in, w_noisy)
    weights = in_hbm(kernel_coarse, kernel_deeper, guide_weight, kernel_block, kernel_branch, kernel_output)
    rest = inner(mesh_shape[1], own_c, own_s, lat_a, lat_b, w_in, w_noisy, *ahead, *during, *weights)
    edge_a = jnp.where(lax.axis_index("lon") % 8 < 2, edge_s, edge_a)
    out = net(
        mesh_shape[1], noise_level, sent_a, sent_b, edge_a, edge_b, state,
        time_scale[None], time_shift[None], w_in, w_noisy, *rest,
    )
    return out.reshape(noisy_state.shape)


def solution(mesh):
    tile = P(None, "lat", "lon")
    member = P(None, None, "lat", "lon")
    return jax.shard_map(
        functools.partial(on_device, (mesh.shape["lon"], mesh.shape["lat"])),
        mesh=mesh,
        in_specs=(tile, member) + (P(),) * 11,
        out_specs=member,
        check_vma=False,
    )
```

```python
import functools

import jax
import jax.numpy as jnp
from jax import lax
from jax.experimental import pallas as pl
from jax.experimental.pallas import tpu as pltpu
from jax.sharding import PartitionSpec as P

F32 = jnp.float32
BF16 = jnp.bfloat16
PITCH = 72
EDGE = 4
STRIP = 16
ROWS = 16
PAIRS = 64
CH = 80
DEEP = 9
THIN = 4
VMEM = pltpu.VMEM
AXES = ("lon", "lat")


def swap_pairs(mesh_shape, lat, lon):
    n_lon, n_lat = mesh_shape
    pairs = []
    for o in range(n_lon):
        for a in range(n_lat):
            b, p = a, o
            if lat:
                b = a ^ 1 if lat == "A" else a - 1 + 2 * (a % 2)
            if lon:
                p = (o ^ 1 if lon == "A" else o - 1 + 2 * (o % 2)) % n_lon
            if 0 <= b < n_lat:
                pairs.append((o * n_lat + a, p * n_lat + b))
    return pairs


def silu(v):
    h = v * 0.5
    return h + h * jnp.tanh(h)


def matmul_nt(x, w):
    return lax.dot_general(x, w, (((1,), (1,)), ((), ())), preferred_element_type=F32)


def prep_body(
    noise, cond_hbm, state_hbm, k_in, k_noisy, own_c, own_s, left, right, small_a, small_b, lat_a, lat_b, w_in, w_noisy,
    cond, state, work, arrived,
):
    copies = [
        pltpu.make_async_copy(cond_hbm, cond, arrived.at[0]),
        pltpu.make_async_copy(state_hbm, state, arrived.at[1]),
        pltpu.make_async_copy(k_in, w_in.at[:, :CH, :], arrived.at[2]),
        pltpu.make_async_copy(k_noisy, w_noisy.at[:, :CH, :], arrived.at[3]),
    ]
    for copy in copies:
        copy.start()
    lat_even = lax.axis_index("lat") % 2 == 0
    sigma = jnp.full((1, 128), noise[0], F32)
    scale_in = 1.0 / jnp.sqrt(sigma * sigma + 0.25)
    row = lax.broadcasted_iota(jnp.int32, (128, 128), 0)
    col = lax.broadcasted_iota(jnp.int32, (128, 128), 1)
    pick = (col == jnp.where(row < PAIRS, 2 * row, 2 * (row - PAIRS) + 1)).astype(BF16)
    blank = jnp.zeros((128 - CH, 128), BF16)
    slot = lax.broadcasted_iota(jnp.int32, (8, 128), 0)
    for w in (w_in, w_noisy):
        w[:, CH:, :] = jnp.zeros((9, 128 - CH, 128), BF16)
    for copy in copies[:2]:
        copy.wait()
    work[...] = cond[...].astype(F32)
    for i in range(ROWS):
        c_row = work[pl.ds(i, CH, stride=ROWS), :].astype(BF16)
        s_row = (scale_in * state[pl.ds(i, CH, stride=ROWS), :]).astype(BF16)
        both = matmul_nt(pick, jnp.concatenate([c_row, blank, s_row, blank], 0))
        c_pair = jnp.concatenate([both[:PAIRS, :128], both[PAIRS:, :128]], 1)
        s_pair = jnp.concatenate([both[:PAIRS, 128:], both[PAIRS:, 128:]], 1)
        own_c[i * PAIRS : (i + 1) * PAIRS, :] = c_pair.astype(BF16)
        own_s[i * PAIRS : (i + 1) * PAIRS, :] = s_pair.astype(BF16)
        for half in range(2):
            lanes = slice(128 * half, 128 * half + 128)
            left[i, :, lanes] = jnp.where(slot < 5, c_pair[:8, lanes], pltpu.roll(s_pair[:8, lanes], 5, 0)).astype(BF16)
            right[i, :, lanes] = jnp.where(slot > 2, c_pair[-8:, lanes], pltpu.roll(s_pair[-8:, lanes], 3, 0)).astype(BF16)
    for side, edge in enumerate((left, right)):
        first, last = edge[:DEEP].astype(F32), edge[ROWS - DEEP :].astype(F32)
        small_a[side] = jnp.where(lat_even, last, first).astype(BF16)
        small_b[side] = jnp.where(lat_even, first, last).astype(BF16)
    lane = lax.broadcasted_iota(jnp.int32, (PAIRS, 128), 1)
    free = 128 - CH
    for k in range(DEEP):
        for half in range(2):
            lanes = slice(128 * half, 128 * half + 128)
            rows = []
            for first, s_first in ((0, 0), (ROWS - DEEP, ROWS - THIN)):
                at = (first + k) * PAIRS
                value = own_c[at : at + PAIRS, lanes].astype(F32)
                n = 2 * k + half
                if n < 4 * THIN:
                    r, h = divmod(n // 2, 2)
                    at = (s_first + r) * PAIRS
                    part = own_s[at : at + PAIRS, 128 * h : 128 * h + 128].astype(F32)
                    part = pltpu.roll(part, (CH - free * (n % 2)) % 128, 1)
                    value = jnp.where(lane < CH, value, part)
                rows.append(value)
            lat_a[k, :, lanes] = jnp.where(lat_even, rows[1], rows[0]).astype(BF16)
            lat_b[k, :, lanes] = jnp.where(lat_even, rows[0], rows[1]).astype(BF16)
    for copy in copies[2:]:
        copy.wait()


def prep(noise, *args):
    vm = pl.BlockSpec(memory_space=VMEM)
    own = jax.ShapeDtypeStruct((ROWS * PAIRS, 256), BF16)
    edge = jax.ShapeDtypeStruct((ROWS, 8, 256), BF16)
    small = jax.ShapeDtypeStruct((2, DEEP, 8, 256), BF16)
    rows = jax.ShapeDtypeStruct((DEEP, PAIRS, 256), BF16)
    weights = jax.ShapeDtypeStruct((9, 128, 128), BF16)
    return pl.pallas_call(
        prep_body,
        out_shape=(own, own, edge, edge, small, small, rows, rows, weights, weights),
        in_specs=[pl.BlockSpec(memory_space=pltpu.SMEM)] + [pl.BlockSpec(memory_space=pltpu.HBM)] * 4,
        out_specs=[vm] * 10,
        scratch_shapes=[
            VMEM((CH * ROWS, 128), BF16),
            VMEM((CH * ROWS, 128), F32),
            VMEM((CH * ROWS, 128), F32),
            pltpu.SemaphoreType.DMA((4,)),
        ],
        compiler_params=pltpu.CompilerParams(vmem_limit_bytes=12 << 20),
        name="prep",
    )(noise, *args)


def pair_weights(w, di):
    k0, k1, k2 = w[3 * di], w[3 * di + 1], w[3 * di + 2]
    z = jnp.zeros_like(k0)
    c = jnp.concatenate
    return c([c([k1, k2], 1), c([k0, k1], 1), c([z, k0], 1), c([k2, z], 1)], 0)


def pair_weights_by_input(w, di):
    k0, k1, k2 = w[3 * di], w[3 * di + 1], w[3 * di + 2]
    z = jnp.zeros_like(k0)
    c = jnp.concatenate
    return c([c([k1, k0, z, k2], 1), c([k2, k1, k0, z], 1)], 0)


def pair_conv(x, w, centre, rows, by_input=False, pitch=PITCH):
    span = rows * pitch
    taps = [x[(centre + d - 1) * pitch : (centre + d - 1) * pitch + span, :] for d in range(3)]
    taps = jnp.concatenate(taps, 1)
    if by_input:
        weights = jnp.concatenate([pair_weights_by_input(w, d) for d in range(3)], 0)
        y = jnp.dot(taps, weights, preferred_element_type=F32)
    else:
        y = matmul_nt(taps, jnp.concatenate([pair_weights(w, d) for d in range(3)], 1))
    even = y[:, 0:128] + pltpu.roll(y[:, 256:384], 1, 0)
    odd = y[:, 128:256] + pltpu.roll(y[:, 384:512], span - 1, 0)
    return even, odd


def half_conv(x, w, centre, rows):
    span = rows * PITCH
    c = jnp.concatenate
    taps = c([x[(centre + d - 1) * PITCH : (centre + d - 1) * PITCH + span, :] for d in range(3)], 1)
    weights = c([c([w[3 * d + b] for d in range(3)], 1) for b in range(3)], 0)
    y = matmul_nt(taps, weights)
    n = y.shape[1] // 3
    return y[:, n : 2 * n] + pltpu.roll(y[:, :n], 1, 0) + pltpu.roll(y[:, 2 * n :], span - 1, 0)


def pool(x, w, centre, rows, pitch):
    even, odd = pair_conv(x, w, centre, rows, True, pitch)
    both = silu(even).astype(BF16).astype(F32) + silu(odd).astype(BF16).astype(F32)
    both = both.reshape(rows // 2, 2, pitch, 128)
    return (both[:, 0] + both[:, 1]) * 0.25


def band(n_lat):
    lat = lax.axis_index("lat")
    return (lat > 0).astype(F32), (lat < n_lat - 1).astype(F32)


def own_body(own_c, own_s, w_in, w_noisy, pooled, opening):
    mean = pool(own_c, w_in, 2, 12, PAIRS)
    for q in range(6):
        pooled[q * PITCH + EDGE : q * PITCH + EDGE + PAIRS, :] = mean[q].astype(BF16)
    for row, rows in ((0, 6), (6, 8)):
        for half, v in enumerate(pair_conv(own_s, w_noisy, 1 + row, rows, True, PAIRS)):
            for q in range(rows):
                at = (row + q) * PITCH + EDGE
                opening[at : at + PAIRS, 128 * half : 128 * half + 128] = v[q * PAIRS : (q + 1) * PAIRS]


def own_rows(*args):
    vm = pl.BlockSpec(memory_space=VMEM)
    return pl.pallas_call(
        own_body,
        out_shape=(jax.ShapeDtypeStruct((6 * PITCH, 128), BF16), jax.ShapeDtypeStruct((14 * PITCH, 256), F32)),
        in_specs=[vm] * len(args),
        out_specs=[vm] * 2,
        compiler_params=pltpu.CompilerParams(vmem_limit_bytes=12 << 20),
        cost_estimate=pl.CostEstimate(flops=2 * 10**9, bytes_accessed=3 * 10**6, transcendentals=5 * 10**5),
        name="own_rows",
    )(*args)


def inner_body(
    n_lat,
    own_c, own_s, lat_b, lat_a, w_in, w_noisy, pool_own, open_own,
    k_coarse, k_deeper, k_guide, k_block, k_branch, k_out,
    w_coarse, w_deeper, w_guide, w_block, w_branch, w_out, pooled, opening,
    x_c, x_s, arrived,
):
    moves = [
        (k_coarse, w_coarse), (k_deeper, w_deeper), (k_guide, w_guide),
        (k_block, w_block), (k_branch, w_branch), (k_out, w_out.at[:, :CH, :]),
    ]
    copies = [pltpu.make_async_copy(src, dst, arrived.at[n]) for n, (src, dst) in enumerate(moves)]
    for copy in copies:
        copy.start()
    w_out[:, CH:, :] = jnp.zeros((9, 128 - CH, 128), BF16)
    top, bottom = band(n_lat)
    lat_even = lax.axis_index("lat") % 2 == 0
    free = 128 - CH
    lane = lax.broadcasted_iota(jnp.int32, (1, 128), 1)
    for x, own, n, deep in ((x_c, own_c, 3, DEEP), (x_s, own_s, 2, THIN)):
        x[deep * PAIRS : (deep + n) * PAIRS, :] = own[: n * PAIRS, :]
        x[(deep + n) * PAIRS : (deep + 2 * n) * PAIRS, :] = own[(ROWS - n) * PAIRS :, :]
    for below in range(2):

        def received(k, lanes):
            a, b = lat_a[k, :, lanes].astype(F32), lat_b[k, :, lanes].astype(F32)
            return jnp.where(lat_even, a, b) if below else jnp.where(lat_even, b, a)

        for k in range(DEEP):
            at = (DEEP + 6 + k if below else k) * PAIRS
            x_c[at : at + PAIRS, :] = received(k, slice(None)).astype(BF16)
        for r in range(THIN):
            at = (THIN + 4 + r if below else r) * PAIRS
            for h in range(2):
                n = 2 * (2 * r + h)
                parts = [
                    pltpu.roll(received(m // 2, slice(128 * (m % 2), 128 * (m % 2) + 128)), (128 - CH + free * (m % 2)) % 128, 1)
                    for m in (n, n + 1)
                ]
                x_s[at : at + PAIRS, 128 * h : 128 * h + 128] = jnp.where(lane < free, *parts).astype(BF16)
    for row, centre in ((0, 1), (11, 13)):
        mean = pool(x_c, w_in, centre, 10, PAIRS)
        for q in range(5):
            v = mean[q]
            if row + q < 4:
                v = v * top
            if row + q >= 12:
                v = v * bottom
            at = (row + q) * PITCH + EDGE
            pooled[at : at + PAIRS, :] = v.astype(BF16)
    for row, centre in ((0, 1), (18, 7)):
        for half, v in enumerate(pair_conv(x_s, w_noisy, centre, 4, True, PAIRS)):
            for q in range(4):
                at = (row + q) * PITCH + EDGE
                opening[at : at + PAIRS, 128 * half : 128 * half + 128] = v[q * PAIRS : (q + 1) * PAIRS]
    pooled[5 * PITCH : 11 * PITCH, :] = pool_own[...]
    opening[4 * PITCH : 18 * PITCH, :] = open_own[...]
    for copy in copies:
        copy.wait()


def inner(n_lat, *args):
    vm = pl.BlockSpec(memory_space=VMEM)
    wide = lambda n, k: jax.ShapeDtypeStruct((9, n, k), BF16)
    out_shape = (
        wide(256, 128), wide(256, 256), jax.ShapeDtypeStruct((128, 256), BF16),
        wide(128, 128), wide(128, 128), wide(128, 128),
        jax.ShapeDtypeStruct((16 * PITCH, 128), BF16), jax.ShapeDtypeStruct((22 * PITCH, 256), F32),
    )
    return pl.pallas_call(
        functools.partial(inner_body, n_lat),
        out_shape=out_shape,
        in_specs=[vm] * 8 + [pl.BlockSpec(memory_space=pltpu.HBM)] * 6,
        out_specs=[vm] * len(out_shape),
        scratch_shapes=[
            VMEM((24 * PAIRS, 256), BF16),
            VMEM((12 * PAIRS, 256), BF16),
            pltpu.SemaphoreType.DMA((6,)),
        ],
        compiler_params=pltpu.CompilerParams(vmem_limit_bytes=20 << 20),
        cost_estimate=pl.CostEstimate(flops=3 * 10**9, bytes_accessed=6 * 10**6, transcendentals=10**6),
        name="inner",
    )(*args)


def net_body(
    n_lat,
    noise, sent_b, sent_a, edge_b, edge_a, state, scale, shift,
    w_in, w_noisy, w_coarse, w_deeper, w_guide, w_block, w_branch, w_out, pooled_in, opening,
    out, x_c, x_s, pooled, middle, guide, hidden, inner, mixed, turn,
):
    top, bottom = band(n_lat)
    lon_even = lax.axis_index("lon") % 2 == 0
    sigma = jnp.full((1, 128), noise[0], F32)
    variance = sigma * sigma + 0.25
    scale_skip = 0.25 / variance
    scale_out = 0.5 * sigma / jnp.sqrt(variance)
    noise_code = jnp.log(sigma) / 4.0

    slot = lax.broadcasted_iota(jnp.int32, (8, 256), 0)
    for k in range(DEEP + ROWS + DEEP):
        sa, sb = sent_a[k].astype(F32), sent_b[k].astype(F32)
        ea, eb = edge_a[k].astype(F32), edge_b[k].astype(F32)
        own_left, own_right = jnp.where(lon_even, sb, sa), jnp.where(lon_even, sa, sb)
        left, right = jnp.where(lon_even, eb, ea), jnp.where(lon_even, ea, eb)
        strip = [
            pltpu.roll(jnp.where(slot > 2, left, own_left), 5, 0),
            pltpu.roll(jnp.where(slot < 5, right, own_right), 3, 0),
        ]
        x_c[k * STRIP : (k + 1) * STRIP, :] = jnp.concatenate(strip, 0).astype(BF16)
        r = k - (DEEP - THIN)
        if 0 <= r < THIN + ROWS + THIN:
            strip = [
                jnp.where(slot < 2, pltpu.roll(left, 7, 0), jnp.where(slot < 5, pltpu.roll(own_left, 5, 0), 0.0)),
                jnp.where(slot > 4, right, jnp.where(slot > 1, pltpu.roll(own_right, 2, 0), 0.0)),
            ]
            x_s[r * STRIP : (r + 1) * STRIP, :] = jnp.concatenate(strip, 0).astype(BF16)

    def put(ref, row, rows, value, above, below, lanes=slice(None)):
        over = min(max(above - row, 0), rows)
        under = min(max(row + rows - below, 0), rows)
        parts = [value[over * PITCH : (rows - under) * PITCH]]
        if over:
            parts.insert(0, value[: over * PITCH] * top)
        if under:
            parts.append(value[(rows - under) * PITCH :] * bottom)
        ref[row * PITCH : (row + rows) * PITCH, lanes] = jnp.concatenate(parts, 0).astype(ref.dtype)

    place = lax.broadcasted_iota(jnp.int32, (8, 128), 0)
    pooled[...] = pooled_in[...]
    mean = pool(x_c, w_in, 1, 32, STRIP)
    for row in range(16):
        v = mean[row] * top if row < 4 else mean[row] * bottom if row > 11 else mean[row]
        at = row * PITCH
        first = pooled_in[at : at + 8, :].astype(F32)
        pooled[at : at + 8, :] = jnp.where(place < 5, pltpu.roll(v[:8], 7, 0), first).astype(BF16)
        last = pooled_in[at + 64 : at + 72, :].astype(F32)
        pooled[at + 64 : at + 72, :] = jnp.where(place > 2, pltpu.roll(v[8:], 1, 0), last).astype(BF16)
    for row, rows in ((0, 14),):
        put(middle, row, rows, silu(half_conv(pooled, w_coarse, row + 1, rows)), 3, 11)
    embedded = scale[...] * noise_code + shift[...]
    for row, rows in ((0, 6), (6, 6)):
        d = silu(half_conv(middle, w_deeper, row + 1, rows)).astype(BF16)
        guide[row * PITCH : (row + rows) * PITCH, :] = matmul_nt(d, w_guide[...]) + embedded
    strips = pair_conv(x_s, w_noisy, 1, 22, True, STRIP)
    for row, rows in ((0, 12), (12, 10)):
        for half, strip in enumerate(strips):
            lanes = slice(128 * half, 128 * half + 128)
            parts = []
            for q in range(row, row + rows):
                at = q * PITCH
                left = pltpu.roll(strip[q * STRIP : q * STRIP + 8], 2, 0)
                first = jnp.where(place < 2, 0.0, jnp.where(place < 5, left, opening[at : at + 8, lanes]))
                right = pltpu.roll(strip[q * STRIP + 8 : q * STRIP + 16], 7, 0)
                last = jnp.where(place > 5, 0.0, jnp.where(place > 2, right, opening[at + 64 : at + 72, lanes]))
                g = (q + 1) // 2 * PITCH
                parts.append(jnp.concatenate([first, opening[at + 8 : at + 64, lanes], last], 0) + guide[g : g + PITCH, :])
            put(hidden, row, rows, silu(jnp.concatenate(parts, 0)), 3, 19, lanes)
    for row in (0, 10):
        for half, v in enumerate(pair_conv(hidden, w_block, 1 + row, 10)):
            put(inner, row, 10, silu(v), 2, 18, slice(128 * half, 128 * half + 128))
    for row, rows in ((0, 10), (10, 8)):
        h = hidden[(2 + row) * PITCH : (2 + row + rows) * PITCH, :].astype(F32)
        for half, v in enumerate(pair_conv(inner, w_branch, 1 + row, rows)):
            lanes = slice(128 * half, 128 * half + 128)
            put(mixed, row, rows, silu(v + h[:, lanes]), 1, 17, lanes)
    for first, rows in ((0, 6), (6, 6), (12, 4)):
        even, odd = pair_conv(mixed, w_out, 1 + first, rows)
        for q in range(rows):
            row = first + q
            at = slice(q * PITCH, (q + 1) * PITCH)
            turn[row, pl.ds(0, PITCH, stride=2), :] = even[at]
            turn[row, pl.ds(1, PITCH, stride=2), :] = odd[at]
            head = turn[row, 2 * EDGE : 2 * (EDGE + PAIRS), :].T[:CH]
            here = pl.ds(row, CH, stride=ROWS)
            out[here, :] = scale_skip * state[here, :] + scale_out * head


def net(n_lat, *args):
    vm = pl.BlockSpec(memory_space=VMEM)
    return pl.pallas_call(
        functools.partial(net_body, n_lat),
        out_shape=jax.ShapeDtypeStruct((CH * ROWS, 128), F32),
        in_specs=[pl.BlockSpec(memory_space=pltpu.SMEM)] + [vm] * (len(args) - 1),
        out_specs=vm,
        scratch_shapes=[
            VMEM((34 * STRIP, 256), BF16),
            VMEM((24 * STRIP, 256), BF16),
            VMEM((16 * PITCH, 128), BF16),
            VMEM((14 * PITCH, 256), BF16),
            VMEM((12 * PITCH, 128), F32),
            VMEM((22 * PITCH, 256), BF16),
            VMEM((20 * PITCH, 256), BF16),
            VMEM((18 * PITCH, 256), BF16),
            VMEM((ROWS, 2 * PITCH, 128), F32),
        ],
        compiler_params=pltpu.CompilerParams(vmem_limit_bytes=24 << 20),
        name="net",
    )(*args)


def on_device(
    mesh_shape,
    conditions,
    noisy_state,
    noise_level,
    kernel_input,
    kernel_coarse,
    kernel_deeper,
    guide_weight,
    time_scale,
    time_shift,
    kernel_noisy,
    kernel_block,
    kernel_branch,
    kernel_output,
):
    lon_even, lat_even = lax.axis_index("lon") % 2 == 0, lax.axis_index("lat") % 2 == 0
    cond = conditions.reshape(CH * ROWS, 128)
    state = noisy_state.reshape(CH * ROWS, 128)
    by_input = lambda kernel: kernel.transpose(0, 2, 1)
    in_hbm = lambda *values: [pltpu.with_memory_space_constraint(value, pltpu.HBM) for value in values]
    own_c, own_s, left, right, small_a, small_b, lat_a, lat_b, w_in, w_noisy = prep(
        noise_level, *in_hbm(cond, state, by_input(kernel_input), by_input(kernel_noisy))
    )
    permute = lambda value, a, o: lax.ppermute(value, AXES, swap_pairs(mesh_shape, a, o))
    small_b = permute(small_b, "B", None)
    small_a = permute(small_a, "A", None)
    lat_b = permute(lat_b, "B", None)
    lat_a = permute(lat_a, "A", None)
    above, below = jnp.where(lat_even, small_b, small_a), jnp.where(lat_even, small_a, small_b)
    left, right = (jnp.concatenate([above[n], edge, below[n]]) for n, edge in enumerate((left, right)))
    sent_a, sent_b = jnp.where(lon_even, right, left), jnp.where(lon_even, left, right)
    sent_b, sent_a, now_c, now_s = lax.optimization_barrier((sent_b, sent_a, own_c, own_s))
    edge_b = permute(sent_b, None, "B")
    edge_a = permute(sent_a, None, "A")
    during = own_rows(now_c, now_s, w_in, w_noisy)
    weights = in_hbm(kernel_coarse, kernel_deeper, guide_weight, kernel_block, kernel_branch, kernel_output)
    rest = inner(mesh_shape[1], own_c, own_s, lat_b, lat_a, w_in, w_noisy, *during, *weights)
    out = net(
        mesh_shape[1], noise_level, sent_b, sent_a, edge_b, edge_a, state,
        time_scale[None], time_shift[None], w_in, w_noisy, *rest,
    )
    return out.reshape(noisy_state.shape)


def solution(mesh):
    tile = P(None, "lat", "lon")
    member = P(None, None, "lat", "lon")
    return jax.shard_map(
        functools.partial(on_device, (mesh.shape["lon"], mesh.shape["lat"])),
        mesh=mesh,
        in_specs=(tile, member) + (P(),) * 11,
        out_specs=member,
        check_vma=False,
    )
```

```python
import functools

import jax
import jax.numpy as jnp
from jax import lax
from jax.experimental import pallas as pl
from jax.experimental.pallas import tpu as pltpu
from jax.sharding import PartitionSpec as P

F32 = jnp.float32
BF16 = jnp.bfloat16
PITCH = 72
EDGE = 4
STRIP = 16
ROWS = 16
PAIRS = 64
CH = 80
DEEP = 9
THIN = 4
VMEM = pltpu.VMEM
AXES = ("lon", "lat")


def swap_pairs(mesh_shape, lat, lon):
    n_lon, n_lat = mesh_shape
    pairs = []
    for o in range(n_lon):
        for a in range(n_lat):
            b, p = a, o
            if lat:
                b = a ^ 1 if lat == "A" else a - 1 + 2 * (a % 2)
            if lon:
                p = (o ^ 1 if lon == "A" else o - 1 + 2 * (o % 2)) % n_lon
            if 0 <= b < n_lat:
                pairs.append((o * n_lat + a, p * n_lat + b))
    return pairs


def silu(v):
    h = v * 0.5
    return h + h * jnp.tanh(h)


def matmul_nt(x, w):
    return lax.dot_general(x, w, (((1,), (1,)), ((), ())), preferred_element_type=F32)


def prep_body(
    noise, cond_hbm, state_hbm, k_in, k_noisy, own_c, own_s, left, right, small_a, small_b, lat_a, lat_b, w_in, w_noisy,
    cond, state, work, arrived,
):
    copies = [
        pltpu.make_async_copy(cond_hbm, cond, arrived.at[0]),
        pltpu.make_async_copy(state_hbm, state, arrived.at[1]),
        pltpu.make_async_copy(k_in, w_in.at[:, :CH, :], arrived.at[2]),
        pltpu.make_async_copy(k_noisy, w_noisy.at[:, :CH, :], arrived.at[3]),
    ]
    for copy in copies:
        copy.start()
    lat_even = lax.axis_index("lat") % 2 == 0
    sigma = jnp.full((1, 128), noise[0], F32)
    scale_in = 1.0 / jnp.sqrt(sigma * sigma + 0.25)
    row = lax.broadcasted_iota(jnp.int32, (128, 128), 0)
    col = lax.broadcasted_iota(jnp.int32, (128, 128), 1)
    pick = (col == jnp.where(row < PAIRS, 2 * row, 2 * (row - PAIRS) + 1)).astype(BF16)
    blank = jnp.zeros((128 - CH, 128), BF16)
    slot = lax.broadcasted_iota(jnp.int32, (8, 128), 0)
    for w in (w_in, w_noisy):
        w[:, CH:, :] = jnp.zeros((9, 128 - CH, 128), BF16)
    for copy in copies[:2]:
        copy.wait()
    work[...] = cond[...].astype(F32)
    for i in range(ROWS):
        c_row = work[pl.ds(i, CH, stride=ROWS), :].astype(BF16)
        s_row = (scale_in * state[pl.ds(i, CH, stride=ROWS), :]).astype(BF16)
        both = matmul_nt(pick, jnp.concatenate([c_row, blank, s_row, blank], 0))
        c_pair = jnp.concatenate([both[:PAIRS, :128], both[PAIRS:, :128]], 1)
        s_pair = jnp.concatenate([both[:PAIRS, 128:], both[PAIRS:, 128:]], 1)
        own_c[i * PAIRS : (i + 1) * PAIRS, :] = c_pair.astype(BF16)
        own_s[i * PAIRS : (i + 1) * PAIRS, :] = s_pair.astype(BF16)
        for half in range(2):
            lanes = slice(128 * half, 128 * half + 128)
            left[i, :, lanes] = jnp.where(slot < 5, c_pair[:8, lanes], pltpu.roll(s_pair[:8, lanes], 5, 0)).astype(BF16)
            right[i, :, lanes] = jnp.where(slot > 2, c_pair[-8:, lanes], pltpu.roll(s_pair[-8:, lanes], 3, 0)).astype(BF16)
    for side, edge in enumerate((left, right)):
        first, last = edge[:DEEP].astype(F32), edge[ROWS - DEEP :].astype(F32)
        small_a[side] = jnp.where(lat_even, last, first).astype(BF16)
        small_b[side] = jnp.where(lat_even, first, last).astype(BF16)
    lane = lax.broadcasted_iota(jnp.int32, (PAIRS, 128), 1)
    free = 128 - CH
    for k in range(DEEP):
        for half in range(2):
            lanes = slice(128 * half, 128 * half + 128)
            rows = []
            for first, s_first in ((0, 0), (ROWS - DEEP, ROWS - THIN)):
                at = (first + k) * PAIRS
                value = own_c[at : at + PAIRS, lanes].astype(F32)
                n = 2 * k + half
                if n < 4 * THIN:
                    r, h = divmod(n // 2, 2)
                    at = (s_first + r) * PAIRS
                    part = own_s[at : at + PAIRS, 128 * h : 128 * h + 128].astype(F32)
                    part = pltpu.roll(part, (CH - free * (n % 2)) % 128, 1)
                    value = jnp.where(lane < CH, value, part)
                rows.append(value)
            lat_a[k, :, lanes] = jnp.where(lat_even, rows[1], rows[0]).astype(BF16)
            lat_b[k, :, lanes] = jnp.where(lat_even, rows[0], rows[1]).astype(BF16)
    for copy in copies[2:]:
        copy.wait()


def prep(noise, *args):
    vm = pl.BlockSpec(memory_space=VMEM)
    own = jax.ShapeDtypeStruct((ROWS * PAIRS, 256), BF16)
    edge = jax.ShapeDtypeStruct((ROWS, 8, 256), BF16)
    small = jax.ShapeDtypeStruct((2, DEEP, 8, 256), BF16)
    rows = jax.ShapeDtypeStruct((DEEP, PAIRS, 256), BF16)
    weights = jax.ShapeDtypeStruct((9, 128, 128), BF16)
    return pl.pallas_call(
        prep_body,
        out_shape=(own, own, edge, edge, small, small, rows, rows, weights, weights),
        in_specs=[pl.BlockSpec(memory_space=pltpu.SMEM)] + [pl.BlockSpec(memory_space=pltpu.HBM)] * 4,
        out_specs=[vm] * 10,
        scratch_shapes=[
            VMEM((CH * ROWS, 128), BF16),
            VMEM((CH * ROWS, 128), F32),
            VMEM((CH * ROWS, 128), F32),
            pltpu.SemaphoreType.DMA((4,)),
        ],
        compiler_params=pltpu.CompilerParams(vmem_limit_bytes=12 << 20),
        name="prep",
    )(noise, *args)


def pair_weights(w, di):
    k0, k1, k2 = w[3 * di], w[3 * di + 1], w[3 * di + 2]
    z = jnp.zeros_like(k0)
    c = jnp.concatenate
    return c([c([k1, k2], 1), c([k0, k1], 1), c([z, k0], 1), c([k2, z], 1)], 0)


def pair_weights_by_input(w, di):
    k0, k1, k2 = w[3 * di], w[3 * di + 1], w[3 * di + 2]
    z = jnp.zeros_like(k0)
    c = jnp.concatenate
    return c([c([k1, k0, z, k2], 1), c([k2, k1, k0, z], 1)], 0)


def pair_conv(x, w, centre, rows, by_input=False, pitch=PITCH):
    span = rows * pitch
    taps = [x[(centre + d - 1) * pitch : (centre + d - 1) * pitch + span, :] for d in range(3)]
    taps = jnp.concatenate(taps, 1)
    if by_input:
        weights = jnp.concatenate([pair_weights_by_input(w, d) for d in range(3)], 0)
        y = jnp.dot(taps, weights, preferred_element_type=F32)
    else:
        y = matmul_nt(taps, jnp.concatenate([pair_weights(w, d) for d in range(3)], 1))
    even = y[:, 0:128] + pltpu.roll(y[:, 256:384], 1, 0)
    odd = y[:, 128:256] + pltpu.roll(y[:, 384:512], span - 1, 0)
    return even, odd


def half_conv(x, w, centre, rows):
    span = rows * PITCH
    c = jnp.concatenate
    taps = c([x[(centre + d - 1) * PITCH : (centre + d - 1) * PITCH + span, :] for d in range(3)], 1)
    weights = c([c([w[3 * d + b] for d in range(3)], 1) for b in range(3)], 0)
    y = matmul_nt(taps, weights)
    n = y.shape[1] // 3
    return y[:, n : 2 * n] + pltpu.roll(y[:, :n], 1, 0) + pltpu.roll(y[:, 2 * n :], span - 1, 0)


def pool(x, w, centre, rows, pitch):
    even, odd = pair_conv(x, w, centre, rows, True, pitch)
    both = silu(even).astype(BF16).astype(F32) + silu(odd).astype(BF16).astype(F32)
    both = both.reshape(rows // 2, 2, pitch, 128)
    return (both[:, 0] + both[:, 1]) * 0.25


def band(n_lat):
    lat = lax.axis_index("lat")
    return (lat > 0).astype(F32), (lat < n_lat - 1).astype(F32)


def own_body(
    own_c, own_s, w_in, w_noisy, k_coarse, k_block, k_branch, k_out,
    w_coarse, w_block, w_branch, w_out, pooled, opening,
    arrived,
):
    moves = [(k_coarse, w_coarse), (k_block, w_block), (k_branch, w_branch), (k_out, w_out.at[:, :CH, :])]
    copies = [pltpu.make_async_copy(src, dst, arrived.at[n]) for n, (src, dst) in enumerate(moves)]
    for copy in copies:
        copy.start()
    w_out[:, CH:, :] = jnp.zeros((9, 128 - CH, 128), BF16)
    mean = pool(own_c, w_in, 2, 12, PAIRS)
    for q in range(6):
        pooled[q * PITCH + EDGE : q * PITCH + EDGE + PAIRS, :] = mean[q].astype(BF16)
    for row, rows in ((0, 6), (6, 8)):
        for half, v in enumerate(pair_conv(own_s, w_noisy, 1 + row, rows, True, PAIRS)):
            for q in range(rows):
                at = (row + q) * PITCH + EDGE
                opening[at : at + PAIRS, 128 * half : 128 * half + 128] = v[q * PAIRS : (q + 1) * PAIRS]
    for copy in copies:
        copy.wait()


def own_rows(*args):
    vm = pl.BlockSpec(memory_space=VMEM)
    wide = lambda n, k: jax.ShapeDtypeStruct((9, n, k), BF16)
    return pl.pallas_call(
        own_body,
        out_shape=(
            wide(256, 128), wide(128, 128), wide(128, 128), wide(128, 128),
            jax.ShapeDtypeStruct((6 * PITCH, 128), BF16), jax.ShapeDtypeStruct((14 * PITCH, 256), F32),
        ),
        in_specs=[vm] * 4 + [pl.BlockSpec(memory_space=pltpu.HBM)] * 4,
        out_specs=[vm] * 6,
        scratch_shapes=[pltpu.SemaphoreType.DMA((4,))],
        compiler_params=pltpu.CompilerParams(vmem_limit_bytes=12 << 20),
        cost_estimate=pl.CostEstimate(flops=2 * 10**9, bytes_accessed=3 * 10**6, transcendentals=5 * 10**5),
        name="own_rows",
    )(*args)


def inner_body(
    n_lat,
    own_c, own_s, lat_b, lat_a, w_in, w_noisy, pool_own, open_own,
    k_deeper, k_guide, w_deeper, w_guide, pooled, opening,
    x_c, x_s, arrived,
):
    moves = [(k_deeper, w_deeper), (k_guide, w_guide)]
    copies = [pltpu.make_async_copy(src, dst, arrived.at[n]) for n, (src, dst) in enumerate(moves)]
    for copy in copies:
        copy.start()
    top, bottom = band(n_lat)
    lat_even = lax.axis_index("lat") % 2 == 0
    free = 128 - CH
    lane = lax.broadcasted_iota(jnp.int32, (1, 128), 1)
    for x, own, n, deep in ((x_c, own_c, 3, DEEP), (x_s, own_s, 2, THIN)):
        x[deep * PAIRS : (deep + n) * PAIRS, :] = own[: n * PAIRS, :]
        x[(deep + n) * PAIRS : (deep + 2 * n) * PAIRS, :] = own[(ROWS - n) * PAIRS :, :]
    for below in range(2):

        def received(k, lanes):
            a, b = lat_a[k, :, lanes].astype(F32), lat_b[k, :, lanes].astype(F32)
            return jnp.where(lat_even, a, b) if below else jnp.where(lat_even, b, a)

        for k in range(DEEP):
            at = (DEEP + 6 + k if below else k) * PAIRS
            x_c[at : at + PAIRS, :] = received(k, slice(None)).astype(BF16)
        for r in range(THIN):
            at = (THIN + 4 + r if below else r) * PAIRS
            for h in range(2):
                n = 2 * (2 * r + h)
                parts = [
                    pltpu.roll(received(m // 2, slice(128 * (m % 2), 128 * (m % 2) + 128)), (128 - CH + free * (m % 2)) % 128, 1)
                    for m in (n, n + 1)
                ]
                x_s[at : at + PAIRS, 128 * h : 128 * h + 128] = jnp.where(lane < free, *parts).astype(BF16)
    for row, centre in ((0, 1), (11, 13)):
        mean = pool(x_c, w_in, centre, 10, PAIRS)
        for q in range(5):
            v = mean[q]
            if row + q < 4:
                v = v * top
            if row + q >= 12:
                v = v * bottom
            at = (row + q) * PITCH + EDGE
            pooled[at : at + PAIRS, :] = v.astype(BF16)
    for row, centre in ((0, 1), (18, 7)):
        for half, v in enumerate(pair_conv(x_s, w_noisy, centre, 4, True, PAIRS)):
            for q in range(4):
                at = (row + q) * PITCH + EDGE
                opening[at : at + PAIRS, 128 * half : 128 * half + 128] = v[q * PAIRS : (q + 1) * PAIRS]
    pooled[5 * PITCH : 11 * PITCH, :] = pool_own[...]
    opening[4 * PITCH : 18 * PITCH, :] = open_own[...]
    for copy in copies:
        copy.wait()


def inner(n_lat, *args):
    vm = pl.BlockSpec(memory_space=VMEM)
    wide = lambda n, k: jax.ShapeDtypeStruct((9, n, k), BF16)
    out_shape = (
        wide(256, 256), jax.ShapeDtypeStruct((128, 256), BF16),
        jax.ShapeDtypeStruct((16 * PITCH, 128), BF16), jax.ShapeDtypeStruct((22 * PITCH, 256), F32),
    )
    return pl.pallas_call(
        functools.partial(inner_body, n_lat),
        out_shape=out_shape,
        in_specs=[vm] * 8 + [pl.BlockSpec(memory_space=pltpu.HBM)] * 2,
        out_specs=[vm] * len(out_shape),
        scratch_shapes=[
            VMEM((24 * PAIRS, 256), BF16),
            VMEM((12 * PAIRS, 256), BF16),
            pltpu.SemaphoreType.DMA((2,)),
        ],
        compiler_params=pltpu.CompilerParams(vmem_limit_bytes=20 << 20),
        cost_estimate=pl.CostEstimate(flops=3 * 10**9, bytes_accessed=6 * 10**6, transcendentals=10**6),
        name="inner",
    )(*args)


def net_body(
    n_lat,
    noise, sent_b, sent_a, edge_b, edge_a, state, scale, shift,
    w_in, w_noisy, w_coarse, w_block, w_branch, w_out, w_deeper, w_guide, pooled_in, opening,
    out, x_c, x_s, pooled, middle, guide, hidden, inner, mixed, turn,
):
    top, bottom = band(n_lat)
    lon_even = lax.axis_index("lon") % 2 == 0
    sigma = jnp.full((1, 128), noise[0], F32)
    variance = sigma * sigma + 0.25
    scale_skip = 0.25 / variance
    scale_out = 0.5 * sigma / jnp.sqrt(variance)
    noise_code = jnp.log(sigma) / 4.0

    slot = lax.broadcasted_iota(jnp.int32, (8, 256), 0)
    for k in range(DEEP + ROWS + DEEP):
        sa, sb = sent_a[k].astype(F32), sent_b[k].astype(F32)
        ea, eb = edge_a[k].astype(F32), edge_b[k].astype(F32)
        own_left, own_right = jnp.where(lon_even, sb, sa), jnp.where(lon_even, sa, sb)
        left, right = jnp.where(lon_even, eb, ea), jnp.where(lon_even, ea, eb)
        strip = [
            pltpu.roll(jnp.where(slot > 2, left, own_left), 5, 0),
            pltpu.roll(jnp.where(slot < 5, right, own_right), 3, 0),
        ]
        x_c[k * STRIP : (k + 1) * STRIP, :] = jnp.concatenate(strip, 0).astype(BF16)
        r = k - (DEEP - THIN)
        if 0 <= r < THIN + ROWS + THIN:
            strip = [
                jnp.where(slot < 2, pltpu.roll(left, 7, 0), jnp.where(slot < 5, pltpu.roll(own_left, 5, 0), 0.0)),
                jnp.where(slot > 4, right, jnp.where(slot > 1, pltpu.roll(own_right, 2, 0), 0.0)),
            ]
            x_s[r * STRIP : (r + 1) * STRIP, :] = jnp.concatenate(strip, 0).astype(BF16)

    def put(ref, row, rows, value, above, below, lanes=slice(None)):
        over = min(max(above - row, 0), rows)
        under = min(max(row + rows - below, 0), rows)
        parts = [value[over * PITCH : (rows - under) * PITCH]]
        if over:
            parts.insert(0, value[: over * PITCH] * top)
        if under:
            parts.append(value[(rows - under) * PITCH :] * bottom)
        ref[row * PITCH : (row + rows) * PITCH, lanes] = jnp.concatenate(parts, 0).astype(ref.dtype)

    place = lax.broadcasted_iota(jnp.int32, (8, 128), 0)
    pooled[...] = pooled_in[...]
    mean = pool(x_c, w_in, 1, 32, STRIP)
    for row in range(16):
        v = mean[row] * top if row < 4 else mean[row] * bottom if row > 11 else mean[row]
        at = row * PITCH
        first = pooled_in[at : at + 8, :].astype(F32)
        pooled[at : at + 8, :] = jnp.where(place < 5, pltpu.roll(v[:8], 7, 0), first).astype(BF16)
        last = pooled_in[at + 64 : at + 72, :].astype(F32)
        pooled[at + 64 : at + 72, :] = jnp.where(place > 2, pltpu.roll(v[8:], 1, 0), last).astype(BF16)
    for row, rows in ((0, 14),):
        put(middle, row, rows, silu(half_conv(pooled, w_coarse, row + 1, rows)), 3, 11)
    embedded = scale[...] * noise_code + shift[...]
    for row, rows in ((0, 6), (6, 6)):
        d = silu(half_conv(middle, w_deeper, row + 1, rows)).astype(BF16)
        guide[row * PITCH : (row + rows) * PITCH, :] = matmul_nt(d, w_guide[...]) + embedded
    strips = pair_conv(x_s, w_noisy, 1, 22, True, STRIP)
    for row, rows in ((0, 12), (12, 10)):
        for half, strip in enumerate(strips):
            lanes = slice(128 * half, 128 * half + 128)
            parts = []
            for q in range(row, row + rows):
                at = q * PITCH
                left = pltpu.roll(strip[q * STRIP : q * STRIP + 8], 2, 0)
                first = jnp.where(place < 2, 0.0, jnp.where(place < 5, left, opening[at : at + 8, lanes]))
                right = pltpu.roll(strip[q * STRIP + 8 : q * STRIP + 16], 7, 0)
                last = jnp.where(place > 5, 0.0, jnp.where(place > 2, right, opening[at + 64 : at + 72, lanes]))
                g = (q + 1) // 2 * PITCH
                parts.append(jnp.concatenate([first, opening[at + 8 : at + 64, lanes], last], 0) + guide[g : g + PITCH, :])
            put(hidden, row, rows, silu(jnp.concatenate(parts, 0)), 3, 19, lanes)
    for row in (0, 10):
        for half, v in enumerate(pair_conv(hidden, w_block, 1 + row, 10)):
            put(inner, row, 10, silu(v), 2, 18, slice(128 * half, 128 * half + 128))
    for row, rows in ((0, 10), (10, 8)):
        h = hidden[(2 + row) * PITCH : (2 + row + rows) * PITCH, :].astype(F32)
        for half, v in enumerate(pair_conv(inner, w_branch, 1 + row, rows)):
            lanes = slice(128 * half, 128 * half + 128)
            put(mixed, row, rows, silu(v + h[:, lanes]), 1, 17, lanes)
    for first, rows in ((0, 6), (6, 6), (12, 4)):
        even, odd = pair_conv(mixed, w_out, 1 + first, rows)
        for q in range(rows):
            row = first + q
            at = slice(q * PITCH, (q + 1) * PITCH)
            turn[row, pl.ds(0, PITCH, stride=2), :] = even[at]
            turn[row, pl.ds(1, PITCH, stride=2), :] = odd[at]
            head = turn[row, 2 * EDGE : 2 * (EDGE + PAIRS), :].T[:CH]
            here = pl.ds(row, CH, stride=ROWS)
            out[here, :] = scale_skip * state[here, :] + scale_out * head


def net(n_lat, *args):
    vm = pl.BlockSpec(memory_space=VMEM)
    return pl.pallas_call(
        functools.partial(net_body, n_lat),
        out_shape=jax.ShapeDtypeStruct((CH * ROWS, 128), F32),
        in_specs=[pl.BlockSpec(memory_space=pltpu.SMEM)] + [vm] * (len(args) - 1),
        out_specs=vm,
        scratch_shapes=[
            VMEM((34 * STRIP, 256), BF16),
            VMEM((24 * STRIP, 256), BF16),
            VMEM((16 * PITCH, 128), BF16),
            VMEM((14 * PITCH, 256), BF16),
            VMEM((12 * PITCH, 128), F32),
            VMEM((22 * PITCH, 256), BF16),
            VMEM((20 * PITCH, 256), BF16),
            VMEM((18 * PITCH, 256), BF16),
            VMEM((ROWS, 2 * PITCH, 128), F32),
        ],
        compiler_params=pltpu.CompilerParams(vmem_limit_bytes=24 << 20),
        name="net",
    )(*args)


def on_device(
    mesh_shape,
    conditions,
    noisy_state,
    noise_level,
    kernel_input,
    kernel_coarse,
    kernel_deeper,
    guide_weight,
    time_scale,
    time_shift,
    kernel_noisy,
    kernel_block,
    kernel_branch,
    kernel_output,
):
    lon_even, lat_even = lax.axis_index("lon") % 2 == 0, lax.axis_index("lat") % 2 == 0
    cond = conditions.reshape(CH * ROWS, 128)
    state = noisy_state.reshape(CH * ROWS, 128)
    by_input = lambda kernel: kernel.transpose(0, 2, 1)
    in_hbm = lambda *values: [pltpu.with_memory_space_constraint(value, pltpu.HBM) for value in values]
    own_c, own_s, left, right, small_a, small_b, lat_a, lat_b, w_in, w_noisy = prep(
        noise_level, *in_hbm(cond, state, by_input(kernel_input), by_input(kernel_noisy))
    )
    permute = lambda value, a, o: lax.ppermute(value, AXES, swap_pairs(mesh_shape, a, o))
    small_b = permute(small_b, "B", None)
    small_a = permute(small_a, "A", None)
    lat_b = permute(lat_b, "B", None)
    lat_a = permute(lat_a, "A", None)
    above, below = jnp.where(lat_even, small_b, small_a), jnp.where(lat_even, small_a, small_b)
    left, right = (jnp.concatenate([above[n], edge, below[n]]) for n, edge in enumerate((left, right)))
    sent_a, sent_b = jnp.where(lon_even, right, left), jnp.where(lon_even, left, right)
    sent_b, sent_a, now_c, now_s = lax.optimization_barrier((sent_b, sent_a, own_c, own_s))
    edge_b = permute(sent_b, None, "B")
    edge_a = permute(sent_a, None, "A")
    *fetched, pool_own, open_own = own_rows(
        now_c, now_s, w_in, w_noisy, *in_hbm(kernel_coarse, kernel_block, kernel_branch, kernel_output)
    )
    rest = inner(
        mesh_shape[1], own_c, own_s, lat_b, lat_a, w_in, w_noisy, pool_own, open_own, *in_hbm(kernel_deeper, guide_weight)
    )
    out = net(
        mesh_shape[1], noise_level, sent_b, sent_a, edge_b, edge_a, state,
        time_scale[None], time_shift[None], w_in, w_noisy, *fetched, *rest,
    )
    return out.reshape(noisy_state.shape)


def solution(mesh):
    tile = P(None, "lat", "lon")
    member = P(None, None, "lat", "lon")
    return jax.shard_map(
        functools.partial(on_device, (mesh.shape["lon"], mesh.shape["lat"])),
        mesh=mesh,
        in_specs=(tile, member) + (P(),) * 11,
        out_specs=member,
        check_vma=False,
    )
```

```python
import functools

import jax
import jax.numpy as jnp
from jax import lax
from jax.experimental import pallas as pl
from jax.experimental.pallas import tpu as pltpu
from jax.sharding import PartitionSpec as P

F32 = jnp.float32
BF16 = jnp.bfloat16
PITCH = 72
EDGE = 4
STRIP = 16
ROWS = 16
PAIRS = 64
CH = 80
DEEP = 9
THIN = 4
VMEM = pltpu.VMEM
AXES = ("lon", "lat")


def swap_pairs(mesh_shape, lat, lon):
    n_lon, n_lat = mesh_shape
    pairs = []
    for o in range(n_lon):
        for a in range(n_lat):
            b, p = a, o
            if lat:
                b = a ^ 1 if lat == "A" else a - 1 + 2 * (a % 2)
            if lon:
                p = (o ^ 1 if lon == "A" else o - 1 + 2 * (o % 2)) % n_lon
            if 0 <= b < n_lat:
                pairs.append((o * n_lat + a, p * n_lat + b))
    return pairs


def silu(v):
    h = v * 0.5
    return h + h * jnp.tanh(h)


def matmul_nt(x, w):
    return lax.dot_general(x, w, (((1,), (1,)), ((), ())), preferred_element_type=F32)


def prep_body(
    noise, cond_hbm, state_hbm, k_in, k_noisy, own_c, own_s, left, right, small_a, small_b, lat_a, lat_b, w_in, w_noisy,
    cond, state, work, arrived,
):
    copies = [
        pltpu.make_async_copy(cond_hbm, cond, arrived.at[0]),
        pltpu.make_async_copy(state_hbm, state, arrived.at[1]),
        pltpu.make_async_copy(k_in, w_in.at[:, :CH, :], arrived.at[2]),
        pltpu.make_async_copy(k_noisy, w_noisy.at[:, :CH, :], arrived.at[3]),
    ]
    for copy in copies:
        copy.start()
    lat_even = lax.axis_index("lat") % 2 == 0
    sigma = jnp.full((1, 128), noise[0], F32)
    scale_in = 1.0 / jnp.sqrt(sigma * sigma + 0.25)
    row = lax.broadcasted_iota(jnp.int32, (128, 128), 0)
    col = lax.broadcasted_iota(jnp.int32, (128, 128), 1)
    pick = (col == jnp.where(row < PAIRS, 2 * row, 2 * (row - PAIRS) + 1)).astype(BF16)
    blank = jnp.zeros((128 - CH, 128), BF16)
    slot = lax.broadcasted_iota(jnp.int32, (8, 128), 0)
    for w in (w_in, w_noisy):
        w[:, CH:, :] = jnp.zeros((9, 128 - CH, 128), BF16)
    for copy in copies[:2]:
        copy.wait()
    work[...] = cond[...].astype(F32)
    for i in range(ROWS):
        c_row = work[pl.ds(i, CH, stride=ROWS), :].astype(BF16)
        s_row = (scale_in * state[pl.ds(i, CH, stride=ROWS), :]).astype(BF16)
        both = matmul_nt(pick, jnp.concatenate([c_row, blank, s_row, blank], 0))
        c_pair = jnp.concatenate([both[:PAIRS, :128], both[PAIRS:, :128]], 1)
        s_pair = jnp.concatenate([both[:PAIRS, 128:], both[PAIRS:, 128:]], 1)
        own_c[i * PAIRS : (i + 1) * PAIRS, :] = c_pair.astype(BF16)
        own_s[i * PAIRS : (i + 1) * PAIRS, :] = s_pair.astype(BF16)
        for half in range(2):
            lanes = slice(128 * half, 128 * half + 128)
            left[i, :, lanes] = jnp.where(slot < 5, c_pair[:8, lanes], pltpu.roll(s_pair[:8, lanes], 5, 0)).astype(BF16)
            right[i, :, lanes] = jnp.where(slot > 2, c_pair[-8:, lanes], pltpu.roll(s_pair[-8:, lanes], 3, 0)).astype(BF16)
    for side, edge in enumerate((left, right)):
        first, last = edge[:DEEP].astype(F32), edge[ROWS - DEEP :].astype(F32)
        small_a[side] = jnp.where(lat_even, last, first).astype(BF16)
        small_b[side] = jnp.where(lat_even, first, last).astype(BF16)
    lane = lax.broadcasted_iota(jnp.int32, (PAIRS, 128), 1)
    free = 128 - CH
    for k in range(DEEP):
        for half in range(2):
            lanes = slice(128 * half, 128 * half + 128)
            rows = []
            for first, s_first in ((0, 0), (ROWS - DEEP, ROWS - THIN)):
                at = (first + k) * PAIRS
                value = own_c[at : at + PAIRS, lanes].astype(F32)
                n = 2 * k + half
                if n < 4 * THIN:
                    r, h = divmod(n // 2, 2)
                    at = (s_first + r) * PAIRS
                    part = own_s[at : at + PAIRS, 128 * h : 128 * h + 128].astype(F32)
                    part = pltpu.roll(part, (CH - free * (n % 2)) % 128, 1)
                    value = jnp.where(lane < CH, value, part)
                rows.append(value)
            lat_a[k, :, lanes] = jnp.where(lat_even, rows[1], rows[0]).astype(BF16)
            lat_b[k, :, lanes] = jnp.where(lat_even, rows[0], rows[1]).astype(BF16)
    for copy in copies[2:]:
        copy.wait()


def prep(noise, *args):
    vm = pl.BlockSpec(memory_space=VMEM)
    own = jax.ShapeDtypeStruct((ROWS * PAIRS, 256), BF16)
    edge = jax.ShapeDtypeStruct((ROWS, 8, 256), BF16)
    small = jax.ShapeDtypeStruct((2, DEEP, 8, 256), BF16)
    rows = jax.ShapeDtypeStruct((DEEP, PAIRS, 256), BF16)
    weights = jax.ShapeDtypeStruct((9, 128, 128), BF16)
    return pl.pallas_call(
        prep_body,
        out_shape=(own, own, edge, edge, small, small, rows, rows, weights, weights),
        in_specs=[pl.BlockSpec(memory_space=pltpu.SMEM)] + [pl.BlockSpec(memory_space=pltpu.HBM)] * 4,
        out_specs=[vm] * 10,
        scratch_shapes=[
            VMEM((CH * ROWS, 128), BF16),
            VMEM((CH * ROWS, 128), F32),
            VMEM((CH * ROWS, 128), F32),
            pltpu.SemaphoreType.DMA((4,)),
        ],
        compiler_params=pltpu.CompilerParams(vmem_limit_bytes=12 << 20),
        name="prep",
    )(noise, *args)


def pair_weights(w, di):
    k0, k1, k2 = w[3 * di], w[3 * di + 1], w[3 * di + 2]
    z = jnp.zeros_like(k0)
    c = jnp.concatenate
    return c([c([k1, k2], 1), c([k0, k1], 1), c([z, k0], 1), c([k2, z], 1)], 0)


def pair_weights_by_input(w, di):
    k0, k1, k2 = w[3 * di], w[3 * di + 1], w[3 * di + 2]
    z = jnp.zeros_like(k0)
    c = jnp.concatenate
    return c([c([k1, k0, z, k2], 1), c([k2, k1, k0, z], 1)], 0)


def pair_conv(x, w, centre, rows, by_input=False, pitch=PITCH):
    span = rows * pitch
    taps = [x[(centre + d - 1) * pitch : (centre + d - 1) * pitch + span, :] for d in range(3)]
    taps = jnp.concatenate(taps, 1)
    if by_input:
        weights = jnp.concatenate([pair_weights_by_input(w, d) for d in range(3)], 0)
        y = jnp.dot(taps, weights, preferred_element_type=F32)
    else:
        y = matmul_nt(taps, jnp.concatenate([pair_weights(w, d) for d in range(3)], 1))
    even = y[:, 0:128] + pltpu.roll(y[:, 256:384], 1, 0)
    odd = y[:, 128:256] + pltpu.roll(y[:, 384:512], span - 1, 0)
    return even, odd


def half_conv(x, w, centre, rows):
    span = rows * PITCH
    c = jnp.concatenate
    taps = c([x[(centre + d - 1) * PITCH : (centre + d - 1) * PITCH + span, :] for d in range(3)], 1)
    weights = c([c([w[3 * d + b] for d in range(3)], 1) for b in range(3)], 0)
    y = matmul_nt(taps, weights)
    n = y.shape[1] // 3
    return y[:, n : 2 * n] + pltpu.roll(y[:, :n], 1, 0) + pltpu.roll(y[:, 2 * n :], span - 1, 0)


def pool(x, w, centre, rows, pitch):
    even, odd = pair_conv(x, w, centre, rows, True, pitch)
    both = silu(even).astype(BF16).astype(F32) + silu(odd).astype(BF16).astype(F32)
    both = both.reshape(rows // 2, 2, pitch, 128)
    return (both[:, 0] + both[:, 1]) * 0.25


def band(n_lat):
    lat = lax.axis_index("lat")
    return (lat > 0).astype(F32), (lat < n_lat - 1).astype(F32)


def own_body(
    own_c, own_s, w_in, w_noisy, k_coarse, k_block, k_branch, k_out,
    w_coarse, w_block, w_branch, w_out, pooled, opening,
    arrived,
):
    moves = [(k_coarse, w_coarse), (k_block, w_block), (k_branch, w_branch), (k_out, w_out.at[:, :CH, :])]
    copies = [pltpu.make_async_copy(src, dst, arrived.at[n]) for n, (src, dst) in enumerate(moves)]
    for copy in copies:
        copy.start()
    w_out[:, CH:, :] = jnp.zeros((9, 128 - CH, 128), BF16)
    mean = pool(own_c, w_in, 2, 12, PAIRS)
    for q in range(6):
        pooled[q * PITCH + EDGE : q * PITCH + EDGE + PAIRS, :] = mean[q].astype(BF16)
    for row, rows in ((0, 6), (6, 8)):
        for half, v in enumerate(pair_conv(own_s, w_noisy, 1 + row, rows, True, PAIRS)):
            for q in range(rows):
                at = (row + q) * PITCH + EDGE
                opening[at : at + PAIRS, 128 * half : 128 * half + 128] = v[q * PAIRS : (q + 1) * PAIRS]
    for copy in copies:
        copy.wait()


def own_rows(*args):
    vm = pl.BlockSpec(memory_space=VMEM)
    wide = lambda n, k: jax.ShapeDtypeStruct((9, n, k), BF16)
    return pl.pallas_call(
        own_body,
        out_shape=(
            wide(256, 128), wide(128, 128), wide(128, 128), wide(128, 128),
            jax.ShapeDtypeStruct((6 * PITCH, 128), BF16), jax.ShapeDtypeStruct((14 * PITCH, 256), F32),
        ),
        in_specs=[vm] * 4 + [pl.BlockSpec(memory_space=pltpu.HBM)] * 4,
        out_specs=[vm] * 6,
        scratch_shapes=[pltpu.SemaphoreType.DMA((4,))],
        compiler_params=pltpu.CompilerParams(vmem_limit_bytes=12 << 20),
        cost_estimate=pl.CostEstimate(flops=2 * 10**9, bytes_accessed=3 * 10**6, transcendentals=5 * 10**5),
        name="own_rows",
    )(*args)


def inner_body(
    n_lat,
    own_c, own_s, lat_b, lat_a, w_in, w_noisy, pool_own, open_own,
    k_deeper, k_guide, w_deeper, w_guide, pooled, opening,
    x_c, x_s, arrived,
):
    moves = [(k_deeper, w_deeper), (k_guide, w_guide)]
    copies = [pltpu.make_async_copy(src, dst, arrived.at[n]) for n, (src, dst) in enumerate(moves)]
    for copy in copies:
        copy.start()
    top, bottom = band(n_lat)
    lat_even = lax.axis_index("lat") % 2 == 0
    free = 128 - CH
    lane = lax.broadcasted_iota(jnp.int32, (1, 128), 1)
    for x, own, n, deep in ((x_c, own_c, 3, DEEP), (x_s, own_s, 2, THIN)):
        x[deep * PAIRS : (deep + n) * PAIRS, :] = own[: n * PAIRS, :]
        x[(deep + n) * PAIRS : (deep + 2 * n) * PAIRS, :] = own[(ROWS - n) * PAIRS :, :]
    for below in range(2):

        def received(k, lanes):
            a, b = lat_a[k, :, lanes].astype(F32), lat_b[k, :, lanes].astype(F32)
            return jnp.where(lat_even, a, b) if below else jnp.where(lat_even, b, a)

        for k in range(DEEP):
            at = (DEEP + 6 + k if below else k) * PAIRS
            x_c[at : at + PAIRS, :] = received(k, slice(None)).astype(BF16)
        for r in range(THIN):
            at = (THIN + 4 + r if below else r) * PAIRS
            for h in range(2):
                n = 2 * (2 * r + h)
                parts = [
                    pltpu.roll(received(m // 2, slice(128 * (m % 2), 128 * (m % 2) + 128)), (128 - CH + free * (m % 2)) % 128, 1)
                    for m in (n, n + 1)
                ]
                x_s[at : at + PAIRS, 128 * h : 128 * h + 128] = jnp.where(lane < free, *parts).astype(BF16)
    for row, centre in ((0, 1), (11, 13)):
        mean = pool(x_c, w_in, centre, 10, PAIRS)
        for q in range(5):
            v = mean[q]
            if row + q < 4:
                v = v * top
            if row + q >= 12:
                v = v * bottom
            at = (row + q) * PITCH + EDGE
            pooled[at : at + PAIRS, :] = v.astype(BF16)
    for row, centre in ((0, 1), (18, 7)):
        for half, v in enumerate(pair_conv(x_s, w_noisy, centre, 4, True, PAIRS)):
            for q in range(4):
                at = (row + q) * PITCH + EDGE
                opening[at : at + PAIRS, 128 * half : 128 * half + 128] = v[q * PAIRS : (q + 1) * PAIRS]
    pooled[5 * PITCH : 11 * PITCH, :] = pool_own[...]
    opening[4 * PITCH : 18 * PITCH, :] = open_own[...]
    for copy in copies:
        copy.wait()


def inner(n_lat, *args):
    vm = pl.BlockSpec(memory_space=VMEM)
    wide = lambda n, k: jax.ShapeDtypeStruct((9, n, k), BF16)
    out_shape = (
        wide(256, 256), jax.ShapeDtypeStruct((128, 256), BF16),
        jax.ShapeDtypeStruct((16 * PITCH, 128), BF16), jax.ShapeDtypeStruct((22 * PITCH, 256), F32),
    )
    return pl.pallas_call(
        functools.partial(inner_body, n_lat),
        out_shape=out_shape,
        in_specs=[vm] * 8 + [pl.BlockSpec(memory_space=pltpu.HBM)] * 2,
        out_specs=[vm] * len(out_shape),
        scratch_shapes=[
            VMEM((24 * PAIRS, 256), BF16),
            VMEM((12 * PAIRS, 256), BF16),
            pltpu.SemaphoreType.DMA((2,)),
        ],
        compiler_params=pltpu.CompilerParams(vmem_limit_bytes=20 << 20),
        cost_estimate=pl.CostEstimate(flops=3 * 10**9, bytes_accessed=6 * 10**6, transcendentals=10**6),
        name="inner",
    )(*args)


def net_body(
    n_lat,
    noise, sent_b, sent_a, edge_b, edge_a, state, scale, shift,
    w_in, w_noisy, w_coarse, w_block, w_branch, w_out, w_deeper, w_guide, pooled_in, opening,
    out, x_c, x_s, pooled, middle, guide, hidden, inner, mixed, turn,
):
    top, bottom = band(n_lat)
    lon_even = lax.axis_index("lon") % 2 == 0
    sigma = jnp.full((1, 128), noise[0], F32)
    variance = sigma * sigma + 0.25
    scale_skip = 0.25 / variance
    scale_out = 0.5 * sigma / jnp.sqrt(variance)
    noise_code = jnp.log(sigma) / 4.0

    slot = lax.broadcasted_iota(jnp.int32, (8, 256), 0)
    for k in range(DEEP + ROWS + DEEP):
        sa, sb = sent_a[k].astype(F32), sent_b[k].astype(F32)
        ea, eb = edge_a[k].astype(F32), edge_b[k].astype(F32)
        own_left, own_right = jnp.where(lon_even, sb, sa), jnp.where(lon_even, sa, sb)
        left, right = jnp.where(lon_even, eb, ea), jnp.where(lon_even, ea, eb)
        strip = [
            pltpu.roll(jnp.where(slot > 2, left, own_left), 5, 0),
            pltpu.roll(jnp.where(slot < 5, right, own_right), 3, 0),
        ]
        x_c[k * STRIP : (k + 1) * STRIP, :] = jnp.concatenate(strip, 0).astype(BF16)
        r = k - (DEEP - THIN)
        if 0 <= r < THIN + ROWS + THIN:
            strip = [
                jnp.where(slot < 2, pltpu.roll(left, 7, 0), jnp.where(slot < 5, pltpu.roll(own_left, 5, 0), 0.0)),
                jnp.where(slot > 4, right, jnp.where(slot > 1, pltpu.roll(own_right, 2, 0), 0.0)),
            ]
            x_s[r * STRIP : (r + 1) * STRIP, :] = jnp.concatenate(strip, 0).astype(BF16)

    def put(ref, row, rows, value, above, below, lanes=slice(None)):
        over = min(max(above - row, 0), rows)
        under = min(max(row + rows - below, 0), rows)
        parts = [value[over * PITCH : (rows - under) * PITCH]]
        if over:
            parts.insert(0, value[: over * PITCH] * top)
        if under:
            parts.append(value[(rows - under) * PITCH :] * bottom)
        ref[row * PITCH : (row + rows) * PITCH, lanes] = jnp.concatenate(parts, 0).astype(ref.dtype)

    place = lax.broadcasted_iota(jnp.int32, (8, 128), 0)
    pooled[...] = pooled_in[...]
    mean = pool(x_c, w_in, 1, 32, STRIP)
    for row in range(16):
        v = mean[row] * top if row < 4 else mean[row] * bottom if row > 11 else mean[row]
        at = row * PITCH
        first = pooled_in[at : at + 8, :].astype(F32)
        pooled[at : at + 8, :] = jnp.where(place < 5, pltpu.roll(v[:8], 7, 0), first).astype(BF16)
        last = pooled_in[at + 64 : at + 72, :].astype(F32)
        pooled[at + 64 : at + 72, :] = jnp.where(place > 2, pltpu.roll(v[8:], 1, 0), last).astype(BF16)
    for row, rows in ((0, 8), (8, 6)):
        put(middle, row, rows, silu(half_conv(pooled, w_coarse, row + 1, rows)), 3, 11)
    embedded = scale[...] * noise_code + shift[...]
    for row, rows in ((0, 6), (6, 6)):
        d = silu(half_conv(middle, w_deeper, row + 1, rows)).astype(BF16)
        guide[row * PITCH : (row + rows) * PITCH, :] = matmul_nt(d, w_guide[...]) + embedded
    strips = pair_conv(x_s, w_noisy, 1, 22, True, STRIP)
    for row, rows in ((0, 12), (12, 10)):
        for half, strip in enumerate(strips):
            lanes = slice(128 * half, 128 * half + 128)
            parts = []
            for q in range(row, row + rows):
                at = q * PITCH
                left = pltpu.roll(strip[q * STRIP : q * STRIP + 8], 2, 0)
                first = jnp.where(place < 2, 0.0, jnp.where(place < 5, left, opening[at : at + 8, lanes]))
                right = pltpu.roll(strip[q * STRIP + 8 : q * STRIP + 16], 7, 0)
                last = jnp.where(place > 5, 0.0, jnp.where(place > 2, right, opening[at + 64 : at + 72, lanes]))
                g = (q + 1) // 2 * PITCH
                parts.append(jnp.concatenate([first, opening[at + 8 : at + 64, lanes], last], 0) + guide[g : g + PITCH, :])
            put(hidden, row, rows, silu(jnp.concatenate(parts, 0)), 3, 19, lanes)
    for row in (0, 10):
        for half, v in enumerate(pair_conv(hidden, w_block, 1 + row, 10)):
            put(inner, row, 10, silu(v), 2, 18, slice(128 * half, 128 * half + 128))
    for row, rows in ((0, 10), (10, 8)):
        h = hidden[(2 + row) * PITCH : (2 + row + rows) * PITCH, :].astype(F32)
        for half, v in enumerate(pair_conv(inner, w_branch, 1 + row, rows)):
            lanes = slice(128 * half, 128 * half + 128)
            put(mixed, row, rows, silu(v + h[:, lanes]), 1, 17, lanes)
    for first, rows in ((0, 6), (6, 6), (12, 4)):
        even, odd = pair_conv(mixed, w_out, 1 + first, rows)
        for q in range(rows):
            row = first + q
            at = slice(q * PITCH, (q + 1) * PITCH)
            turn[row, pl.ds(0, PITCH, stride=2), :] = even[at]
            turn[row, pl.ds(1, PITCH, stride=2), :] = odd[at]
            head = turn[row, 2 * EDGE : 2 * (EDGE + PAIRS), :].T[:CH]
            here = pl.ds(row, CH, stride=ROWS)
            out[here, :] = scale_skip * state[here, :] + scale_out * head


def net(n_lat, *args):
    vm = pl.BlockSpec(memory_space=VMEM)
    return pl.pallas_call(
        functools.partial(net_body, n_lat),
        out_shape=jax.ShapeDtypeStruct((CH * ROWS, 128), F32),
        in_specs=[pl.BlockSpec(memory_space=pltpu.SMEM)] + [vm] * (len(args) - 1),
        out_specs=vm,
        scratch_shapes=[
            VMEM((34 * STRIP, 256), BF16),
            VMEM((24 * STRIP, 256), BF16),
            VMEM((16 * PITCH, 128), BF16),
            VMEM((14 * PITCH, 256), BF16),
            VMEM((12 * PITCH, 128), F32),
            VMEM((22 * PITCH, 256), BF16),
            VMEM((20 * PITCH, 256), BF16),
            VMEM((18 * PITCH, 256), BF16),
            VMEM((ROWS, 2 * PITCH, 128), F32),
        ],
        compiler_params=pltpu.CompilerParams(vmem_limit_bytes=24 << 20),
        name="net",
    )(*args)


def on_device(
    mesh_shape,
    conditions,
    noisy_state,
    noise_level,
    kernel_input,
    kernel_coarse,
    kernel_deeper,
    guide_weight,
    time_scale,
    time_shift,
    kernel_noisy,
    kernel_block,
    kernel_branch,
    kernel_output,
):
    lon_even, lat_even = lax.axis_index("lon") % 2 == 0, lax.axis_index("lat") % 2 == 0
    cond = conditions.reshape(CH * ROWS, 128)
    state = noisy_state.reshape(CH * ROWS, 128)
    by_input = lambda kernel: kernel.transpose(0, 2, 1)
    in_hbm = lambda *values: [pltpu.with_memory_space_constraint(value, pltpu.HBM) for value in values]
    own_c, own_s, left, right, small_a, small_b, lat_a, lat_b, w_in, w_noisy = prep(
        noise_level, *in_hbm(cond, state, by_input(kernel_input), by_input(kernel_noisy))
    )
    permute = lambda value, a, o: lax.ppermute(value, AXES, swap_pairs(mesh_shape, a, o))
    small_b = permute(small_b, "B", None)
    small_a = permute(small_a, "A", None)
    lat_b = permute(lat_b, "B", None)
    lat_a = permute(lat_a, "A", None)
    above, below = jnp.where(lat_even, small_b, small_a), jnp.where(lat_even, small_a, small_b)
    left, right = (jnp.concatenate([above[n], edge, below[n]]) for n, edge in enumerate((left, right)))
    sent_a, sent_b = jnp.where(lon_even, right, left), jnp.where(lon_even, left, right)
    sent_b, sent_a, now_c, now_s = lax.optimization_barrier((sent_b, sent_a, own_c, own_s))
    edge_b = permute(sent_b, None, "B")
    edge_a = permute(sent_a, None, "A")
    *fetched, pool_own, open_own = own_rows(
        now_c, now_s, w_in, w_noisy, *in_hbm(kernel_coarse, kernel_block, kernel_branch, kernel_output)
    )
    rest = inner(
        mesh_shape[1], own_c, own_s, lat_b, lat_a, w_in, w_noisy, pool_own, open_own, *in_hbm(kernel_deeper, guide_weight)
    )
    out = net(
        mesh_shape[1], noise_level, sent_b, sent_a, edge_b, edge_a, state,
        time_scale[None], time_shift[None], w_in, w_noisy, *fetched, *rest,
    )
    return out.reshape(noisy_state.shape)


def solution(mesh):
    tile = P(None, "lat", "lon")
    member = P(None, None, "lat", "lon")
    return jax.shard_map(
        functools.partial(on_device, (mesh.shape["lon"], mesh.shape["lat"])),
        mesh=mesh,
        in_specs=(tile, member) + (P(),) * 11,
        out_specs=member,
        check_vma=False,
    )
```
